256 devices in a mesh: seq: 32 (over z_hi, x, core), head: 8 (over z_lo, y).
Axes of the slice: x: 4, y: 4, z: 8 (z_hi: 4, z_lo: 2; z = z_hi * 2 + z_lo), core: 2. Of those that a mesh axis runs over, the one named last changes fastest.
Arguments:
- queries: bfloat16 [98304, 4096], P(('seq', 'head')), may hold values from -72 to 72
- key_states: bfloat16 [98304, 4096], P(('seq', 'head')), may hold values from -7 to 7
- value_states: bfloat16 [98304, 4096], P(('seq', 'head')), may hold values from -6 to 6
- partner: int32 [384], replicated, may hold values from 0 to 383, as said below
- buckets: int32 [2, 511], replicated, may hold values from 0 to 31
- bias_table: float32 [32, 32], P(None, 'head'), may hold values from -4 to 4
Outputs:
- attended: bfloat16 [98304, 4096], P(('seq', 'head'))
The draws below stay inside these ranges and needn't reach their ends.
Inputs may be any that keep to these rules, and one draw needn't show every extreme that they name: `partner`: A permutation of the 384 blocks; block i lies on seq index i // 12. The 12 blocks of one seq index have their partners on 12 different seq indices, and they are the partners of blocks on 12 different seq indices.
All inputs are finite; a program needn't handle non-finite values.
Results may differ from the reference program's by a relative error of at most 0.004.
Values may be sent and summed in bfloat16 or wider, within the bound.
A program may use at most 192 MiB of HBM per device.

```python
import math
from functools import partial
import jax
import jax.numpy as jnp
from jax import lax

D = 4096
HEADS = 32
HEAD_DIM = 128
BLOCK = 256
NBUCKET = 32
BLK_DEV = 12
NBLK = 384
TOKENS = 98304


def partner_table(key):
    base_key = jax.random.fold_in(key, 11)
    seq_count = NBLK // BLK_DEV
    first_key, second_key, third_key, fourth_key = jax.random.split(base_key, 4)
    outer_order = jax.random.permutation(first_key, seq_count)
    inner_order = jax.random.permutation(second_key, seq_count)
    offsets = jax.random.permutation(third_key, seq_count)[:BLK_DEV]
    slot_orders = jax.vmap(lambda sub_key: jax.random.permutation(sub_key, BLK_DEV))(jax.random.split(fourth_key, seq_count))
    indices = jnp.arange(NBLK)
    source = indices // BLK_DEV
    within = indices % BLK_DEV
    target = outer_order[(inner_order[source] + offsets[within]) % seq_count]
    return (target * BLK_DEV + slot_orders[target, within]).astype(jnp.int32)


def block_keys(key, block_index):
    sub_key = jax.random.fold_in(jax.random.fold_in(key, 23), block_index)
    drawn = jnp.clip(jax.random.normal(sub_key, (BLOCK, D), jnp.float32), -6.0, 6.0)
    return drawn


def draw_partner(key, part):
    return partner_table(key)


def draw_key_states(key, part):
    drawn = jax.vmap(partial(block_keys, key))(jnp.arange(NBLK))
    return drawn.reshape(NBLK * BLOCK, D).astype(jnp.bfloat16)


def draw_queries(key, part):
    query_key = jax.random.fold_in(key, 37)
    drawn = jnp.clip(jax.random.normal(query_key, (NBLK * BLOCK, D), jnp.float32), -6.0, 6.0)
    return drawn.astype(jnp.bfloat16)


def touch_ends(values, stream_key, least, top_value):
    longest = values.shape.index(max(values.shape))
    spots = []
    for shift in (0, 1):
        where = [jax.random.randint(jax.random.fold_in(stream_key, axis), (), 0, length) for axis, length in enumerate(values.shape)]
        where[longest] = (where[longest] + shift) % values.shape[longest]
        spots.append(tuple(where))
    return values.at[spots[0]].set(least).at[spots[1]].set(top_value)


def block_scale(key, extent, cuts, smallest, largest):
    loudness = 1.0
    for position, shards_of in cuts:
        heights = jax.random.uniform(jax.random.fold_in(jax.random.fold_in(key, 6), position), (shards_of,), jnp.float32, smallest / len(cuts), largest / len(cuts))
        loudness = loudness * jnp.repeat(jnp.exp(heights), extent[position] // shards_of).reshape((-1,) + (1,) * (len(extent) - 1 - position))
    return loudness


def scatter_about(key, extent, deviation, limit, shards=(), kind=jnp.bfloat16):
    entries = jax.random.normal(key, extent, jnp.float32) * deviation
    if len(shards) > 0:
        entries = block_scale(key, extent, shards, -0.22, 0.18) * entries
    return jnp.clip(entries, min=-limit, max=limit).astype(kind)


def setup_inputs(seed: int = 0) -> dict:
    splits = jax.random.split(jax.random.key(seed), 7)
    return {
        "queries": draw_queries(jax.random.fold_in(splits[6], 71), 0),
        "key_states": draw_key_states(jax.random.fold_in(splits[6], 71), 0),
        "value_states": scatter_about(splits[2], (TOKENS, D), 1.0, 6.0, ((0, 256),)),
        "partner": draw_partner(jax.random.fold_in(splits[6], 71), 0),
        "buckets": touch_ends(jax.random.randint(splits[4], (2, 2 * BLOCK - 1), 0, NBUCKET), jax.random.fold_in(splits[4], 1), 0, NBUCKET - 1).astype(jnp.int32),
        "bias_table": scatter_about(splits[5], (NBUCKET, HEADS), 1.0, 4.0, ((1, 8),), jnp.float32),
    }


def block_part(query_block, key_block, value_block, bias_part, score_scale):
    scores = jnp.einsum('qhd,khd->hqk', query_block.astype(jnp.float32), key_block.astype(jnp.float32), precision=lax.Precision.HIGHEST)
    scores = scores * score_scale + bias_part
    highest = lax.optimization_barrier(jnp.max(scores, axis=-1))
    weights = jnp.exp(scores - highest[..., None])
    totals = lax.optimization_barrier(jnp.sum(weights, axis=-1))
    rounded = lax.optimization_barrier(weights.astype(jnp.bfloat16)).astype(jnp.float32)
    summed = jnp.einsum('hqk,khd->qhd', rounded, value_block.astype(jnp.float32), precision=lax.Precision.HIGHEST)
    return (summed, highest, totals)

def combine_block(first_part, second_part):
    first_sum, first_high, first_total = first_part
    second_sum, second_high, second_total = second_part
    joint_high = jnp.maximum(first_high, second_high)
    first_factor = jnp.exp(first_high - joint_high)
    second_factor = jnp.exp(second_high - joint_high)
    denominator = first_factor * first_total + second_factor * second_total
    numerator = first_sum * jnp.swapaxes(first_factor, 0, 1)[..., None] + second_sum * jnp.swapaxes(second_factor, 0, 1)[..., None]
    return (numerator / jnp.swapaxes(denominator, 0, 1)[..., None]).astype(jnp.bfloat16)

def full_buckets(buckets):
    offsets = jnp.arange(BLOCK, dtype=jnp.int32)[None, :] - jnp.arange(BLOCK, dtype=jnp.int32)[:, None] + (BLOCK - 1)
    return jnp.concatenate([buckets[0][offsets], buckets[1][offsets]], axis=1)

def reference(queries, key_states, value_states, partner, buckets, bias_table):
    block_shape = (NBLK, BLOCK, HEADS, HEAD_DIM)
    query_blocks = queries.reshape(block_shape)
    key_blocks = key_states.reshape(block_shape)
    value_blocks = value_states.reshape(block_shape)
    bias_all = jnp.transpose(bias_table[full_buckets(buckets)], (2, 0, 1))
    score_scale = 1.0 / math.sqrt(HEAD_DIM)

    def attend(index):
        far_index = partner[index]
        own_part = block_part(query_blocks[index], key_blocks[index], value_blocks[index], bias_all[:, :, :BLOCK], score_scale)
        far_part = block_part(query_blocks[index], key_blocks[far_index], value_blocks[far_index], bias_all[:, :, BLOCK:], score_scale)
        return combine_block(own_part, far_part)
    attended = lax.map(attend, jnp.arange(NBLK, dtype=jnp.int32))
    return attended.reshape(NBLK * BLOCK, D)
```

```python
import functools
import math

import jax
import jax.numpy as jnp
from jax import lax
from jax.experimental import pallas as pl
from jax.experimental.pallas import tpu as pltpu
from jax.sharding import PartitionSpec as P

BLOCK = 256
HALF = 128
HEADS = 32
LANES = 128
ROWS = 16
CHUNKS = 8
GROUP = 4


def pack_kernel(parity_ref, low_ref, high_ref, half_ref, out_ref):
    shift = parity_ref[0] * (HEADS // 2)
    for head in range(HEADS):
        other = (head + HEADS // 2) % HEADS
        out_ref[0, head, 0] = low_ref[:, head * LANES : (head + 1) * LANES]
        out_ref[0, head, 1] = high_ref[:, other * LANES : (other + 1) * LANES]
        moved = lax.rem(head + shift, HEADS)
        out_ref[0, head, 2] = half_ref[:, pl.ds(pl.multiple_of(moved * LANES, LANES), LANES)]


def pack_tiles(parity, states):
    rows, columns = states.shape
    block = (ROWS, columns)
    return pl.pallas_call(
        pack_kernel,
        grid_spec=pltpu.PrefetchScalarGridSpec(
            num_scalar_prefetch=1,
            grid=(CHUNKS,),
            in_specs=[
                pl.BlockSpec(block, lambda c, e: (CHUNKS * e[0] + c, 0)),
                pl.BlockSpec(block, lambda c, e: (CHUNKS * e[0] + CHUNKS + c, 0)),
                pl.BlockSpec(block, lambda c, e: (2 * CHUNKS * (1 - e[0]) + c, 0)),
            ],
            out_specs=pl.BlockSpec((1, HEADS, 3, ROWS, LANES), lambda c, e: (c, 0, 0, 0, 0)),
        ),
        out_shape=jax.ShapeDtypeStruct((CHUNKS, HEADS, 3, ROWS, LANES), states.dtype),
        cost_estimate=pl.CostEstimate(flops=0, transcendentals=0, bytes_accessed=4 * rows * columns),
        name="pack_tiles",
    )(parity, states, states, states)


def pick_kernel(table_ref, held_ref, out_ref):
    count = out_ref.shape[0]
    first = pl.program_id(0) * count

    @pl.loop(0, count, step=16)
    def _(start):
        for offset in range(16):
            out_ref[start + offset] = held_ref[table_ref[first + start + offset]]


def pick_tiles(table, held):
    total = held.shape[0]
    wanted = table.shape[0]
    steps = 4
    return pl.pallas_call(
        pick_kernel,
        grid_spec=pltpu.PrefetchScalarGridSpec(
            num_scalar_prefetch=1,
            grid=(steps,),
            in_specs=[
                pl.BlockSpec((total, ROWS, LANES), lambda i, t: (0, 0, 0)),
            ],
            out_specs=pl.BlockSpec((wanted // steps, ROWS, LANES), lambda i, t: (i, 0, 0)),
        ),
        out_shape=jax.ShapeDtypeStruct((wanted, ROWS, LANES), held.dtype),
        cost_estimate=pl.CostEstimate(flops=0, transcendentals=0, bytes_accessed=16 * 1024 * 1024),
        compiler_params=pltpu.CompilerParams(vmem_limit_bytes=32 * 1024 * 1024),
        name="pick_tiles",
    )(table, held)


def toeplitz_bias(row):
    spread = pltpu.roll(
        jnp.broadcast_to(row, (HALF, 2 * BLOCK)), 2 * BLOCK - HALF + 1, 1, stride=1, stride_axis=0
    )
    return jnp.concatenate([spread[:, HALF : HALF + BLOCK], spread[:, :BLOCK]], axis=0)


def attend_heads(score_scale, query, key, value, far_key, far_value, bias_rows, out_ref):
    for g in range(GROUP):
        columns = slice(g * LANES, (g + 1) * LANES)
        near_keys = key[:, columns]
        near_values = value[:, columns]
        far_keys = jnp.concatenate([half[:, g, 0].reshape(HALF, LANES) for half in far_key], axis=0)
        far_values = jnp.concatenate([half[:, g, 0].reshape(HALF, LANES) for half in far_value], axis=0)
        contract = (((1,), (1,)), ((), ()))
        near = lax.dot_general(
            query[:, columns], near_keys, contract, preferred_element_type=jnp.float32
        )
        far = lax.dot_general(
            query[:, columns], far_keys, contract, preferred_element_type=jnp.float32
        )
        near = near * score_scale + toeplitz_bias(bias_rows[g, 0:1])
        far = far * score_scale + toeplitz_bias(bias_rows[g, 1:2])
        highest = jnp.max(jnp.maximum(near, far), axis=1, keepdims=True)
        near = jnp.exp(near - highest)
        far = jnp.exp(far - highest)
        total = jnp.sum(near + far, axis=1, keepdims=True)
        summed = jnp.dot(
            near.astype(jnp.bfloat16), near_values, preferred_element_type=jnp.float32
        ) + jnp.dot(far.astype(jnp.bfloat16), far_values, preferred_element_type=jnp.float32)
        out_ref[:, columns] = (summed / total).astype(jnp.bfloat16)


def attend_kernel(
    score_scale, parity_ref, q, k, v, ka, kb, va, vb, rows, *rest
):
    out_ref = rest[-1]
    attend_heads(score_scale, q, k, v, (ka, kb), (va, vb), rows, out_ref)


def attend(parity, queries, keys, values, far_keys, key_slot, far_values, value_slot, bias_rows, mode, into):
    width = GROUP * LANES
    steps = HEADS // 2 // GROUP
    score_scale = 1.0 / math.sqrt(LANES)

    def group_of(i, e):
        if mode == "low":
            return i
        if mode == "high":
            return i + steps
        return i + steps * e[0]

    def other_of(i, e):
        if mode == "low":
            return i + steps
        if mode == "high":
            return i
        return i + steps * (1 - e[0])

    if mode == "half":
        local = pl.BlockSpec((BLOCK, width), lambda i, e: (0, i))
        out_shape = jax.ShapeDtypeStruct((BLOCK, steps * width), jnp.bfloat16)
    else:
        local = pl.BlockSpec(
            (pl.Element(BLOCK), pl.Element(width)),
            lambda i, e: (e[0] * HALF, group_of(i, e) * width),
        )
        out_shape = jax.ShapeDtypeStruct(queries.shape, jnp.bfloat16)
    tiles = (CHUNKS, GROUP, 1, ROWS, LANES)
    in_specs = [
        local,
        local,
        local,
        pl.BlockSpec(tiles, lambda i, e: (0, group_of(i, e), key_slot, 0, 0)),
        pl.BlockSpec(tiles, lambda i, e: (0, other_of(i, e), key_slot, 0, 0)),
        pl.BlockSpec(tiles, lambda i, e: (0, group_of(i, e), value_slot, 0, 0)),
        pl.BlockSpec(tiles, lambda i, e: (0, other_of(i, e), value_slot, 0, 0)),
        pl.BlockSpec((GROUP, 2, 2 * BLOCK), lambda i, e: (group_of(i, e), 0, 0)),
    ]
    operands = [parity, queries, keys, values, far_keys, far_keys, far_values, far_values, bias_rows]
    aliases = {}
    if into is not None:
        in_specs.append(pl.BlockSpec(memory_space=pl.ANY))
        aliases = {len(operands): 0}
        operands.append(into)
    return pl.pallas_call(
        functools.partial(attend_kernel, score_scale),
        grid_spec=pltpu.PrefetchScalarGridSpec(
            num_scalar_prefetch=1,
            grid=(steps,),
            in_specs=in_specs,
            out_specs=local,
        ),
        out_shape=out_shape,
        input_output_aliases=aliases,
        cost_estimate=pl.CostEstimate(
            flops=16 * 8 * BLOCK * BLOCK * LANES,
            transcendentals=16 * 2 * BLOCK * BLOCK,
            bytes_accessed=24 * 1024 * 1024,
        ),
        compiler_params=pltpu.CompilerParams(vmem_limit_bytes=40 * 1024 * 1024),
        name="attend_" + mode,
    )(*operands)


def place_kernel(parity_ref, own_ref, other_ref, into_ref, out_ref):
    mine = pl.program_id(0) == parity_ref[0]

    @pl.when(mine)
    def _():
        out_ref[...] = own_ref[...]

    @pl.when(jnp.logical_not(mine))
    def _():
        out_ref[...] = other_ref[...]


def place_half(parity, own, other, into):
    width = own.shape[1]
    return pl.pallas_call(
        place_kernel,
        grid_spec=pltpu.PrefetchScalarGridSpec(
            num_scalar_prefetch=1,
            grid=(2,),
            in_specs=[
                pl.BlockSpec((HALF, width), lambda j, e: (e[0], 0)),
                pl.BlockSpec((HALF, width), lambda j, e: (0, 0)),
                pl.BlockSpec(memory_space=pl.ANY),
            ],
            out_specs=pl.BlockSpec((HALF, width), lambda j, e: (2 * (1 - e[0]), j)),
        ),
        out_shape=jax.ShapeDtypeStruct(into.shape, into.dtype),
        input_output_aliases={3: 0},
        cost_estimate=pl.CostEstimate(flops=0, transcendentals=0, bytes_accessed=4 * HALF * width * 2),
        name="place_half",
    )(parity, own, other, into)


def tile_table(partner, low_side):
    triples = partner.reshape(-1, 3)
    first, middle, last = triples[:, 0], triples[:, 1], triples[:, 2]
    wanted = jnp.stack(
        [
            jnp.stack([first, middle, first], axis=1),
            jnp.stack([last, middle, last], axis=1),
        ],
        axis=1,
    )
    want_low = jnp.array([[True, True, False], [True, False, False]])
    use_first = want_low[None] == low_side
    place = wanted % 3
    head_place = jnp.where(place == 0, 0, jnp.where(place == 1, 2, 3))
    tail_place = jnp.where(place == 0, 1, jnp.where(place == 1, 5, 4))
    return (wanted // 3) * 6 + jnp.where(use_first, head_place, tail_place)


def on_device(queries, key_states, value_states, partner, buckets, bias_table):
    rows, columns = queries.shape
    both = ("seq", "head")
    me = lax.axis_index("seq") * lax.axis_size("head") + lax.axis_index("head")
    devices = lax.axis_size("seq") * lax.axis_size("head")
    odd = lax.rem(me, 2).astype(jnp.int32)
    parity = odd.reshape(1)
    low_side = lax.rem(me, HEADS) < HEADS // 2

    def spread(tiles):
        shape = tiles.shape
        flat = tiles.reshape((devices,) + shape[-3:])
        return lax.all_to_all(flat, both, split_axis=0, concat_axis=0, tiled=True)

    key_tiles = spread(pack_tiles(parity, key_states))
    value_tiles = spread(pack_tiles(parity, value_states))

    swap = [(i, i ^ 1) for i in range(lax.axis_size("head"))]
    half_columns = columns // 2
    half_start = HALF * 2 * (1 - odd)
    halves = jnp.stack(
        [lax.dynamic_slice_in_dim(a, half_start, HALF, 0) for a in (queries, key_states, value_states)]
    )
    kept = lax.dynamic_slice_in_dim(halves, odd * half_columns, half_columns, 2)
    given = lax.dynamic_slice_in_dim(halves, (1 - odd) * half_columns, half_columns, 2)
    taken = lax.ppermute(given, "head", swap)
    is_odd = odd == 1
    middle = jnp.concatenate(
        [jnp.where(is_odd, taken, kept), jnp.where(is_odd, kept, taken)], axis=1
    )

    full_table = lax.all_gather(bias_table, "head", axis=1, tiled=True)
    one_hot = (
        buckets[..., None] == jnp.arange(full_table.shape[0], dtype=jnp.int32)
    ).astype(jnp.float32)
    bias_rows = jnp.einsum("skb,bh->hsk", one_hot, full_table, precision=lax.Precision.HIGHEST)
    bias_rows = jnp.pad(bias_rows, ((0, 0), (0, 0), (0, 1)))

    table = tile_table(partner, low_side)
    tile_shape = (CHUNKS, HEADS, -1, ROWS, LANES)
    far_keys = spread(
        pick_tiles(table.reshape(-1), key_tiles.reshape(-1, ROWS, LANES)).reshape(devices, 3, ROWS, LANES)
    ).reshape(tile_shape)
    flat_values = value_tiles.reshape(-1, ROWS, LANES)
    early_values = spread(
        pick_tiles(table[..., :2].reshape(-1), flat_values).reshape(devices, 2, ROWS, LANES)
    ).reshape(tile_shape)
    late_values = spread(
        pick_tiles(table[..., 2].reshape(-1), flat_values).reshape(devices, 1, ROWS, LANES)
    ).reshape(tile_shape)

    middle_out = attend(
        parity, middle[0], middle[1], middle[2], far_keys, 1, early_values, 1, bias_rows, "half", None
    )
    outgoing = lax.dynamic_slice_in_dim(middle_out, (1 - odd) * HALF, HALF, 0)
    incoming = lax.ppermute(outgoing, "head", swap)
    out = attend(
        parity, queries, key_states, value_states, far_keys, 0, early_values, 0, bias_rows, "low", None
    )
    out = place_half(parity, middle_out, incoming, out)
    return attend(
        parity, queries, key_states, value_states, far_keys, 2, late_values, 0, bias_rows, "high", out
    )


def solution(mesh):
    whole = P(("seq", "head"), None)
    return jax.shard_map(
        on_device,
        mesh=mesh,
        in_specs=(whole, whole, whole, P(), P(), P(None, "head")),
        out_specs=whole,
        check_vma=False,
    )
```

```python
import functools
import math

import jax
import jax.numpy as jnp
from jax import lax
from jax.experimental import pallas as pl
from jax.experimental.pallas import tpu as pltpu
from jax.sharding import PartitionSpec as P

BLOCK = 256
HALF = 128
HEADS = 32
LANES = 128
ROWS = 16
CHUNKS = 8
GROUP = 4


MESH = pl.DeviceIdType.MESH
PLANES = 8
PLANE_DEVICES = 32
SLOTS = 3


def place_of(plane, spot):
    return ((plane // 2) * 8 + spot // 4, lax.rem(plane, 2) * 4 + lax.rem(spot, 4))


def move_kernel(
    table_ref,
    q_ref,
    k_ref,
    v_ref,
    far_ref,
    mid_q_ref,
    mid_k_ref,
    mid_v_ref,
    fanned,
    held_k,
    held_v,
    picked_k,
    picked_v,
    landed,
    half_send,
    half_recv,
    z1_send,
    z1_recv,
    p1_send,
    p1_recv,
    z2_send,
    z2_recv,
    p2_send,
    p2_recv,
):
    seq = lax.axis_index("seq")
    head = lax.axis_index("head")
    plane = 2 * (seq // 8) + head // 4
    spot = lax.rem(seq, 8) * 4 + lax.rem(head, 4)
    odd = lax.rem(head, 2)
    pair = spot + 1 - 2 * odd

    barrier = pltpu.get_barrier_semaphore()
    for step in range(1, PLANES):
        pl.semaphore_signal(
            barrier,
            inc=1,
            device_id=place_of(lax.rem(plane + step, PLANES), spot),
            device_id_type=MESH,
        )

    def greet(step, carry):
        pl.semaphore_signal(
            barrier,
            inc=1,
            device_id=place_of(plane, lax.rem(spot + step, PLANE_DEVICES)),
            device_id_type=MESH,
        )
        return carry

    lax.fori_loop(1, PLANE_DEVICES, greet, 0)
    pl.semaphore_wait(barrier, PLANES - 1 + PLANE_DEVICES - 1)

    def finish(ref, sem):
        pltpu.make_async_copy(ref, ref, sem).wait()

    def z_stage(source, target, send, recv):
        for step in (4, 3, 5, 2, 6, 1, 7):
            other = lax.rem(plane + step, PLANES)
            pltpu.make_async_remote_copy(
                src_ref=source(other),
                dst_ref=target,
                send_sem=send,
                recv_sem=recv,
                device_id=place_of(other, spot),
                device_id_type=MESH,
            ).start()
        pltpu.make_async_copy(source(plane), target, recv).start()

    def plane_stage(source, target, send, recv):
        def body(step, carry):
            other = lax.rem(spot + step, PLANE_DEVICES)
            pltpu.make_async_remote_copy(
                src_ref=source(other),
                dst_ref=target,
                send_sem=send,
                recv_sem=recv,
                device_id=place_of(plane, other),
                device_id_type=MESH,
            ).start()
            return carry

        lax.fori_loop(1, PLANE_DEVICES, body, 0)
        pltpu.make_async_copy(source(spot), target, recv).start()

    def fan_out(chunk):
        kind, slot = divmod(chunk, SLOTS)
        ref = (k_ref, v_ref)[kind]
        first = (odd * HALF, odd * HALF + HALF, 2 * HALF * (1 - odd))[slot]
        z_stage(
            lambda other: ref.at[pl.ds(pl.multiple_of(first + ROWS * other, ROWS), ROWS), :],
            fanned.at[chunk, plane],
            z1_send.at[chunk],
            z1_recv.at[chunk],
        )

    def by_head(chunk):
        kind, slot = divmod(chunk, SLOTS)
        held = (held_k, held_v)[kind]
        shift = (0, HEADS // 2, odd * (HEADS // 2))[slot]

        def source(other):
            start = pl.multiple_of(lax.rem(other + shift, HEADS) * LANES, LANES)
            return fanned.at[chunk, :, :, pl.ds(start, LANES)]

        plane_stage(
            source,
            held.at[pl.ds((slot * PLANE_DEVICES + spot) * PLANES, PLANES)],
            p1_send.at[chunk],
            p1_recv.at[chunk],
        )

    side = spot // (HEADS // 2)
    blocks = table_ref.shape[0] // 2

    def pick(kind, slot):
        held = (held_k, held_v)[kind]
        picked = (picked_k, picked_v)[kind]

        def body(z, carry):
            first = (z // 2) * 96 + lax.rem(z, 2) * 6
            base = (slot * PLANES + z) * PLANE_DEVICES
            for p in range(PLANE_DEVICES):
                e = p % 2
                low = (True, e == 0, False)[slot]
                member = 1 if slot == 1 else 2 * e
                block = first + (p // 4) * 12 + (p % 4 // 2) * 3 + member
                chosen = side if low else 1 - side
                picked[base + p] = held[table_ref[chosen * blocks + block]]
            return carry

        lax.fori_loop(0, PLANES, body, 0)

    def send_picked(chunk):
        kind, slot = divmod(chunk, SLOTS)
        picked = (picked_k, picked_v)[kind]
        z_stage(
            lambda other: picked.at[pl.ds((slot * PLANES + other) * PLANE_DEVICES, PLANE_DEVICES)],
            landed.at[chunk, plane],
            z2_send.at[chunk],
            z2_recv.at[chunk],
        )

    def deliver(chunk):
        plane_stage(
            lambda other: landed.at[chunk, :, other],
            far_ref.at[chunk, spot],
            p2_send.at[chunk],
            p2_recv.at[chunk],
        )

    for chunk in range(SLOTS):
        fan_out(chunk)
    for i, (source, target) in enumerate(((q_ref, mid_q_ref), (k_ref, mid_k_ref), (v_ref, mid_v_ref))):
        rows = pl.ds(pl.multiple_of(2 * HALF * (1 - odd), HALF), HALF)
        width = target.shape[1]
        own = pl.ds(pl.multiple_of(odd * width, LANES), width)
        given = pl.ds(pl.multiple_of((1 - odd) * width, LANES), width)
        place = target.at[pl.ds(pl.multiple_of(odd * HALF, HALF), HALF), :]
        pltpu.make_async_remote_copy(
            src_ref=source.at[rows, given],
            dst_ref=place,
            send_sem=half_send.at[i],
            recv_sem=half_recv.at[i],
            device_id=place_of(plane, pair),
            device_id_type=MESH,
        ).start()
        pltpu.make_async_copy(source.at[rows, own], place, half_recv.at[i]).start()
    for chunk in range(SLOTS):
        finish(fanned.at[chunk], z1_recv.at[chunk])
        by_head(chunk)
        fan_out(chunk + SLOTS)
    for kind in range(2):
        held = (held_k, held_v)[kind]
        for slot in range(SLOTS):
            part = held.at[pl.ds(slot * PLANE_DEVICES * PLANES, PLANE_DEVICES * PLANES)]
            finish(part, p1_recv.at[kind * SLOTS + slot])
        for slot in range(SLOTS):
            pick(kind, slot)
            send_picked(kind * SLOTS + slot)
        if kind == 0:
            for chunk in range(SLOTS, 2 * SLOTS):
                finish(fanned.at[chunk], z1_recv.at[chunk])
                by_head(chunk)
    for chunk in range(2 * SLOTS):
        finish(landed.at[chunk], z2_recv.at[chunk])
        deliver(chunk)
    for i, target in enumerate((mid_q_ref, mid_k_ref, mid_v_ref)):
        finish(target, half_recv.at[i])
        finish(target.at[pl.ds(0, HALF), :], half_send.at[i])
    for chunk in range(2 * SLOTS):
        finish(fanned.at[chunk, pl.ds(0, PLANES - 1)], z1_send.at[chunk])
        finish(far_ref.at[chunk, pl.ds(0, PLANE_DEVICES - 1)], p1_send.at[chunk])
        finish(landed.at[chunk, pl.ds(0, PLANES - 1)], z2_send.at[chunk])
        finish(far_ref.at[chunk, pl.ds(0, PLANE_DEVICES - 1)], p2_send.at[chunk])
    for chunk in range(2 * SLOTS):
        finish(far_ref.at[chunk], p2_recv.at[chunk])


def move_tiles(table, queries, keys, values):
    rows, columns = keys.shape
    kind = keys.dtype
    chunks = 2 * SLOTS
    tiles = SLOTS * PLANES * PLANE_DEVICES
    middle = jax.ShapeDtypeStruct((BLOCK, columns // 2), kind)
    anywhere = pl.BlockSpec(memory_space=pl.ANY)
    semaphores = [pltpu.SemaphoreType.DMA((3,))] * 2 + [pltpu.SemaphoreType.DMA((chunks,))] * 8
    return pl.pallas_call(
        move_kernel,
        in_specs=[pl.BlockSpec(memory_space=pltpu.SMEM)] + [anywhere] * 3,
        out_specs=[anywhere] * 4,
        out_shape=[
            jax.ShapeDtypeStruct((chunks, PLANE_DEVICES, PLANES, ROWS, LANES), kind),
            middle,
            middle,
            middle,
        ],
        scratch_shapes=[
            pltpu.VMEM((chunks, PLANES, ROWS, columns), kind),
            pltpu.VMEM((tiles, ROWS, LANES), kind),
            pltpu.VMEM((tiles, ROWS, LANES), kind),
            pltpu.VMEM((tiles, ROWS, LANES), kind),
            pltpu.VMEM((tiles, ROWS, LANES), kind),
            pltpu.VMEM((chunks, PLANES, PLANE_DEVICES, ROWS, LANES), kind),
        ]
        + semaphores,
        cost_estimate=pl.CostEstimate(
            flops=0, transcendentals=0, bytes_accessed=1024 * 1024 * 1024
        ),
        compiler_params=pltpu.CompilerParams(
            collective_id=0, has_side_effects=True, vmem_limit_bytes=48 * 1024 * 1024
        ),
        name="move_tiles",
    )(table, queries, keys, values)


def toeplitz_bias(row):
    spread = pltpu.roll(
        jnp.broadcast_to(row, (HALF, 2 * BLOCK)), 2 * BLOCK - HALF + 1, 1, stride=1, stride_axis=0
    )
    return jnp.concatenate([spread[:, HALF : HALF + BLOCK], spread[:, :BLOCK]], axis=0)


def attend_heads(score_scale, query, key, value, far_key, far_value, bias_rows, out_ref):
    for g in range(GROUP):
        columns = slice(g * LANES, (g + 1) * LANES)
        near_keys = key[:, columns]
        near_values = value[:, columns]
        far_keys = jnp.concatenate([half[0, g].reshape(HALF, LANES) for half in far_key], axis=0)
        far_values = jnp.concatenate([half[0, g].reshape(HALF, LANES) for half in far_value], axis=0)
        contract = (((1,), (1,)), ((), ()))
        near = lax.dot_general(
            query[:, columns], near_keys, contract, preferred_element_type=jnp.float32
        )
        far = lax.dot_general(
            query[:, columns], far_keys, contract, preferred_element_type=jnp.float32
        )
        near = near * score_scale + toeplitz_bias(bias_rows[g, 0:1])
        far = far * score_scale + toeplitz_bias(bias_rows[g, 1:2])
        highest = jnp.max(jnp.maximum(near, far), axis=1, keepdims=True)
        near = jnp.exp(near - highest)
        far = jnp.exp(far - highest)
        total = jnp.sum(near + far, axis=1, keepdims=True)
        summed = jnp.dot(
            near.astype(jnp.bfloat16), near_values, preferred_element_type=jnp.float32
        ) + jnp.dot(far.astype(jnp.bfloat16), far_values, preferred_element_type=jnp.float32)
        out_ref[:, columns] = (summed / total).astype(jnp.bfloat16)


def attend_kernel(
    score_scale, parity_ref, q, k, v, ka, kb, va, vb, rows, *rest
):
    out_ref = rest[-1]
    attend_heads(score_scale, q, k, v, (ka, kb), (va, vb), rows, out_ref)


def attend(parity, queries, keys, values, far, bias_rows, mode, into):
    slot = {"low": 0, "half": 1, "high": 2}[mode]
    width = GROUP * LANES
    steps = HEADS // 2 // GROUP
    score_scale = 1.0 / math.sqrt(LANES)

    def group_of(i, e):
        if mode == "low":
            return i
        if mode == "high":
            return i + steps
        return i + steps * e[0]

    def other_of(i, e):
        if mode == "low":
            return i + steps
        if mode == "high":
            return i
        return i + steps * (1 - e[0])

    if mode == "half":
        local = pl.BlockSpec((BLOCK, width), lambda i, e: (0, i))
        out_shape = jax.ShapeDtypeStruct((BLOCK, steps * width), jnp.bfloat16)
    else:
        local = pl.BlockSpec(
            (pl.Element(BLOCK), pl.Element(width)),
            lambda i, e: (e[0] * HALF, group_of(i, e) * width),
        )
        out_shape = jax.ShapeDtypeStruct(queries.shape, jnp.bfloat16)
    tiles = (1, GROUP, CHUNKS, ROWS, LANES)
    in_specs = [
        local,
        local,
        local,
        pl.BlockSpec(tiles, lambda i, e: (slot, group_of(i, e), 0, 0, 0)),
        pl.BlockSpec(tiles, lambda i, e: (slot, other_of(i, e), 0, 0, 0)),
        pl.BlockSpec(tiles, lambda i, e: (SLOTS + slot, group_of(i, e), 0, 0, 0)),
        pl.BlockSpec(tiles, lambda i, e: (SLOTS + slot, other_of(i, e), 0, 0, 0)),
        pl.BlockSpec((GROUP, 2, 2 * BLOCK), lambda i, e: (group_of(i, e), 0, 0)),
    ]
    operands = [parity, queries, keys, values, far, far, far, far, bias_rows]
    aliases = {}
    if into is not None:
        in_specs.append(pl.BlockSpec(memory_space=pl.ANY))
        aliases = {len(operands): 0}
        operands.append(into)
    return pl.pallas_call(
        functools.partial(attend_kernel, score_scale),
        grid_spec=pltpu.PrefetchScalarGridSpec(
            num_scalar_prefetch=1,
            grid=(steps,),
            in_specs=in_specs,
            out_specs=local,
        ),
        out_shape=out_shape,
        input_output_aliases=aliases,
        cost_estimate=pl.CostEstimate(
            flops=16 * 8 * BLOCK * BLOCK * LANES,
            transcendentals=16 * 2 * BLOCK * BLOCK,
            bytes_accessed=24 * 1024 * 1024,
        ),
        compiler_params=pltpu.CompilerParams(vmem_limit_bytes=40 * 1024 * 1024),
        name="attend_" + mode,
    )(*operands)


def place_kernel(parity_ref, own_ref, other_ref, into_ref, out_ref):
    mine = pl.program_id(0) == parity_ref[0]

    @pl.when(mine)
    def _():
        out_ref[...] = own_ref[...]

    @pl.when(jnp.logical_not(mine))
    def _():
        out_ref[...] = other_ref[...]


def place_half(parity, own, other, into):
    width = own.shape[1]
    return pl.pallas_call(
        place_kernel,
        grid_spec=pltpu.PrefetchScalarGridSpec(
            num_scalar_prefetch=1,
            grid=(2,),
            in_specs=[
                pl.BlockSpec((HALF, width), lambda j, e: (e[0], 0)),
                pl.BlockSpec((HALF, width), lambda j, e: (0, 0)),
                pl.BlockSpec(memory_space=pl.ANY),
            ],
            out_specs=pl.BlockSpec((HALF, width), lambda j, e: (2 * (1 - e[0]), j)),
        ),
        out_shape=jax.ShapeDtypeStruct(into.shape, into.dtype),
        input_output_aliases={3: 0},
        cost_estimate=pl.CostEstimate(flops=0, transcendentals=0, bytes_accessed=4 * HALF * width * 2),
        name="place_half",
    )(parity, own, other, into)


def tile_table(partner):
    trio = partner // 3
    member = partner - 3 * trio
    entries = []
    for source, slot in (
        (jnp.where(member == 2, 1, 0), jnp.where(member == 1, 2, 0)),
        (jnp.where(member == 0, 0, 1), jnp.where(member == 1, 2, 1)),
    ):
        device = 2 * trio + source
        seq, head = device // 8, device % 8
        plane = (seq // 8) * 2 + head // 4
        spot = (seq % 8) * 4 + head % 4
        entries.append((slot * PLANE_DEVICES + spot) * PLANES + plane)
    return jnp.concatenate(entries)


def on_device(queries, key_states, value_states, partner, buckets, bias_table):
    odd = lax.rem(lax.axis_index("head"), 2).astype(jnp.int32)
    parity = odd.reshape(1)

    full_table = lax.all_gather(bias_table, "head", axis=1, tiled=True)
    one_hot = (
        buckets[..., None] == jnp.arange(full_table.shape[0], dtype=jnp.int32)
    ).astype(jnp.float32)
    bias_rows = jnp.einsum("skb,bh->hsk", one_hot, full_table, precision=lax.Precision.HIGHEST)
    bias_rows = jnp.pad(bias_rows, ((0, 0), (0, 0), (0, 1)))

    far, *middle = move_tiles(tile_table(partner), queries, key_states, value_states)

    middle_out = attend(parity, *middle, far, bias_rows, "half", None)
    outgoing = lax.dynamic_slice_in_dim(middle_out, (1 - odd) * HALF, HALF, 0)
    swap = [(i, i ^ 1) for i in range(lax.axis_size("head"))]
    incoming = lax.ppermute(outgoing, "head", swap)
    out = attend(parity, queries, key_states, value_states, far, bias_rows, "low", None)
    out = attend(parity, queries, key_states, value_states, far, bias_rows, "high", out)
    return place_half(parity, middle_out, incoming, out)


def solution(mesh):
    whole = P(("seq", "head"), None)
    return jax.shard_map(
        on_device,
        mesh=mesh,
        in_specs=(whole, whole, whole, P(), P(), P(None, "head")),
        out_specs=whole,
        check_vma=False,
    )
```

```python
import math

import jax
import jax.numpy as jnp
from jax import lax
from jax.experimental import pallas as pl
from jax.experimental.pallas import tpu as pltpu
from jax.sharding import PartitionSpec as P

BLOCK = 256
HALF = 128
HEADS = 32
LANES = 128
ROWS = 16
CHUNKS = 8
GROUP = 4


MESH = pl.DeviceIdType.MESH
PLANES = 8
PLANE_DEVICES = 32
SLOTS = 3
ROW_SET = 8


def place_of(plane, spot):
    return ((plane // 2) * 8 + spot // 4, lax.rem(plane, 2) * 4 + lax.rem(spot, 4))


def move_kernel(
    table_ref,
    q_ref,
    k_ref,
    v_ref,
    row_ref,
    far_ref,
    mid_q_ref,
    mid_k_ref,
    mid_v_ref,
    skew_ref,
    fanned,
    held_k,
    held_v,
    picked_k,
    picked_v,
    landed,
    rows,
    skewed,
    row_send,
    row_recv,
    skew_sem,
    half_send,
    half_recv,
    z1_send,
    z1_recv,
    p1_send,
    p1_recv,
    z2_send,
    z2_recv,
    p2_send,
    p2_recv,
):
    seq = lax.axis_index("seq")
    head = lax.axis_index("head")
    plane = 2 * (seq // 8) + head // 4
    spot = lax.rem(seq, 8) * 4 + lax.rem(head, 4)
    odd = lax.rem(head, 2)
    pair = spot + 1 - 2 * odd

    barrier = pltpu.get_barrier_semaphore()
    for step in range(1, PLANES):
        pl.semaphore_signal(
            barrier,
            inc=1,
            device_id=place_of(lax.rem(plane + step, PLANES), spot),
            device_id_type=MESH,
        )

    def greet(step, carry):
        pl.semaphore_signal(
            barrier,
            inc=1,
            device_id=place_of(plane, lax.rem(spot + step, PLANE_DEVICES)),
            device_id_type=MESH,
        )
        return carry

    lax.fori_loop(1, PLANE_DEVICES, greet, 0)
    pl.semaphore_wait(barrier, PLANES - 1 + PLANE_DEVICES - 1)

    def finish(ref, sem):
        pltpu.make_async_copy(ref, ref, sem).wait()

    def z_stage(source, target, send, recv):
        for step in (4, 3, 5, 2, 6, 1, 7):
            other = lax.rem(plane + step, PLANES)
            pltpu.make_async_remote_copy(
                src_ref=source(other),
                dst_ref=target,
                send_sem=send,
                recv_sem=recv,
                device_id=place_of(other, spot),
                device_id_type=MESH,
            ).start()
        pltpu.make_async_copy(source(plane), target, recv).start()

    def plane_stage(source, target, send, recv):
        def body(step, carry):
            other = lax.rem(spot + step, PLANE_DEVICES)
            pltpu.make_async_remote_copy(
                src_ref=source(other),
                dst_ref=target,
                send_sem=send,
                recv_sem=recv,
                device_id=place_of(plane, other),
                device_id_type=MESH,
            ).start()
            return carry

        lax.fori_loop(1, PLANE_DEVICES, body, 0)
        pltpu.make_async_copy(source(spot), target, recv).start()

    def fan_out(chunk):
        kind, slot = divmod(chunk, SLOTS)
        ref = (k_ref, v_ref)[kind]
        first = (odd * HALF, odd * HALF + HALF, 2 * HALF * (1 - odd))[slot]
        z_stage(
            lambda other: ref.at[pl.ds(pl.multiple_of(first + ROWS * other, ROWS), ROWS), :],
            fanned.at[chunk, plane],
            z1_send.at[chunk],
            z1_recv.at[chunk],
        )

    def by_head(chunk):
        kind, slot = divmod(chunk, SLOTS)
        held = (held_k, held_v)[kind]
        shift = (0, HEADS // 2, odd * (HEADS // 2))[slot]

        def source(other):
            start = pl.multiple_of(lax.rem(other + shift, HEADS) * LANES, LANES)
            return fanned.at[chunk, :, :, pl.ds(start, LANES)]

        plane_stage(
            source,
            held.at[pl.ds((slot * PLANE_DEVICES + spot) * PLANES, PLANES)],
            p1_send.at[chunk],
            p1_recv.at[chunk],
        )

    side = spot // (HEADS // 2)
    blocks = table_ref.shape[0] // 2

    def pick(kind, slot):
        held = (held_k, held_v)[kind]
        picked = (picked_k, picked_v)[kind]

        def body(z, carry):
            first = (z // 2) * 96 + lax.rem(z, 2) * 6
            base = (slot * PLANES + z) * PLANE_DEVICES
            for p in range(PLANE_DEVICES):
                e = p % 2
                low = (True, e == 0, False)[slot]
                member = 1 if slot == 1 else 2 * e
                block = first + (p // 4) * 12 + (p % 4 // 2) * 3 + member
                chosen = side if low else 1 - side
                picked[base + p] = held[table_ref[chosen * blocks + block]]
            return carry

        lax.fori_loop(0, PLANES, body, 0)

    def send_picked(chunk):
        kind, slot = divmod(chunk, SLOTS)
        picked = (picked_k, picked_v)[kind]
        z_stage(
            lambda other: picked.at[pl.ds((slot * PLANES + other) * PLANE_DEVICES, PLANE_DEVICES)],
            landed.at[chunk, plane],
            z2_send.at[chunk],
            z2_recv.at[chunk],
        )

    def deliver(chunk):
        plane_stage(
            lambda other: landed.at[chunk, :, other],
            far_ref.at[chunk, spot],
            p2_send.at[chunk],
            p2_recv.at[chunk],
        )

    lower = lax.rem(plane, 2)
    set_rows = 4 * ROW_SET
    near_rows = rows.at[pl.ds(pl.multiple_of(lower * set_rows, ROW_SET), set_rows)]
    far_rows = rows.at[pl.ds(pl.multiple_of((1 - lower) * set_rows, ROW_SET), set_rows)]
    own_rows = rows.at[pl.ds(pl.multiple_of(head * ROW_SET, ROW_SET), ROW_SET)]

    for step in range(1, 4):
        other = spot - lax.rem(spot, 4) + lax.rem(spot + step, 4)
        pltpu.make_async_remote_copy(
            src_ref=row_ref,
            dst_ref=own_rows,
            send_sem=row_send.at[0],
            recv_sem=row_recv.at[0],
            device_id=place_of(plane, other),
            device_id_type=MESH,
        ).start()
    pltpu.make_async_copy(row_ref, own_rows, row_recv.at[0]).start()

    def share_rows():
        finish(near_rows, row_recv.at[0])
        pltpu.make_async_remote_copy(
            src_ref=near_rows,
            dst_ref=near_rows,
            send_sem=row_send.at[1],
            recv_sem=row_recv.at[1],
            device_id=place_of(plane + 1 - 2 * lower, spot),
            device_id_type=MESH,
        ).start()

    def skew_rows():
        finish(far_rows, row_recv.at[1])

        def body(i, carry):
            start = pl.multiple_of(i * ROW_SET, ROW_SET)
            some = rows[pl.ds(start, ROW_SET), :]
            for j in range(ROW_SET):
                turned = pltpu.roll(
                    jnp.broadcast_to(some[j : j + 1], (HALF, 2 * BLOCK)),
                    2 * BLOCK - HALF + 1,
                    1,
                    stride=1,
                    stride_axis=0,
                )
                skewed[start + j] = turned[:, : BLOCK + HALF]
            return carry

        lax.fori_loop(0, 2 * HEADS // ROW_SET, body, 0)
        pltpu.make_async_copy(skewed, skew_ref, skew_sem).start()

    for chunk in range(SLOTS):
        fan_out(chunk)
    for i, (source, target) in enumerate(((q_ref, mid_q_ref), (k_ref, mid_k_ref), (v_ref, mid_v_ref))):
        half_rows = pl.ds(pl.multiple_of(2 * HALF * (1 - odd), HALF), HALF)
        width = target.shape[1]
        own = pl.ds(pl.multiple_of(odd * width, LANES), width)
        given = pl.ds(pl.multiple_of((1 - odd) * width, LANES), width)
        place = target.at[pl.ds(pl.multiple_of(odd * HALF, HALF), HALF), :]
        pltpu.make_async_remote_copy(
            src_ref=source.at[half_rows, given],
            dst_ref=place,
            send_sem=half_send.at[i],
            recv_sem=half_recv.at[i],
            device_id=place_of(plane, pair),
            device_id_type=MESH,
        ).start()
        pltpu.make_async_copy(source.at[half_rows, own], place, half_recv.at[i]).start()
    for chunk in range(SLOTS):
        finish(fanned.at[chunk], z1_recv.at[chunk])
        by_head(chunk)
        fan_out(chunk + SLOTS)
    for kind in range(2):
        held = (held_k, held_v)[kind]
        for slot in range(SLOTS):
            part = held.at[pl.ds(slot * PLANE_DEVICES * PLANES, PLANE_DEVICES * PLANES)]
            finish(part, p1_recv.at[kind * SLOTS + slot])
        for slot in range(SLOTS):
            pick(kind, slot)
            send_picked(kind * SLOTS + slot)
        if kind == 0:
            share_rows()
            for chunk in range(SLOTS, 2 * SLOTS):
                finish(fanned.at[chunk], z1_recv.at[chunk])
                by_head(chunk)
            skew_rows()
    for chunk in range(2 * SLOTS):
        finish(landed.at[chunk], z2_recv.at[chunk])
        deliver(chunk)
    for i, target in enumerate((mid_q_ref, mid_k_ref, mid_v_ref)):
        finish(target, half_recv.at[i])
        finish(target.at[pl.ds(0, HALF), :], half_send.at[i])
    for chunk in range(2 * SLOTS):
        finish(fanned.at[chunk, pl.ds(0, PLANES - 1)], z1_send.at[chunk])
        finish(far_ref.at[chunk, pl.ds(0, PLANE_DEVICES - 1)], p1_send.at[chunk])
        finish(landed.at[chunk, pl.ds(0, PLANES - 1)], z2_send.at[chunk])
        finish(far_ref.at[chunk, pl.ds(0, PLANE_DEVICES - 1)], p2_send.at[chunk])
    finish(rows.at[pl.ds(0, 3 * ROW_SET)], row_send.at[0])
    finish(near_rows, row_send.at[1])
    finish(skew_ref, skew_sem)
    for chunk in range(2 * SLOTS):
        finish(far_ref.at[chunk], p2_recv.at[chunk])


def move_tiles(table, queries, keys, values, own_rows):
    rows, columns = keys.shape
    kind = keys.dtype
    chunks = 2 * SLOTS
    tiles = SLOTS * PLANES * PLANE_DEVICES
    middle = jax.ShapeDtypeStruct((BLOCK, columns // 2), kind)
    anywhere = pl.BlockSpec(memory_space=pltpu.HBM)
    semaphores = [pltpu.SemaphoreType.DMA((2,))] * 2 + [pltpu.SemaphoreType.DMA]
    semaphores += [pltpu.SemaphoreType.DMA((3,))] * 2 + [pltpu.SemaphoreType.DMA((chunks,))] * 8
    return pl.pallas_call(
        move_kernel,
        in_specs=[pl.BlockSpec(memory_space=pltpu.SMEM)]
        + [anywhere] * 3
        + [pl.BlockSpec(memory_space=pltpu.VMEM)],
        out_specs=[anywhere] * 5,
        out_shape=[
            jax.ShapeDtypeStruct((chunks, PLANE_DEVICES, PLANES, ROWS, LANES), kind),
            middle,
            middle,
            middle,
            jax.ShapeDtypeStruct((2 * HEADS, HALF, BLOCK + HALF), jnp.float32),
        ],
        scratch_shapes=[
            pltpu.VMEM((chunks, PLANES, ROWS, columns), kind),
            pltpu.VMEM((tiles, ROWS, LANES), kind),
            pltpu.VMEM((tiles, ROWS, LANES), kind),
            pltpu.VMEM((tiles, ROWS, LANES), kind),
            pltpu.VMEM((tiles, ROWS, LANES), kind),
            pltpu.VMEM((chunks, PLANES, PLANE_DEVICES, ROWS, LANES), kind),
            pltpu.VMEM((2 * HEADS, 2 * BLOCK), jnp.float32),
            pltpu.VMEM((2 * HEADS, HALF, BLOCK + HALF), jnp.float32),
        ]
        + semaphores,
        cost_estimate=pl.CostEstimate(
            flops=0, transcendentals=0, bytes_accessed=1024 * 1024 * 1024
        ),
        compiler_params=pltpu.CompilerParams(
            collective_id=0, has_side_effects=True, vmem_limit_bytes=48 * 1024 * 1024
        ),
        name="move_tiles",
    )(table, queries, keys, values, own_rows)


def attend_kernel(parity_ref, q, k, v, ka, kb, va, vb, skew, out_ref):
    scale = math.log2(math.e) / math.sqrt(LANES)
    contract = (((1,), (1,)), ((), ()))
    ones = jnp.ones((BLOCK, LANES), jnp.bfloat16)
    for g in range(GROUP):
        columns = slice(g * LANES, (g + 1) * LANES)
        near_keys = k[:, columns]
        far_keys = jnp.concatenate([half[0, g].reshape(HALF, LANES) for half in (ka, kb)], axis=0)
        far_values = jnp.concatenate([half[0, g].reshape(HALF, LANES) for half in (va, vb)], axis=0)
        near_values = jnp.concatenate([v[:, columns], ones], axis=1)
        far_values = jnp.concatenate([far_values, ones], axis=1)
        for half in range(2):
            shift = HALF * (1 - half)
            rows = slice(half * HALF, (half + 1) * HALF)
            query = q[rows, columns]
            near = lax.dot_general(query, near_keys, contract, preferred_element_type=jnp.float32)
            far = lax.dot_general(query, far_keys, contract, preferred_element_type=jnp.float32)
            near = near * scale + skew[2 * g, :, shift : shift + BLOCK]
            far = far * scale + skew[2 * g + 1, :, shift : shift + BLOCK]
            highest = jnp.max(jnp.maximum(near, far), axis=1, keepdims=True)
            near = jnp.exp2(near - highest).astype(jnp.bfloat16)
            far = jnp.exp2(far - highest).astype(jnp.bfloat16)
            summed = jnp.dot(near, near_values, preferred_element_type=jnp.float32) + jnp.dot(
                far, far_values, preferred_element_type=jnp.float32
            )
            out_ref[rows, columns] = (summed[:, :LANES] / summed[:, LANES:]).astype(jnp.bfloat16)


def attend(parity, queries, keys, values, far, skewed, middle):
    width = GROUP * LANES
    half_steps = HEADS // 2 // GROUP
    steps = half_steps if middle else 2 * half_steps

    def group_of(i, e):
        return i + half_steps * e[0] if middle else i

    def other_of(i, e):
        return lax.rem(group_of(i, e) + half_steps, 2 * half_steps)

    def slot_of(i):
        return 1 if middle else 2 * (i // half_steps)

    if middle:
        local = pl.BlockSpec((BLOCK, width), lambda i, e: (0, i))
    else:
        local = pl.BlockSpec(
            (pl.Element(BLOCK), pl.Element(width)), lambda i, e: (e[0] * HALF, i * width)
        )
    tiles = (1, GROUP, CHUNKS, ROWS, LANES)
    return pl.pallas_call(
        attend_kernel,
        grid_spec=pltpu.PrefetchScalarGridSpec(
            num_scalar_prefetch=1,
            grid=(steps,),
            in_specs=[
                local,
                local,
                local,
                pl.BlockSpec(tiles, lambda i, e: (slot_of(i), group_of(i, e), 0, 0, 0)),
                pl.BlockSpec(tiles, lambda i, e: (slot_of(i), other_of(i, e), 0, 0, 0)),
                pl.BlockSpec(tiles, lambda i, e: (SLOTS + slot_of(i), group_of(i, e), 0, 0, 0)),
                pl.BlockSpec(tiles, lambda i, e: (SLOTS + slot_of(i), other_of(i, e), 0, 0, 0)),
                pl.BlockSpec(
                    (2 * GROUP, HALF, BLOCK + HALF), lambda i, e: (group_of(i, e), 0, 0)
                ),
            ],
            out_specs=local,
        ),
        out_shape=jax.ShapeDtypeStruct(queries.shape, jnp.bfloat16),
        cost_estimate=pl.CostEstimate(
            flops=steps * GROUP * 8 * BLOCK * BLOCK * LANES,
            transcendentals=steps * GROUP * 2 * BLOCK * BLOCK,
            bytes_accessed=steps * 4 * 1024 * 1024,
        ),
        compiler_params=pltpu.CompilerParams(vmem_limit_bytes=60 * 1024 * 1024),
        name="attend_middle" if middle else "attend_whole",
    )(parity, queries, keys, values, far, far, far, far, skewed)


def place_kernel(parity_ref, own_ref, other_ref, into_ref, out_ref, sems):
    odd = parity_ref[0]
    width = own_ref.shape[1]
    rows = pl.ds(pl.multiple_of(2 * HALF * (1 - odd), HALF), HALF)
    own = pltpu.make_async_copy(
        own_ref.at[pl.ds(pl.multiple_of(odd * HALF, HALF), HALF), :],
        out_ref.at[rows, pl.ds(pl.multiple_of(odd * width, LANES), width)],
        sems.at[0],
    )
    other = pltpu.make_async_copy(
        other_ref,
        out_ref.at[rows, pl.ds(pl.multiple_of((1 - odd) * width, LANES), width)],
        sems.at[1],
    )
    own.start()
    other.start()
    own.wait()
    other.wait()


def place_half(parity, own, other, into):
    anywhere = pl.BlockSpec(memory_space=pltpu.HBM)
    return pl.pallas_call(
        place_kernel,
        in_specs=[pl.BlockSpec(memory_space=pltpu.SMEM)] + [anywhere] * 3,
        out_specs=anywhere,
        out_shape=jax.ShapeDtypeStruct(into.shape, into.dtype),
        scratch_shapes=[pltpu.SemaphoreType.DMA((2,))],
        input_output_aliases={3: 0},
        cost_estimate=pl.CostEstimate(
            flops=0, transcendentals=0, bytes_accessed=4 * HALF * own.shape[1] * 2
        ),
        compiler_params=pltpu.CompilerParams(vmem_limit_bytes=60 * 1024 * 1024),
        name="place_half",
    )(parity, own, other, into)


def tile_table(partner):
    trio = partner // 3
    member = partner - 3 * trio
    entries = []
    for source, slot in (
        (jnp.where(member == 2, 1, 0), jnp.where(member == 1, 2, 0)),
        (jnp.where(member == 0, 0, 1), jnp.where(member == 1, 2, 1)),
    ):
        device = 2 * trio + source
        seq, head = device // 8, device % 8
        plane = (seq // 8) * 2 + head // 4
        spot = (seq % 8) * 4 + head % 4
        entries.append((slot * PLANE_DEVICES + spot) * PLANES + plane)
    return jnp.concatenate(entries)


def on_device(queries, key_states, value_states, partner, buckets, bias_table):
    odd = lax.rem(lax.axis_index("head"), 2).astype(jnp.int32)
    parity = odd.reshape(1)

    one_hot = (
        buckets[..., None] == jnp.arange(bias_table.shape[0], dtype=jnp.int32)
    ).astype(jnp.float32)
    own_rows = jnp.einsum("skb,bh->hsk", one_hot, bias_table, precision=lax.Precision.HIGHEST)
    own_rows = jnp.pad(own_rows * math.log2(math.e), ((0, 0), (0, 0), (0, 1)))

    far, mid_q, mid_k, mid_v, skewed = move_tiles(
        tile_table(partner), queries, key_states, value_states, own_rows.reshape(ROW_SET, 2 * BLOCK)
    )
    middle = attend(parity, mid_q, mid_k, mid_v, far, skewed, True)
    outgoing = lax.dynamic_slice_in_dim(middle, (1 - odd) * HALF, HALF, 0)
    swap = [(i, i ^ 1) for i in range(lax.axis_size("head"))]
    incoming = lax.ppermute(outgoing, "head", swap)
    out = attend(parity, queries, key_states, value_states, far, skewed, False)
    return place_half(parity, middle, incoming, out)


def solution(mesh):
    whole = P(("seq", "head"), None)
    return jax.shard_map(
        on_device,
        mesh=mesh,
        in_specs=(whole, whole, whole, P(), P(), P(None, "head")),
        out_specs=whole,
        check_vma=False,
    )
```

```python
import math

import jax
import jax.numpy as jnp
from jax import lax
from jax.experimental import pallas as pl
from jax.experimental.pallas import tpu as pltpu
from jax.sharding import PartitionSpec as P

BLOCK = 256
HALF = 128
HEADS = 32
LANES = 128
ROWS = 16
CHUNKS = 8
GROUP = 4


MESH = pl.DeviceIdType.MESH
PLANES = 8
PLANE_DEVICES = 32
SLOTS = 3
ROW_SET = 8


def place_of(plane, spot):
    return ((plane // 2) * 8 + spot // 4, lax.rem(plane, 2) * 4 + lax.rem(spot, 4))


def move_kernel(
    table_ref,
    q_ref,
    k_ref,
    v_ref,
    row_ref,
    out_ref,
    far_ref,
    mid_q_ref,
    mid_k_ref,
    mid_v_ref,
    whole_q,
    whole_k,
    whole_v,
    whole_out,
    middle_out,
    fanned,
    held_k,
    held_v,
    picked_k,
    picked_v,
    landed,
    rows,
    skewed,
    row_send,
    row_recv,
    whole_sem,
    out_sem,
    swap_send,
    swap_recv,
    half_send,
    half_recv,
    z1_send,
    z1_recv,
    p1_send,
    p1_recv,
    z2_send,
    z2_recv,
    p2_send,
    p2_recv,
):
    seq = lax.axis_index("seq")
    head = lax.axis_index("head")
    plane = 2 * (seq // 8) + head // 4
    spot = lax.rem(seq, 8) * 4 + lax.rem(head, 4)
    odd = lax.rem(head, 2)
    pair = spot + 1 - 2 * odd

    barrier = pltpu.get_barrier_semaphore()
    for step in range(1, PLANES):
        pl.semaphore_signal(
            barrier,
            inc=1,
            device_id=place_of(lax.rem(plane + step, PLANES), spot),
            device_id_type=MESH,
        )

    def greet(step, carry):
        pl.semaphore_signal(
            barrier,
            inc=1,
            device_id=place_of(plane, lax.rem(spot + step, PLANE_DEVICES)),
            device_id_type=MESH,
        )
        return carry

    lax.fori_loop(1, PLANE_DEVICES, greet, 0)
    pl.semaphore_wait(barrier, PLANES - 1 + PLANE_DEVICES - 1)

    def finish(ref, sem):
        pltpu.make_async_copy(ref, ref, sem).wait()

    def z_stage(source, target, send, recv):
        for step in (4, 3, 5, 2, 6, 1, 7):
            other = lax.rem(plane + step, PLANES)
            pltpu.make_async_remote_copy(
                src_ref=source(other),
                dst_ref=target,
                send_sem=send,
                recv_sem=recv,
                device_id=place_of(other, spot),
                device_id_type=MESH,
            ).start()
        pltpu.make_async_copy(source(plane), target, recv).start()

    def plane_stage(source, target, send, recv):
        def body(step, carry):
            other = lax.rem(spot + step, PLANE_DEVICES)
            pltpu.make_async_remote_copy(
                src_ref=source(other),
                dst_ref=target,
                send_sem=send,
                recv_sem=recv,
                device_id=place_of(plane, other),
                device_id_type=MESH,
            ).start()
            return carry

        lax.fori_loop(1, PLANE_DEVICES, body, 0)
        pltpu.make_async_copy(source(spot), target, recv).start()

    def fan_out(chunk):
        kind, slot = divmod(chunk, SLOTS)
        ref = (k_ref, v_ref)[kind]
        first = (odd * HALF, odd * HALF + HALF, 2 * HALF * (1 - odd))[slot]
        z_stage(
            lambda other: ref.at[pl.ds(pl.multiple_of(first + ROWS * other, ROWS), ROWS), :],
            fanned.at[chunk, plane],
            z1_send.at[chunk],
            z1_recv.at[chunk],
        )

    def by_head(chunk):
        kind, slot = divmod(chunk, SLOTS)
        held = (held_k, held_v)[kind]
        shift = (0, HEADS // 2, odd * (HEADS // 2))[slot]

        def source(other):
            start = pl.multiple_of(lax.rem(other + shift, HEADS) * LANES, LANES)
            return fanned.at[chunk, :, :, pl.ds(start, LANES)]

        plane_stage(
            source,
            held.at[pl.ds((slot * PLANE_DEVICES + spot) * PLANES, PLANES)],
            p1_send.at[chunk],
            p1_recv.at[chunk],
        )

    side = spot // (HEADS // 2)
    blocks = table_ref.shape[0] // 2

    def pick(kind, slot):
        held = (held_k, held_v)[kind]
        picked = (picked_k, picked_v)[kind]

        def body(z, carry):
            first = (z // 2) * 96 + lax.rem(z, 2) * 6
            base = (slot * PLANES + z) * PLANE_DEVICES
            for p in range(PLANE_DEVICES):
                e = p % 2
                low = (True, e == 0, False)[slot]
                member = 1 if slot == 1 else 2 * e
                block = first + (p // 4) * 12 + (p % 4 // 2) * 3 + member
                chosen = side if low else 1 - side
                picked[base + p] = held[table_ref[chosen * blocks + block]]
            return carry

        lax.fori_loop(0, PLANES, body, 0)

    def send_picked(chunk):
        kind, slot = divmod(chunk, SLOTS)
        picked = (picked_k, picked_v)[kind]
        z_stage(
            lambda other: picked.at[pl.ds((slot * PLANES + other) * PLANE_DEVICES, PLANE_DEVICES)],
            landed.at[chunk, plane],
            z2_send.at[chunk],
            z2_recv.at[chunk],
        )

    def deliver(chunk):
        plane_stage(
            lambda other: landed.at[chunk, :, other],
            far_ref.at[chunk, spot],
            p2_send.at[chunk],
            p2_recv.at[chunk],
        )

    lower = lax.rem(plane, 2)
    set_rows = 4 * ROW_SET
    near_rows = rows.at[pl.ds(pl.multiple_of(lower * set_rows, ROW_SET), set_rows)]
    far_rows = rows.at[pl.ds(pl.multiple_of((1 - lower) * set_rows, ROW_SET), set_rows)]
    own_rows = rows.at[pl.ds(pl.multiple_of(head * ROW_SET, ROW_SET), ROW_SET)]

    for step in range(1, 4):
        other = spot - lax.rem(spot, 4) + lax.rem(spot + step, 4)
        pltpu.make_async_remote_copy(
            src_ref=row_ref,
            dst_ref=own_rows,
            send_sem=row_send.at[0],
            recv_sem=row_recv.at[0],
            device_id=place_of(plane, other),
            device_id_type=MESH,
        ).start()
    pltpu.make_async_copy(row_ref, own_rows, row_recv.at[0]).start()

    def share_rows():
        finish(near_rows, row_recv.at[0])
        pltpu.make_async_remote_copy(
            src_ref=near_rows,
            dst_ref=near_rows,
            send_sem=row_send.at[1],
            recv_sem=row_recv.at[1],
            device_id=place_of(plane + 1 - 2 * lower, spot),
            device_id_type=MESH,
        ).start()

    def skew_rows():
        finish(far_rows, row_recv.at[1])

        def body(i, carry):
            start = pl.multiple_of(i * ROW_SET, ROW_SET)
            some = rows[pl.ds(start, ROW_SET), :]
            for j in range(ROW_SET):
                turned = pltpu.roll(
                    jnp.broadcast_to(some[j : j + 1], (HALF, 2 * BLOCK)),
                    2 * BLOCK - HALF + 1,
                    1,
                    stride=1,
                    stride_axis=0,
                )
                skewed[start + j] = turned[:, : BLOCK + HALF]
            return carry

        lax.fori_loop(0, 2 * HEADS // ROW_SET, body, 0)

    scale = math.log2(math.e) / math.sqrt(LANES)
    contract = (((1,), (1,)), ((), ()))
    half_heads = HEADS // 2

    def attend(slot):
        middle = slot == 1
        first = (0, half_heads * odd, half_heads)[slot]
        q, k, v = (mid_q_ref, mid_k_ref, mid_v_ref) if middle else (whole_q, whole_k, whole_v)
        target = middle_out if middle else whole_out
        ones = jnp.ones((BLOCK, LANES), jnp.bfloat16)

        def body(i, carry):
            for g in range(GROUP):
                head = first + i * GROUP + g
                other = lax.rem(head + half_heads, HEADS)
                start = (i * GROUP + g if middle else head) * LANES
                columns = pl.ds(pl.multiple_of(start, LANES), LANES)
                near_keys = k[:, columns]
                near_values = jnp.concatenate([v[:, columns], ones], axis=1)
                far_keys, far_values = (
                    jnp.concatenate(
                        [far_ref[chunk, one].reshape(HALF, LANES) for one in (head, other)], axis=0
                    )
                    for chunk in (slot, SLOTS + slot)
                )
                far_values = jnp.concatenate([far_values, ones], axis=1)
                for half in range(2):
                    shift = HALF * (1 - half)
                    rows_here = slice(half * HALF, (half + 1) * HALF)
                    query = q[rows_here, columns]
                    near = lax.dot_general(
                        query, near_keys, contract, preferred_element_type=jnp.float32
                    )
                    far = lax.dot_general(
                        query, far_keys, contract, preferred_element_type=jnp.float32
                    )
                    near = near * scale + skewed[2 * head, :, shift : shift + BLOCK]
                    far = far * scale + skewed[2 * head + 1, :, shift : shift + BLOCK]
                    highest = jnp.max(jnp.maximum(near, far), axis=1, keepdims=True)
                    near = jnp.exp2(near - highest).astype(jnp.bfloat16)
                    far = jnp.exp2(far - highest).astype(jnp.bfloat16)
                    summed = jnp.dot(
                        near, near_values, preferred_element_type=jnp.float32
                    ) + jnp.dot(far, far_values, preferred_element_type=jnp.float32)
                    target[rows_here, columns] = (summed[:, :LANES] / summed[:, LANES:]).astype(
                        jnp.bfloat16
                    )
            return carry

        lax.fori_loop(0, half_heads // GROUP, body, 0)

    whole_rows = pl.ds(pl.multiple_of(odd * HALF, HALF), BLOCK)
    side_width = half_heads * LANES

    def store_whole(side):
        columns = pl.ds(side * side_width, side_width)
        return pltpu.make_async_copy(
            whole_out.at[:, columns], out_ref.at[whole_rows, columns], out_sem.at[side]
        )

    own_columns = pl.ds(pl.multiple_of(odd * side_width, LANES), side_width)
    own_place = out_ref.at[pl.ds(pl.multiple_of(2 * HALF * (1 - odd), HALF), HALF), own_columns]
    store_middle = pltpu.make_async_copy(
        middle_out.at[pl.ds(pl.multiple_of(odd * HALF, HALF), HALF), :], own_place, out_sem.at[2]
    )
    swap_middle = pltpu.make_async_remote_copy(
        src_ref=middle_out.at[pl.ds(pl.multiple_of((1 - odd) * HALF, HALF), HALF), :],
        dst_ref=out_ref.at[pl.ds(pl.multiple_of(2 * HALF * odd, HALF), HALF), own_columns],
        send_sem=swap_send,
        recv_sem=swap_recv,
        device_id=place_of(plane, pair),
        device_id_type=MESH,
    )
    loads = [
        pltpu.make_async_copy(source.at[whole_rows, :], target, whole_sem.at[i])
        for i, (source, target) in enumerate(((q_ref, whole_q), (k_ref, whole_k), (v_ref, whole_v)))
    ]

    for chunk in range(SLOTS):
        fan_out(chunk)
    for i, (source, target) in enumerate(((q_ref, mid_q_ref), (k_ref, mid_k_ref), (v_ref, mid_v_ref))):
        half_rows = pl.ds(pl.multiple_of(2 * HALF * (1 - odd), HALF), HALF)
        width = target.shape[1]
        own = pl.ds(pl.multiple_of(odd * width, LANES), width)
        given = pl.ds(pl.multiple_of((1 - odd) * width, LANES), width)
        place = target.at[pl.ds(pl.multiple_of(odd * HALF, HALF), HALF), :]
        pltpu.make_async_remote_copy(
            src_ref=source.at[half_rows, given],
            dst_ref=place,
            send_sem=half_send.at[i],
            recv_sem=half_recv.at[i],
            device_id=place_of(plane, pair),
            device_id_type=MESH,
        ).start()
        pltpu.make_async_copy(source.at[half_rows, own], place, half_recv.at[i]).start()
    for load in loads:
        load.start()
    for chunk in range(SLOTS):
        finish(fanned.at[chunk], z1_recv.at[chunk])
        by_head(chunk)
        fan_out(chunk + SLOTS)
    for kind in range(2):
        held = (held_k, held_v)[kind]
        for slot in range(SLOTS):
            part = held.at[pl.ds(slot * PLANE_DEVICES * PLANES, PLANE_DEVICES * PLANES)]
            finish(part, p1_recv.at[kind * SLOTS + slot])
        for slot in (1, 0, 2):
            pick(kind, slot)
            send_picked(kind * SLOTS + slot)
        if kind == 0:
            share_rows()
            for chunk in range(SLOTS, 2 * SLOTS):
                finish(fanned.at[chunk], z1_recv.at[chunk])
                by_head(chunk)
            skew_rows()
    for slot in (1, 0, 2):
        finish(landed.at[slot], z2_recv.at[slot])
        deliver(slot)
    for slot in (1, 0, 2):
        chunk = SLOTS + slot
        finish(landed.at[chunk], z2_recv.at[chunk])
        deliver(chunk)
        finish(far_ref.at[slot], p2_recv.at[slot])
        finish(far_ref.at[chunk], p2_recv.at[chunk])
        if slot == 1:
            for i, target in enumerate((mid_q_ref, mid_k_ref, mid_v_ref)):
                finish(target, half_recv.at[i])
            for load in loads:
                load.wait()
        attend(slot)
        if slot == 1:
            store_middle.start()
            swap_middle.start()
        else:
            store_whole(slot // 2).start()
    for i, target in enumerate((mid_q_ref, mid_k_ref, mid_v_ref)):
        finish(target.at[pl.ds(0, HALF), :], half_send.at[i])
    for chunk in range(2 * SLOTS):
        finish(fanned.at[chunk, pl.ds(0, PLANES - 1)], z1_send.at[chunk])
        finish(far_ref.at[chunk, pl.ds(0, PLANE_DEVICES - 1)], p1_send.at[chunk])
        finish(landed.at[chunk, pl.ds(0, PLANES - 1)], z2_send.at[chunk])
        finish(far_ref.at[chunk, pl.ds(0, PLANE_DEVICES - 1)], p2_send.at[chunk])
    finish(rows.at[pl.ds(0, 3 * ROW_SET)], row_send.at[0])
    finish(near_rows, row_send.at[1])
    store_middle.wait()
    swap_middle.wait()
    store_whole(0).wait()
    store_whole(1).wait()


def move_tiles(table, queries, keys, values, own_rows):
    rows, columns = keys.shape
    kind = keys.dtype
    chunks = 2 * SLOTS
    tiles = SLOTS * PLANES * PLANE_DEVICES
    anywhere = pl.BlockSpec(memory_space=pltpu.HBM)
    semaphores = (
        [pltpu.SemaphoreType.DMA((2,))] * 2
        + [pltpu.SemaphoreType.DMA((3,))] * 2
        + [pltpu.SemaphoreType.DMA] * 2
        + [pltpu.SemaphoreType.DMA((3,))] * 2
        + [pltpu.SemaphoreType.DMA((chunks,))] * 8
    )
    return pl.pallas_call(
        move_kernel,
        in_specs=[pl.BlockSpec(memory_space=pltpu.SMEM)]
        + [anywhere] * 3
        + [pl.BlockSpec(memory_space=pltpu.VMEM)],
        out_specs=anywhere,
        out_shape=jax.ShapeDtypeStruct((rows, columns), kind),
        scratch_shapes=[pltpu.VMEM((chunks, PLANE_DEVICES, PLANES, ROWS, LANES), kind)]
        + [pltpu.VMEM((BLOCK, columns // 2), kind)] * 3
        + [pltpu.VMEM((BLOCK, columns), kind)] * 4
        + [pltpu.VMEM((BLOCK, columns // 2), kind)]
        + [pltpu.VMEM((chunks, PLANES, ROWS, columns), kind)]
        + [pltpu.VMEM((tiles, ROWS, LANES), kind)] * 4
        + [
            pltpu.VMEM((chunks, PLANES, PLANE_DEVICES, ROWS, LANES), kind),
            pltpu.VMEM((2 * HEADS, 2 * BLOCK), jnp.float32),
            pltpu.VMEM((2 * HEADS, HALF, BLOCK + HALF), jnp.float32),
        ]
        + semaphores,
        cost_estimate=pl.CostEstimate(
            flops=0, transcendentals=0, bytes_accessed=1024 * 1024 * 1024
        ),
        compiler_params=pltpu.CompilerParams(
            collective_id=0, has_side_effects=True, vmem_limit_bytes=60 * 1024 * 1024
        ),
        name="move_tiles",
    )(table, queries, keys, values, own_rows)


def tile_table(partner):
    trio = partner // 3
    member = partner - 3 * trio
    entries = []
    for source, slot in (
        (jnp.where(member == 2, 1, 0), jnp.where(member == 1, 2, 0)),
        (jnp.where(member == 0, 0, 1), jnp.where(member == 1, 2, 1)),
    ):
        device = 2 * trio + source
        seq, head = device // 8, device % 8
        plane = (seq // 8) * 2 + head // 4
        spot = (seq % 8) * 4 + head % 4
        entries.append((slot * PLANE_DEVICES + spot) * PLANES + plane)
    return jnp.concatenate(entries)


def on_device(queries, key_states, value_states, partner, buckets, bias_table):
    one_hot = (
        buckets[..., None] == jnp.arange(bias_table.shape[0], dtype=jnp.int32)
    ).astype(jnp.float32)
    own_rows = jnp.einsum("skb,bh->hsk", one_hot, bias_table, precision=lax.Precision.HIGHEST)
    own_rows = jnp.pad(own_rows * math.log2(math.e), ((0, 0), (0, 0), (0, 1)))

    return move_tiles(
        tile_table(partner), queries, key_states, value_states, own_rows.reshape(ROW_SET, 2 * BLOCK)
    )


def solution(mesh):
    whole = P(("seq", "head"), None)
    return jax.shard_map(
        on_device,
        mesh=mesh,
        in_specs=(whole, whole, whole, P(), P(), P(None, "head")),
        out_specs=whole,
        check_vma=False,
    )
```

```python
import math

import jax
import jax.numpy as jnp
from jax import lax
from jax.experimental import pallas as pl
from jax.experimental.pallas import tpu as pltpu
from jax.sharding import PartitionSpec as P

BLOCK = 256
HALF = 128
HEADS = 32
LANES = 128
ROWS = 16
CHUNKS = 8
GROUP = 4


MESH = pl.DeviceIdType.MESH
PLANES = 8
PLANE_DEVICES = 32
SLOTS = 3
ROW_SET = 8
ORDER = (1, 0, 2)


def place_of(plane, spot):
    return ((plane // 2) * 8 + spot // 4, lax.rem(plane, 2) * 4 + lax.rem(spot, 4))


def move_kernel(
    table_ref,
    q_ref,
    k_ref,
    v_ref,
    row_ref,
    out_ref,
    far_ref,
    mid_q_ref,
    mid_k_ref,
    mid_v_ref,
    whole_q,
    whole_k,
    whole_v,
    whole_out,
    middle_out,
    weights,
    fanned,
    held_k,
    held_v,
    picked_k,
    picked_v,
    landed,
    rows,
    skewed,
    row_send,
    row_recv,
    whole_sem,
    out_sem,
    swap_send,
    swap_recv,
    half_send,
    half_recv,
    z1_send,
    z1_recv,
    p1_send,
    p1_recv,
    z2_send,
    z2_recv,
    p2_send,
    p2_recv,
):
    seq = lax.axis_index("seq")
    head = lax.axis_index("head")
    plane = 2 * (seq // 8) + head // 4
    spot = lax.rem(seq, 8) * 4 + lax.rem(head, 4)
    odd = lax.rem(head, 2)
    pair = spot + 1 - 2 * odd

    barrier = pltpu.get_barrier_semaphore()
    for step in range(1, PLANES):
        pl.semaphore_signal(
            barrier,
            inc=1,
            device_id=place_of(lax.rem(plane + step, PLANES), spot),
            device_id_type=MESH,
        )

    def greet(step, carry):
        pl.semaphore_signal(
            barrier,
            inc=1,
            device_id=place_of(plane, lax.rem(spot + step, PLANE_DEVICES)),
            device_id_type=MESH,
        )
        return carry

    lax.fori_loop(1, PLANE_DEVICES, greet, 0)
    pl.semaphore_wait(barrier, PLANES - 1 + PLANE_DEVICES - 1)

    def finish(ref, sem):
        pltpu.make_async_copy(ref, ref, sem).wait()

    def z_stage(source, target, send, recv):
        for step in (4, 3, 5, 2, 6, 1, 7):
            other = lax.rem(plane + step, PLANES)
            pltpu.make_async_remote_copy(
                src_ref=source(other),
                dst_ref=target,
                send_sem=send,
                recv_sem=recv,
                device_id=place_of(other, spot),
                device_id_type=MESH,
            ).start()
        pltpu.make_async_copy(source(plane), target, recv).start()

    def plane_stage(source, target, send, recv):
        def body(step, carry):
            other = lax.rem(spot + step, PLANE_DEVICES)
            pltpu.make_async_remote_copy(
                src_ref=source(other),
                dst_ref=target,
                send_sem=send,
                recv_sem=recv,
                device_id=place_of(plane, other),
                device_id_type=MESH,
            ).start()
            return carry

        lax.fori_loop(1, PLANE_DEVICES, body, 0)
        pltpu.make_async_copy(source(spot), target, recv).start()

    def fan_out(chunk):
        kind, slot = divmod(chunk, SLOTS)
        ref = (k_ref, v_ref)[kind]
        first = (odd * HALF, odd * HALF + HALF, 2 * HALF * (1 - odd))[slot]
        z_stage(
            lambda other: ref.at[pl.ds(pl.multiple_of(first + ROWS * other, ROWS), ROWS), :],
            fanned.at[chunk, plane],
            z1_send.at[chunk],
            z1_recv.at[chunk],
        )

    def by_head(chunk):
        kind, slot = divmod(chunk, SLOTS)
        held = (held_k, held_v)[kind]
        shift = (0, HEADS // 2, odd * (HEADS // 2))[slot]

        def source(other):
            start = pl.multiple_of(lax.rem(other + shift, HEADS) * LANES, LANES)
            return fanned.at[chunk, :, :, pl.ds(start, LANES)]

        plane_stage(
            source,
            held.at[pl.ds((slot * PLANE_DEVICES + spot) * PLANES, PLANES)],
            p1_send.at[chunk],
            p1_recv.at[chunk],
        )

    side = spot // (HEADS // 2)
    blocks = table_ref.shape[0] // 2

    def pick(kind, slot):
        held = (held_k, held_v)[kind]
        picked = (picked_k, picked_v)[kind]

        def body(z, carry):
            first = (z // 2) * 96 + lax.rem(z, 2) * 6
            base = slot * PLANES * PLANE_DEVICES + z
            for p in range(PLANE_DEVICES):
                e = p % 2
                low = (True, e == 0, False)[slot]
                member = 1 if slot == 1 else 2 * e
                block = first + (p // 4) * 12 + (p % 4 // 2) * 3 + member
                chosen = side if low else 1 - side
                picked[base + p * PLANES] = held[table_ref[chosen * blocks + block]]
            return carry

        lax.fori_loop(0, PLANES, body, 0)

    def share_picked(chunk):
        kind, slot = divmod(chunk, SLOTS)
        picked = (picked_k, picked_v)[kind]
        plane_stage(
            lambda other: picked.at[pl.ds((slot * PLANE_DEVICES + other) * PLANES, PLANES)],
            landed.at[chunk, :, spot],
            p2_send.at[chunk],
            p2_recv.at[chunk],
        )

    def deliver(chunk):
        finish(landed.at[chunk], p2_recv.at[chunk])
        z_stage(
            lambda other: landed.at[chunk, other],
            far_ref.at[chunk, plane],
            z2_send.at[chunk],
            z2_recv.at[chunk],
        )

    lower = lax.rem(plane, 2)
    set_rows = 4 * ROW_SET
    near_rows = rows.at[pl.ds(pl.multiple_of(lower * set_rows, ROW_SET), set_rows)]
    far_rows = rows.at[pl.ds(pl.multiple_of((1 - lower) * set_rows, ROW_SET), set_rows)]
    own_rows = rows.at[pl.ds(pl.multiple_of(head * ROW_SET, ROW_SET), ROW_SET)]

    for step in range(1, 4):
        other = spot - lax.rem(spot, 4) + lax.rem(spot + step, 4)
        pltpu.make_async_remote_copy(
            src_ref=row_ref,
            dst_ref=own_rows,
            send_sem=row_send.at[0],
            recv_sem=row_recv.at[0],
            device_id=place_of(plane, other),
            device_id_type=MESH,
        ).start()
    pltpu.make_async_copy(row_ref, own_rows, row_recv.at[0]).start()

    def share_rows():
        finish(near_rows, row_recv.at[0])
        pltpu.make_async_remote_copy(
            src_ref=near_rows,
            dst_ref=near_rows,
            send_sem=row_send.at[1],
            recv_sem=row_recv.at[1],
            device_id=place_of(plane + 1 - 2 * lower, spot),
            device_id_type=MESH,
        ).start()

    def skew_rows():
        finish(far_rows, row_recv.at[1])

        def body(i, carry):
            start = pl.multiple_of(i * ROW_SET, ROW_SET)
            some = rows[pl.ds(start, ROW_SET), :]
            for j in range(ROW_SET):
                turned = pltpu.roll(
                    jnp.broadcast_to(some[j : j + 1], (HALF, 2 * BLOCK)),
                    2 * BLOCK - HALF + 1,
                    1,
                    stride=1,
                    stride_axis=0,
                )
                skewed[start + j] = turned[:, : BLOCK + HALF]
            return carry

        lax.fori_loop(0, 2 * HEADS // ROW_SET, body, 0)

    scale = math.log2(math.e) / math.sqrt(LANES)
    contract = (((1,), (1,)), ((), ()))
    half_heads = HEADS // 2

    ones = jnp.ones((BLOCK, LANES), jnp.bfloat16)

    def far_block(chunk, head):
        other = lax.rem(head + half_heads, HEADS)
        return jnp.concatenate(
            [far_ref[chunk, :, one].reshape(HALF, LANES) for one in (head, other)], axis=0
        )

    def weigh(query, near_keys, far_keys, head, half):
        shift = HALF * (1 - half)
        near = lax.dot_general(query, near_keys, contract, preferred_element_type=jnp.float32)
        far = lax.dot_general(query, far_keys, contract, preferred_element_type=jnp.float32)
        near = near * scale + skewed[2 * head, :, shift : shift + BLOCK]
        far = far * scale + skewed[2 * head + 1, :, shift : shift + BLOCK]
        highest = jnp.max(jnp.maximum(near, far), axis=1, keepdims=True)
        return tuple(jnp.exp2(part - highest).astype(jnp.bfloat16) for part in (near, far))

    def blend(near, far, near_values, far_values):
        summed = jnp.dot(near, near_values, preferred_element_type=jnp.float32) + jnp.dot(
            far, far_values, preferred_element_type=jnp.float32
        )
        return (summed[:, :LANES] / summed[:, LANES:]).astype(jnp.bfloat16)

    def over_heads(slot, visit):
        middle = slot == 1
        first = (0, half_heads * odd, half_heads)[slot]

        def body(i, carry):
            for g in range(GROUP):
                place = i * GROUP + g
                start = (place if middle else first + place) * LANES
                visit(place, first + place, pl.ds(pl.multiple_of(start, LANES), LANES))
            return carry

        lax.fori_loop(0, half_heads // GROUP, body, 0)

    def attend(slot):
        middle = slot == 1
        q, k, v = (mid_q_ref, mid_k_ref, mid_v_ref) if middle else (whole_q, whole_k, whole_v)
        target = middle_out if middle else whole_out

        def visit(place, head, columns):
            near_keys = k[:, columns]
            far_keys = far_block(slot, head)
            near_values = jnp.concatenate([v[:, columns], ones], axis=1)
            far_values = jnp.concatenate([far_block(SLOTS + slot, head), ones], axis=1)
            for half in range(2):
                part = slice(half * HALF, (half + 1) * HALF)
                near, far = weigh(q[part, columns], near_keys, far_keys, head, half)
                target[part, columns] = blend(near, far, near_values, far_values)

        over_heads(slot, visit)

    def weigh_last():
        def visit(place, head, columns):
            near_keys = whole_k[:, columns]
            far_keys = far_block(2, head)
            for half in range(2):
                part = slice(half * HALF, (half + 1) * HALF)
                near, far = weigh(whole_q[part, columns], near_keys, far_keys, head, half)
                weights[place, part, :BLOCK] = near
                weights[place, part, BLOCK:] = far

        over_heads(2, visit)

    def blend_last():
        def visit(place, head, columns):
            near_values = jnp.concatenate([whole_v[:, columns], ones], axis=1)
            far_values = jnp.concatenate([far_block(SLOTS + 2, head), ones], axis=1)
            whole_out[:, columns] = blend(
                weights[place, :, :BLOCK], weights[place, :, BLOCK:], near_values, far_values
            )

        over_heads(2, visit)

    whole_rows = pl.ds(pl.multiple_of(odd * HALF, HALF), BLOCK)
    side_width = half_heads * LANES

    def store_whole(side):
        columns = pl.ds(side * side_width, side_width)
        return pltpu.make_async_copy(
            whole_out.at[:, columns], out_ref.at[whole_rows, columns], out_sem.at[side]
        )

    own_columns = pl.ds(pl.multiple_of(odd * side_width, LANES), side_width)
    own_place = out_ref.at[pl.ds(pl.multiple_of(2 * HALF * (1 - odd), HALF), HALF), own_columns]
    store_middle = pltpu.make_async_copy(
        middle_out.at[pl.ds(pl.multiple_of(odd * HALF, HALF), HALF), :], own_place, out_sem.at[2]
    )
    swap_middle = pltpu.make_async_remote_copy(
        src_ref=middle_out.at[pl.ds(pl.multiple_of((1 - odd) * HALF, HALF), HALF), :],
        dst_ref=out_ref.at[pl.ds(pl.multiple_of(2 * HALF * odd, HALF), HALF), own_columns],
        send_sem=swap_send,
        recv_sem=swap_recv,
        device_id=place_of(plane, pair),
        device_id_type=MESH,
    )
    loads = [
        pltpu.make_async_copy(source.at[whole_rows, :], target, whole_sem.at[i])
        for i, (source, target) in enumerate(((q_ref, whole_q), (k_ref, whole_k), (v_ref, whole_v)))
    ]

    for chunk in range(SLOTS):
        fan_out(chunk)
    for i, (source, target) in enumerate(((q_ref, mid_q_ref), (k_ref, mid_k_ref), (v_ref, mid_v_ref))):
        half_rows = pl.ds(pl.multiple_of(2 * HALF * (1 - odd), HALF), HALF)
        width = target.shape[1]
        own = pl.ds(pl.multiple_of(odd * width, LANES), width)
        given = pl.ds(pl.multiple_of((1 - odd) * width, LANES), width)
        place = target.at[pl.ds(pl.multiple_of(odd * HALF, HALF), HALF), :]
        pltpu.make_async_remote_copy(
            src_ref=source.at[half_rows, given],
            dst_ref=place,
            send_sem=half_send.at[i],
            recv_sem=half_recv.at[i],
            device_id=place_of(plane, pair),
            device_id_type=MESH,
        ).start()
        pltpu.make_async_copy(source.at[half_rows, own], place, half_recv.at[i]).start()
    for load in loads:
        load.start()
    def choose(kind):
        held = (held_k, held_v)[kind]
        for slot in range(SLOTS):
            part = held.at[pl.ds(slot * PLANE_DEVICES * PLANES, PLANE_DEVICES * PLANES)]
            finish(part, p1_recv.at[kind * SLOTS + slot])
        for slot in ORDER:
            pick(kind, slot)
            share_picked(kind * SLOTS + slot)

    for chunk in range(SLOTS):
        finish(fanned.at[chunk], z1_recv.at[chunk])
        by_head(chunk)
        fan_out(chunk + SLOTS)
    choose(0)
    share_rows()
    for i, slot in enumerate(ORDER):
        finish(fanned.at[SLOTS + i], z1_recv.at[SLOTS + i])
        by_head(SLOTS + i)
        deliver(slot)
    skew_rows()
    choose(1)
    for slot in ORDER:
        deliver(SLOTS + slot)
    for slot in ORDER:
        finish(far_ref.at[slot], z2_recv.at[slot])
    for i, target in enumerate((mid_q_ref, mid_k_ref, mid_v_ref)):
        finish(target, half_recv.at[i])
    for load in loads:
        load.wait()
    weigh_last()
    for slot in ORDER:
        finish(far_ref.at[SLOTS + slot], z2_recv.at[SLOTS + slot])
        if slot == 2:
            blend_last()
        else:
            attend(slot)
        if slot == 1:
            store_middle.start()
            swap_middle.start()
        else:
            store_whole(slot // 2).start()
    for i, target in enumerate((mid_q_ref, mid_k_ref, mid_v_ref)):
        finish(target.at[pl.ds(0, HALF), :], half_send.at[i])
    for chunk in range(2 * SLOTS):
        finish(fanned.at[chunk, pl.ds(0, PLANES - 1)], z1_send.at[chunk])
        finish(landed.at[chunk, :, pl.ds(0, PLANE_DEVICES - 1)], p1_send.at[chunk])
        finish(landed.at[chunk, :, pl.ds(0, PLANE_DEVICES - 1)], p2_send.at[chunk])
        finish(landed.at[chunk, pl.ds(0, PLANES - 1)], z2_send.at[chunk])
    finish(rows.at[pl.ds(0, 3 * ROW_SET)], row_send.at[0])
    finish(near_rows, row_send.at[1])
    store_middle.wait()
    swap_middle.wait()
    store_whole(0).wait()
    store_whole(1).wait()


def move_tiles(table, queries, keys, values, own_rows):
    rows, columns = keys.shape
    kind = keys.dtype
    chunks = 2 * SLOTS
    tiles = SLOTS * PLANES * PLANE_DEVICES
    anywhere = pl.BlockSpec(memory_space=pltpu.HBM)
    semaphores = (
        [pltpu.SemaphoreType.DMA((2,))] * 2
        + [pltpu.SemaphoreType.DMA((3,))] * 2
        + [pltpu.SemaphoreType.DMA] * 2
        + [pltpu.SemaphoreType.DMA((3,))] * 2
        + [pltpu.SemaphoreType.DMA((chunks,))] * 8
    )
    return pl.pallas_call(
        move_kernel,
        in_specs=[pl.BlockSpec(memory_space=pltpu.SMEM)]
        + [anywhere] * 3
        + [pl.BlockSpec(memory_space=pltpu.VMEM)],
        out_specs=anywhere,
        out_shape=jax.ShapeDtypeStruct((rows, columns), kind),
        scratch_shapes=[pltpu.VMEM((chunks, PLANES, PLANE_DEVICES, ROWS, LANES), kind)]
        + [pltpu.VMEM((BLOCK, columns // 2), kind)] * 3
        + [pltpu.VMEM((BLOCK, columns), kind)] * 4
        + [pltpu.VMEM((BLOCK, columns // 2), kind)]
        + [pltpu.VMEM((HEADS // 2, BLOCK, 2 * BLOCK), kind)]
        + [pltpu.VMEM((chunks, PLANES, ROWS, columns), kind)]
        + [pltpu.VMEM((tiles, ROWS, LANES), kind)] * 4
        + [
            pltpu.VMEM((chunks, PLANES, PLANE_DEVICES, ROWS, LANES), kind),
            pltpu.VMEM((2 * HEADS, 2 * BLOCK), jnp.float32),
            pltpu.VMEM((2 * HEADS, HALF, BLOCK + HALF), jnp.float32),
        ]
        + semaphores,
        cost_estimate=pl.CostEstimate(
            flops=0, transcendentals=0, bytes_accessed=1024 * 1024 * 1024
        ),
        compiler_params=pltpu.CompilerParams(
            collective_id=0, has_side_effects=True, vmem_limit_bytes=60 * 1024 * 1024
        ),
        name="move_tiles",
    )(table, queries, keys, values, own_rows)


def tile_table(partner):
    trio = partner // 3
    member = partner - 3 * trio
    entries = []
    for source, slot in (
        (jnp.where(member == 2, 1, 0), jnp.where(member == 1, 2, 0)),
        (jnp.where(member == 0, 0, 1), jnp.where(member == 1, 2, 1)),
    ):
        device = 2 * trio + source
        seq, head = device // 8, device % 8
        plane = (seq // 8) * 2 + head // 4
        spot = (seq % 8) * 4 + head % 4
        entries.append((slot * PLANE_DEVICES + spot) * PLANES + plane)
    return jnp.concatenate(entries)


def on_device(queries, key_states, value_states, partner, buckets, bias_table):
    one_hot = (
        buckets[..., None] == jnp.arange(bias_table.shape[0], dtype=jnp.int32)
    ).astype(jnp.float32)
    own_rows = jnp.einsum("skb,bh->hsk", one_hot, bias_table, precision=lax.Precision.HIGHEST)
    own_rows = jnp.pad(own_rows * math.log2(math.e), ((0, 0), (0, 0), (0, 1)))

    return move_tiles(
        tile_table(partner), queries, key_states, value_states, own_rows.reshape(ROW_SET, 2 * BLOCK)
    )


def solution(mesh):
    whole = P(("seq", "head"), None)
    return jax.shard_map(
        on_device,
        mesh=mesh,
        in_specs=(whole, whole, whole, P(), P(), P(None, "head")),
        out_specs=whole,
        check_vma=False,
    )
```

```python
import math

import jax
import jax.numpy as jnp
from jax import lax
from jax.experimental import pallas as pl
from jax.experimental.pallas import tpu as pltpu
from jax.sharding import PartitionSpec as P

BLOCK = 256
HALF = 128
HEADS = 32
LANES = 128
ROWS = 16
CHUNKS = 8
GROUP = 4


MESH = pl.DeviceIdType.MESH
PLANES = 8
PLANE_DEVICES = 32
SLOTS = 3
ROW_SET = 8
ORDER = (1, 0, 2)


def place_of(plane, spot):
    return ((plane // 2) * 8 + spot // 4, lax.rem(plane, 2) * 4 + lax.rem(spot, 4))


def move_kernel(
    table_ref,
    q_ref,
    k_ref,
    v_ref,
    row_ref,
    out_ref,
    far_ref,
    mid_q_ref,
    mid_k_ref,
    mid_v_ref,
    whole_q,
    whole_k,
    whole_v,
    whole_out,
    middle_out,
    weights,
    fanned,
    held_k,
    held_v,
    picked_k,
    picked_v,
    landed,
    rows,
    skewed,
    row_send,
    row_recv,
    whole_sem,
    out_sem,
    swap_send,
    swap_recv,
    half_send,
    half_recv,
    z1_send,
    z1_recv,
    p1_send,
    p1_recv,
    z2_send,
    z2_recv,
    p2_send,
    p2_recv,
):
    seq = lax.axis_index("seq")
    head = lax.axis_index("head")
    plane = 2 * (seq // 8) + head // 4
    spot = lax.rem(seq, 8) * 4 + lax.rem(head, 4)
    odd = lax.rem(head, 2)
    pair = spot + 1 - 2 * odd

    barrier = pltpu.get_barrier_semaphore()
    for step in range(1, PLANES):
        pl.semaphore_signal(
            barrier,
            inc=1,
            device_id=place_of(lax.rem(plane + step, PLANES), spot),
            device_id_type=MESH,
        )

    def greet(step, carry):
        pl.semaphore_signal(
            barrier,
            inc=1,
            device_id=place_of(plane, lax.rem(spot + step, PLANE_DEVICES)),
            device_id_type=MESH,
        )
        return carry

    lax.fori_loop(1, PLANE_DEVICES, greet, 0)
    pl.semaphore_wait(barrier, PLANES - 1 + PLANE_DEVICES - 1)

    def finish(ref, sem):
        pltpu.make_async_copy(ref, ref, sem).wait()

    def z_stage(source, target, send, recv):
        for step in (4, 3, 5, 2, 6, 1, 7):
            other = lax.rem(plane + step, PLANES)
            pltpu.make_async_remote_copy(
                src_ref=source(other),
                dst_ref=target,
                send_sem=send,
                recv_sem=recv,
                device_id=place_of(other, spot),
                device_id_type=MESH,
            ).start()
        pltpu.make_async_copy(source(plane), target, recv).start()

    def plane_stage(source, target, send, recv):
        def body(step, carry):
            other = lax.rem(spot + step, PLANE_DEVICES)
            pltpu.make_async_remote_copy(
                src_ref=source(other),
                dst_ref=target,
                send_sem=send,
                recv_sem=recv,
                device_id=place_of(plane, other),
                device_id_type=MESH,
            ).start()
            return carry

        lax.fori_loop(1, PLANE_DEVICES, body, 0)
        pltpu.make_async_copy(source(spot), target, recv).start()

    def fan_out(chunk):
        kind, slot = divmod(chunk, SLOTS)
        ref = (k_ref, v_ref)[kind]
        first = (odd * HALF, odd * HALF + HALF, 2 * HALF * (1 - odd))[slot]
        z_stage(
            lambda other: ref.at[pl.ds(pl.multiple_of(first + ROWS * other, ROWS), ROWS), :],
            fanned.at[chunk, plane],
            z1_send.at[chunk],
            z1_recv.at[chunk],
        )

    def by_head(chunk):
        kind, slot = divmod(chunk, SLOTS)
        held = (held_k, held_v)[kind]
        shift = (0, HEADS // 2, odd * (HEADS // 2))[slot]

        def source(other):
            start = pl.multiple_of(lax.rem(other + shift, HEADS) * LANES, LANES)
            return fanned.at[chunk, :, :, pl.ds(start, LANES)]

        plane_stage(
            source,
            held.at[pl.ds((slot * PLANE_DEVICES + spot) * PLANES, PLANES)],
            p1_send.at[chunk],
            p1_recv.at[chunk],
        )

    side = spot // (HEADS // 2)
    blocks = table_ref.shape[0] // 2

    def pick(kind, slot):
        held = (held_k, held_v)[kind]
        picked = (picked_k, picked_v)[kind]

        def body(z, carry):
            first = (z // 2) * 96 + lax.rem(z, 2) * 6
            base = slot * PLANES * PLANE_DEVICES + z
            for p in range(PLANE_DEVICES):
                e = p % 2
                low = (True, e == 0, False)[slot]
                member = 1 if slot == 1 else 2 * e
                block = first + (p // 4) * 12 + (p % 4 // 2) * 3 + member
                chosen = side if low else 1 - side
                picked[base + p * PLANES] = held[table_ref[chosen * blocks + block]]
            return carry

        lax.fori_loop(0, PLANES, body, 0)

    def share_picked(chunk):
        kind, slot = divmod(chunk, SLOTS)
        picked = (picked_k, picked_v)[kind]
        plane_stage(
            lambda other: picked.at[pl.ds((slot * PLANE_DEVICES + other) * PLANES, PLANES)],
            landed.at[chunk, :, spot],
            p2_send.at[chunk],
            p2_recv.at[chunk],
        )

    def deliver(chunk):
        finish(landed.at[chunk], p2_recv.at[chunk])
        z_stage(
            lambda other: landed.at[chunk, other],
            far_ref.at[chunk, plane],
            z2_send.at[chunk],
            z2_recv.at[chunk],
        )

    lower = lax.rem(plane, 2)
    set_rows = 4 * ROW_SET
    near_rows = rows.at[pl.ds(pl.multiple_of(lower * set_rows, ROW_SET), set_rows)]
    far_rows = rows.at[pl.ds(pl.multiple_of((1 - lower) * set_rows, ROW_SET), set_rows)]
    own_rows = rows.at[pl.ds(pl.multiple_of(head * ROW_SET, ROW_SET), ROW_SET)]

    for step in range(1, 4):
        other = spot - lax.rem(spot, 4) + lax.rem(spot + step, 4)
        pltpu.make_async_remote_copy(
            src_ref=row_ref,
            dst_ref=own_rows,
            send_sem=row_send.at[0],
            recv_sem=row_recv.at[0],
            device_id=place_of(plane, other),
            device_id_type=MESH,
        ).start()
    pltpu.make_async_copy(row_ref, own_rows, row_recv.at[0]).start()

    def share_rows():
        finish(near_rows, row_recv.at[0])
        pltpu.make_async_remote_copy(
            src_ref=near_rows,
            dst_ref=near_rows,
            send_sem=row_send.at[1],
            recv_sem=row_recv.at[1],
            device_id=place_of(plane + 1 - 2 * lower, spot),
            device_id_type=MESH,
        ).start()

    def skew_rows():
        finish(far_rows, row_recv.at[1])

        def body(i, carry):
            start = pl.multiple_of(i * ROW_SET, ROW_SET)
            some = rows[pl.ds(start, ROW_SET), :]
            for j in range(ROW_SET):
                turned = pltpu.roll(
                    jnp.broadcast_to(some[j : j + 1], (HALF, 2 * BLOCK)),
                    2 * BLOCK - HALF + 1,
                    1,
                    stride=1,
                    stride_axis=0,
                )
                skewed[start + j] = turned[:, : BLOCK + HALF]
            return carry

        lax.fori_loop(0, 2 * HEADS // ROW_SET, body, 0)

    scale = math.log2(math.e) / math.sqrt(LANES)
    contract = (((1,), (1,)), ((), ()))
    half_heads = HEADS // 2

    ones = jnp.ones((BLOCK, LANES), jnp.bfloat16)

    def far_block(chunk, head):
        other = lax.rem(head + half_heads, HEADS)
        return jnp.concatenate(
            [far_ref[chunk, :, one].reshape(HALF, LANES) for one in (head, other)], axis=0
        )

    def weigh(query, near_keys, far_keys, head, half):
        shift = HALF * (1 - half)
        near = lax.dot_general(query, near_keys, contract, preferred_element_type=jnp.float32)
        far = lax.dot_general(query, far_keys, contract, preferred_element_type=jnp.float32)
        near = near * scale + skewed[2 * head, :, shift : shift + BLOCK]
        far = far * scale + skewed[2 * head + 1, :, shift : shift + BLOCK]
        highest = jnp.max(jnp.maximum(near, far), axis=1, keepdims=True)
        return tuple(jnp.exp2(part - highest).astype(jnp.bfloat16) for part in (near, far))

    def blend(near, far, near_values, far_values):
        summed = jnp.dot(near, near_values, preferred_element_type=jnp.float32) + jnp.dot(
            far, far_values, preferred_element_type=jnp.float32
        )
        return (summed[:, :LANES] / summed[:, LANES:]).astype(jnp.bfloat16)

    def over_heads(slot, visit):
        middle = slot == 1
        first = (0, half_heads * odd, half_heads)[slot]

        def body(i, carry):
            for g in range(GROUP):
                place = i * GROUP + g
                start = (place if middle else first + place) * LANES
                visit(place, first + place, pl.ds(pl.multiple_of(start, LANES), LANES))
            return carry

        lax.fori_loop(0, half_heads // GROUP, body, 0)

    def attend(slot):
        middle = slot == 1
        q, k, v = (mid_q_ref, mid_k_ref, mid_v_ref) if middle else (whole_q, whole_k, whole_v)
        target = middle_out if middle else whole_out

        def visit(place, head, columns):
            near_keys = k[:, columns]
            far_keys = far_block(slot, head)
            near_values = jnp.concatenate([v[:, columns], ones], axis=1)
            far_values = jnp.concatenate([far_block(SLOTS + slot, head), ones], axis=1)
            for half in range(2):
                part = slice(half * HALF, (half + 1) * HALF)
                near, far = weigh(q[part, columns], near_keys, far_keys, head, half)
                target[part, columns] = blend(near, far, near_values, far_values)

        over_heads(slot, visit)

    def weigh_last():
        def visit(place, head, columns):
            near_keys = whole_k[:, columns]
            far_keys = far_block(2, head)
            for half in range(2):
                part = slice(half * HALF, (half + 1) * HALF)
                near, far = weigh(whole_q[part, columns], near_keys, far_keys, head, half)
                weights[place, part, :BLOCK] = near
                weights[place, part, BLOCK:] = far

        over_heads(2, visit)

    def blend_last():
        def visit(place, head, columns):
            near_values = jnp.concatenate([whole_v[:, columns], ones], axis=1)
            far_values = jnp.concatenate([far_block(SLOTS + 2, head), ones], axis=1)
            whole_out[:, columns] = blend(
                weights[place, :, :BLOCK], weights[place, :, BLOCK:], near_values, far_values
            )

        over_heads(2, visit)

    whole_rows = pl.ds(pl.multiple_of(odd * HALF, HALF), BLOCK)
    side_width = half_heads * LANES

    def store_whole(side):
        columns = pl.ds(side * side_width, side_width)
        return pltpu.make_async_copy(
            whole_out.at[:, columns], out_ref.at[whole_rows, columns], out_sem.at[side]
        )

    own_columns = pl.ds(pl.multiple_of(odd * side_width, LANES), side_width)
    own_place = out_ref.at[pl.ds(pl.multiple_of(2 * HALF * (1 - odd), HALF), HALF), own_columns]
    store_middle = pltpu.make_async_copy(
        middle_out.at[pl.ds(pl.multiple_of(odd * HALF, HALF), HALF), :], own_place, out_sem.at[2]
    )
    swap_middle = pltpu.make_async_remote_copy(
        src_ref=middle_out.at[pl.ds(pl.multiple_of((1 - odd) * HALF, HALF), HALF), :],
        dst_ref=out_ref.at[pl.ds(pl.multiple_of(2 * HALF * odd, HALF), HALF), own_columns],
        send_sem=swap_send,
        recv_sem=swap_recv,
        device_id=place_of(plane, pair),
        device_id_type=MESH,
    )
    loads = [
        pltpu.make_async_copy(source.at[whole_rows, :], target, whole_sem.at[i])
        for i, (source, target) in enumerate(((q_ref, whole_q), (k_ref, whole_k), (v_ref, whole_v)))
    ]

    for chunk in range(SLOTS):
        fan_out(chunk)
    for i, (source, target) in enumerate(((q_ref, mid_q_ref), (k_ref, mid_k_ref), (v_ref, mid_v_ref))):
        half_rows = pl.ds(pl.multiple_of(2 * HALF * (1 - odd), HALF), HALF)
        width = target.shape[1]
        own = pl.ds(pl.multiple_of(odd * width, LANES), width)
        given = pl.ds(pl.multiple_of((1 - odd) * width, LANES), width)
        place = target.at[pl.ds(pl.multiple_of(odd * HALF, HALF), HALF), :]
        pltpu.make_async_remote_copy(
            src_ref=source.at[half_rows, given],
            dst_ref=place,
            send_sem=half_send.at[i],
            recv_sem=half_recv.at[i],
            device_id=place_of(plane, pair),
            device_id_type=MESH,
        ).start()
        pltpu.make_async_copy(source.at[half_rows, own], place, half_recv.at[i]).start()
    for load in loads:
        load.start()
    def choose(kind):
        held = (held_k, held_v)[kind]
        for slot in range(SLOTS):
            part = held.at[pl.ds(slot * PLANE_DEVICES * PLANES, PLANE_DEVICES * PLANES)]
            finish(part, p1_recv.at[kind * SLOTS + slot])
        for slot in ORDER:
            pick(kind, slot)
            share_picked(kind * SLOTS + slot)

    for chunk in range(SLOTS):
        finish(fanned.at[chunk], z1_recv.at[chunk])
        by_head(chunk)
        fan_out(chunk + SLOTS)
    choose(0)
    share_rows()
    for i, slot in enumerate(ORDER):
        finish(fanned.at[SLOTS + i], z1_recv.at[SLOTS + i])
        by_head(SLOTS + i)
        deliver(slot)
    skew_rows()
    choose(1)
    for slot in ORDER:
        deliver(SLOTS + slot)
    for slot in ORDER:
        finish(far_ref.at[slot], z2_recv.at[slot])
    for i, target in enumerate((mid_q_ref, mid_k_ref, mid_v_ref)):
        finish(target, half_recv.at[i])
    for load in loads:
        load.wait()
    weigh_last()
    for slot in ORDER:
        finish(far_ref.at[SLOTS + slot], z2_recv.at[SLOTS + slot])
        if slot == 2:
            blend_last()
        else:
            attend(slot)
        if slot == 1:
            store_middle.start()
            swap_middle.start()
        else:
            store_whole(slot // 2).start()
    for i, target in enumerate((mid_q_ref, mid_k_ref, mid_v_ref)):
        finish(target.at[pl.ds(0, HALF), :], half_send.at[i])
    for chunk in range(2 * SLOTS):
        finish(fanned.at[chunk, pl.ds(0, PLANES - 1)], z1_send.at[chunk])
        finish(landed.at[chunk, :, pl.ds(0, PLANE_DEVICES - 1)], p1_send.at[chunk])
        finish(landed.at[chunk, :, pl.ds(0, PLANE_DEVICES - 1)], p2_send.at[chunk])
        finish(landed.at[chunk, pl.ds(0, PLANES - 1)], z2_send.at[chunk])
    finish(rows.at[pl.ds(0, 3 * ROW_SET)], row_send.at[0])
    finish(near_rows, row_send.at[1])
    store_middle.wait()
    swap_middle.wait()
    store_whole(0).wait()
    store_whole(1).wait()


def move_tiles(table, queries, keys, values, own_rows):
    rows, columns = keys.shape
    kind = keys.dtype
    chunks = 2 * SLOTS
    tiles = SLOTS * PLANES * PLANE_DEVICES
    anywhere = pl.BlockSpec(memory_space=pltpu.HBM)
    semaphores = (
        [pltpu.SemaphoreType.DMA((2,))] * 2
        + [pltpu.SemaphoreType.DMA((3,))] * 2
        + [pltpu.SemaphoreType.DMA] * 2
        + [pltpu.SemaphoreType.DMA((3,))] * 2
        + [pltpu.SemaphoreType.DMA((chunks,))] * 8
    )
    return pl.pallas_call(
        move_kernel,
        in_specs=[pl.BlockSpec(memory_space=pltpu.SMEM)]
        + [anywhere] * 3
        + [pl.BlockSpec(memory_space=pltpu.VMEM)],
        out_specs=anywhere,
        out_shape=jax.ShapeDtypeStruct((rows, columns), kind),
        scratch_shapes=[pltpu.VMEM((chunks, PLANES, PLANE_DEVICES, ROWS, LANES), kind)]
        + [pltpu.VMEM((BLOCK, columns // 2), kind)] * 3
        + [pltpu.VMEM((BLOCK, columns), kind)] * 4
        + [pltpu.VMEM((BLOCK, columns // 2), kind)]
        + [pltpu.VMEM((HEADS // 2, BLOCK, 2 * BLOCK), kind)]
        + [pltpu.VMEM((chunks, PLANES, ROWS, columns), kind)]
        + [pltpu.VMEM((tiles, ROWS, LANES), kind)] * 4
        + [
            pltpu.VMEM((chunks, PLANES, PLANE_DEVICES, ROWS, LANES), kind),
            pltpu.VMEM((2 * HEADS, 2 * BLOCK), jnp.float32),
            pltpu.VMEM((2 * HEADS, HALF, BLOCK + HALF), jnp.float32),
        ]
        + semaphores,
        cost_estimate=pl.CostEstimate(
            flops=0, transcendentals=0, bytes_accessed=1024 * 1024 * 1024
        ),
        compiler_params=pltpu.CompilerParams(
            collective_id=0, has_side_effects=True, vmem_limit_bytes=60 * 1024 * 1024
        ),
        name="move_tiles",
    )(table, queries, keys, values, own_rows)


PARTS = 4
PIECE = BLOCK // PARTS
HELD = 48
ROOM = ((13, 10), (14, 11))
HOPS = (2, 1, -1, -2)


def room_starts(room):
    far, near = room
    return (0, far, far + near, far + 2 * near)


def room_size(room):
    return 2 * sum(room)


def route_kernel(row_ref, column_ref, send_ref, relay_ref, final_ref, over_ref):
    count = row_ref.shape[1]
    i_row = lax.broadcasted_iota(jnp.int32, (1, count), 1)
    i_column = lax.broadcasted_iota(jnp.int32, (count, 1), 0)

    def both(f, *pairs):
        return tuple(f(*(pair[s] for pair in pairs)) for s in range(2))

    def rank(key):
        same = key[1] == key[0]
        in_row = jnp.sum(jnp.where(same & (i_column < i_row), 1.0, 0.0), axis=0, keepdims=True)
        in_column = jnp.sum(jnp.where(same & (i_row < i_column), 1.0, 0.0), axis=1, keepdims=True)
        return in_row.astype(jnp.int32), in_column.astype(jnp.int32)

    block = (row_ref[...], column_ref[...])
    seq = both(lambda m: m // 12, block)
    rest = both(lambda m, s: m - 12 * s, block, seq)
    source = both(lambda s, r: (s // 8) * 2 + jnp.where(r >= 6, 1, 0), seq, rest)
    local = both(
        lambda s, r: (s - 8 * (s // 8)) * 6 + jnp.where(r >= 6, r - 6, r), seq, rest
    )
    target = both(lambda i: i // HELD, (i_row, i_column))
    ahead = both(lambda a, b: jnp.where(b >= a, b - a, b - a + PLANES), source, target)
    turn = both(lambda r: r - 2 * (r // 2), rank(both(lambda a, b: a * 8 + b, source, target)))
    sign = both(
        lambda k, t: jnp.where(k < 4, 1, jnp.where((k == 4) & (t == 0), 1, -1)), ahead, turn
    )
    distance = both(lambda k: jnp.where(k <= 4, k, PLANES - k), ahead)
    first = both(
        lambda d, t: jnp.where(
            d == 0,
            0,
            jnp.where(d == 1, t, jnp.where(d == 2, 2 * t, jnp.where(d == 3, 1 + t, 2))),
        ),
        distance,
        turn,
    )
    second = both(lambda d, o: d - o, distance, first)
    relay = both(
        lambda z, s, o: jnp.bitwise_and(z + s * o + PLANES, PLANES - 1), source, sign, first
    )

    def slots(plane, hop, room):
        way = both(lambda s, h: jnp.where(h == 0, 0, s * h), sign, hop)
        order = rank(both(lambda p, w: p * 8 + w + 2, plane, way))
        at = room_starts(room)
        slot = both(
            lambda w, r: r
            + jnp.where(w == 2, at[0], jnp.where(w == 1, at[1], jnp.where(w == -1, at[2], at[3]))),
            way,
            order,
        )
        limit = jnp.where(hop[0] == 2, room[0], room[1])
        over = jnp.where((way[0] != 0) & (order[0] >= limit), 1.0, 0.0)
        return slot, jnp.sum(over, axis=1, keepdims=True)

    slot_one, over_one = slots(source, first, ROOM[0])
    slot_two, over_two = slots(relay, second, ROOM[1])
    at_relay = both(lambda o, l, s: jnp.where(o == 0, l, HELD + s), first, local, slot_one)

    def fill(out_ref, plane, hop, slot, room, value):
        size = room_size(room)
        place = lax.broadcasted_iota(jnp.int32, (1, PLANES * size), 1)
        code = jnp.where(hop[1] == 0, -1, plane[1] * size + slot[1])
        chosen = jnp.where(code == place, value[1].astype(jnp.float32), 0.0)
        out_ref[...] = jnp.sum(chosen, axis=0, keepdims=True).astype(jnp.int32)

    fill(send_ref, source, first, slot_one, ROOM[0], local)
    fill(relay_ref, relay, second, slot_two, ROOM[1], at_relay)
    final_ref[...] = jnp.where(
        second[0] == 0, at_relay[0], HELD + room_size(ROOM[0]) + slot_two[0]
    )
    over_ref[...] = (over_one + over_two).astype(jnp.int32)


def plan_routes(partner):
    order = partner.reshape(4, 8, 2, 6).transpose(0, 2, 1, 3).reshape(-1)
    full = pl.BlockSpec(memory_space=pltpu.VMEM)
    shapes = [(1, PLANES * room_size(room)) for room in ROOM] + [(1, order.shape[0]), (1, 1)]
    return pl.pallas_call(
        route_kernel,
        in_specs=[full] * 2,
        out_specs=[full] * 4,
        out_shape=[jax.ShapeDtypeStruct(shape, jnp.int32) for shape in shapes],
        name="plan_routes",
    )(order.reshape(1, -1), order.reshape(-1, 1))


def short_kernel(
    send_ref, relay_ref, final_ref, q_ref, k_ref, v_ref, row_ref, out_ref, *scratch
):
    chunks = 2 * PARTS
    held, near_in, far_in = (scratch[i * chunks : (i + 1) * chunks] for i in range(3))
    (
        staged_one,
        staged_two,
        staged_out,
        far_ref,
        weights_f,
        weights_b,
        all_q,
        full_k,
        full_v,
        mid_k,
        mid_v,
        all_out,
        rows,
        row_send,
        row_recv,
        load_sem,
        out_sem,
        half_send,
        half_recv,
        p0_send,
        p0b_send,
        p0_recv,
        z1_send,
        z1_recv,
        z2_send,
        z2_recv,
        out_send,
        out_recv,
    ) = scratch[3 * chunks :]
    seq = lax.axis_index("seq")
    head = lax.axis_index("head")
    plane = 2 * (seq // 8) + head // 4
    spot = lax.rem(seq, 8) * 4 + lax.rem(head, 4)
    odd = lax.rem(head, 2)
    pair = spot + 1 - 2 * odd

    def above(hop):
        return lax.rem(plane + hop + PLANES, PLANES)

    barrier = pltpu.get_barrier_semaphore()
    for hop in HOPS:
        pl.semaphore_signal(
            barrier, inc=1, device_id=place_of(above(hop), spot), device_id_type=MESH
        )

    def greet(step, carry):
        pl.semaphore_signal(
            barrier,
            inc=1,
            device_id=place_of(plane, lax.rem(spot + step, PLANE_DEVICES)),
            device_id_type=MESH,
        )
        return carry

    lax.fori_loop(1, PLANE_DEVICES, greet, 0)
    pl.semaphore_wait(barrier, len(HOPS) + PLANE_DEVICES - 1)

    def finish(ref, sem):
        pltpu.make_async_copy(ref, ref, sem).wait()

    def plane_stage(source, target, send, recv):
        def body(step, carry):
            other = lax.rem(spot + step, PLANE_DEVICES)
            pltpu.make_async_remote_copy(
                src_ref=source(other),
                dst_ref=target,
                send_sem=send,
                recv_sem=recv,
                device_id=place_of(plane, other),
                device_id_type=MESH,
            ).start()
            return carry

        lax.fori_loop(1, PLANE_DEVICES, body, 0)
        pltpu.make_async_copy(source(spot), target, recv).start()

    def first_block(place):
        return (place // 4) * 6 + (lax.rem(place, 4) // 2) * 3

    full_rows = pl.ds(pl.multiple_of(odd * HALF, HALF), BLOCK)
    half_rows = pl.ds(pl.multiple_of(2 * HALF * (1 - odd), HALF), HALF)

    def spread(chunk):
        kind, part = divmod(chunk, PARTS)
        ref = (k_ref, v_ref)[kind]

        def piece(start):
            lines = pl.ds(pl.multiple_of(start, PIECE), PIECE)
            return lambda other: ref.at[
                lines, pl.ds(pl.multiple_of(other * LANES, LANES), LANES)
            ]

        plane_stage(
            piece(odd * HALF + PIECE * part),
            held[chunk].at[first_block(spot) + 2 * odd],
            p0_send.at[chunk],
            p0_recv.at[chunk],
        )

        @pl.when(odd == part // 2)
        def _():
            plane_stage(
                piece(2 * HALF * (1 - odd) + PIECE * (part % 2)),
                held[chunk].at[first_block(spot) + 1],
                p0b_send.at[chunk],
                p0_recv.at[chunk],
            )

    def z_stage(staged, landed, room, send, recv):
        for start, size, hop in zip(room_starts(room), (*room, *room[::-1]), HOPS):
            pltpu.make_async_remote_copy(
                src_ref=staged.at[pl.ds(start, size)],
                dst_ref=landed.at[pl.ds(start, size)],
                send_sem=send,
                recv_sem=recv,
                device_id=place_of(above(hop), spot),
                device_id_type=MESH,
            ).start()

    size_one, size_two = (room_size(room) for room in ROOM)

    def leg_one(chunk):
        finish(held[chunk], p0_recv.at[chunk])
        slot = chunk % 2
        if chunk >= 2:
            finish(staged_one.at[slot], z1_send.at[chunk - 2])

        def body(i, carry):
            for j in range(2):
                where = 2 * i + j
                staged_one[slot, where] = held[chunk][send_ref[0, plane * size_one + where]]
            return carry

        lax.fori_loop(0, size_one // 2, body, 0)
        z_stage(staged_one.at[slot], near_in[chunk], ROOM[0], z1_send.at[chunk], z1_recv.at[chunk])

    def held_or_near(chunk, index):
        kept = held[chunk][jnp.minimum(index, HELD - 1)]
        came = near_in[chunk][jnp.clip(index - HELD, 0, size_one - 1)]
        return jnp.where(index < HELD, kept, came)

    def leg_two(chunk):
        finish(near_in[chunk], z1_recv.at[chunk])
        slot = chunk % 2
        if chunk >= 2:
            finish(staged_two.at[slot], z2_send.at[chunk - 2])

        def body(i, carry):
            for j in range(2):
                where = 2 * i + j
                index = relay_ref[0, plane * size_two + where]
                staged_two[slot, where] = held_or_near(chunk, index)
            return carry

        lax.fori_loop(0, size_two // 2, body, 0)
        z_stage(staged_two.at[slot], far_in[chunk], ROOM[1], z2_send.at[chunk], z2_recv.at[chunk])

    def arrived(chunk, count=PLANE_DEVICES):
        kind, part = divmod(chunk, PARTS)
        return far_ref.at[kind, pl.ds(0, count), :, pl.ds(part * PIECE, PIECE)]

    done = set()

    def finish_far(chunk):
        if chunk not in done:
            done.add(chunk)
            finish(arrived(chunk), out_recv.at[chunk])

    def deliver(chunk):
        finish(far_in[chunk], z2_recv.at[chunk])
        slot = chunk % 2
        if chunk >= 2:
            finish(arrived(chunk - 2, PLANE_DEVICES - 1), out_send.at[chunk - 2])
            finish_far(chunk - 2)
        border = HELD + size_one

        def body(i, carry):
            for j in range(2):
                where = 2 * i + j
                index = final_ref[0, plane * HELD + where]
                last = far_in[chunk][jnp.clip(index - border, 0, size_two - 1)]
                staged_out[slot, where] = jnp.where(
                    index < border, held_or_near(chunk, index), last
                )
            return carry

        lax.fori_loop(0, HELD // 2, body, 0)
        kind, part = divmod(chunk, PARTS)
        plane_stage(
            lambda other: staged_out.at[slot, pl.ds(first_block(other) + lax.rem(other, 2), 2)],
            far_ref.at[kind, spot, :, pl.ds(part * PIECE, PIECE)],
            out_send.at[chunk],
            out_recv.at[chunk],
        )

    lower = lax.rem(plane, 2)
    set_rows = 4 * ROW_SET
    near_rows = rows.at[pl.ds(pl.multiple_of(lower * set_rows, ROW_SET), set_rows)]
    far_rows = rows.at[pl.ds(pl.multiple_of((1 - lower) * set_rows, ROW_SET), set_rows)]
    own_rows = rows.at[pl.ds(pl.multiple_of(head * ROW_SET, ROW_SET), ROW_SET)]

    def show_rows():
        for step in range(1, 4):
            other = spot - lax.rem(spot, 4) + lax.rem(spot + step, 4)
            pltpu.make_async_remote_copy(
                src_ref=row_ref,
                dst_ref=own_rows,
                send_sem=row_send.at[0],
                recv_sem=row_recv.at[0],
                device_id=place_of(plane, other),
                device_id_type=MESH,
            ).start()
        pltpu.make_async_copy(row_ref, own_rows, row_recv.at[0]).start()

    def share_rows():
        finish(near_rows, row_recv.at[0])
        pltpu.make_async_remote_copy(
            src_ref=near_rows,
            dst_ref=near_rows,
            send_sem=row_send.at[1],
            recv_sem=row_recv.at[1],
            device_id=place_of(plane + 1 - 2 * lower, spot),
            device_id_type=MESH,
        ).start()

    loads = [
        pltpu.make_async_copy(source, target, load_sem.at[i])
        for i, (source, target) in enumerate(
            ((q_ref, all_q), (k_ref.at[full_rows, :], full_k), (v_ref.at[full_rows, :], full_v))
        )
    ]

    def swap_halves():
        for i, (source, target) in enumerate(((k_ref, mid_k), (v_ref, mid_v))):
            place = target.at[pl.ds(pl.multiple_of(odd * HALF, HALF), HALF), :]
            pltpu.make_async_remote_copy(
                src_ref=source.at[half_rows, :],
                dst_ref=place,
                send_sem=half_send.at[i],
                recv_sem=half_recv.at[i],
                device_id=place_of(plane, pair),
                device_id_type=MESH,
            ).start()
            pltpu.make_async_copy(source.at[half_rows, :], place, half_recv.at[i]).start()

    scale = math.log2(math.e) / math.sqrt(LANES)
    contract = (((1,), (1,)), ((), ()))
    ones = jnp.ones((BLOCK, LANES), jnp.bfloat16)

    def weigh(query, near_keys, far_keys, near_bias, far_bias):
        near = lax.dot_general(query, near_keys, contract, preferred_element_type=jnp.float32)
        far = lax.dot_general(query, far_keys, contract, preferred_element_type=jnp.float32)
        near = near * scale + near_bias
        far = far * scale + far_bias
        highest = jnp.max(jnp.maximum(near, far), axis=1, keepdims=True)
        return tuple(jnp.exp2(part - highest).astype(jnp.bfloat16) for part in (near, far))

    def skew(line):
        return pltpu.roll(
            jnp.broadcast_to(line, (HALF, 2 * BLOCK)),
            2 * BLOCK - HALF + 1,
            1,
            stride=1,
            stride_axis=0,
        )

    def weigh_heads(first, last):
        def body(i, carry):
            lines = rows[pl.ds(pl.multiple_of(i * ROW_SET, ROW_SET), ROW_SET), :]
            for g in range(GROUP):
                one = i * GROUP + g
                columns = pl.ds(pl.multiple_of(one * LANES, LANES), LANES)
                skews = [skew(lines[2 * g + side : 2 * g + side + 1]) for side in range(2)]
                upper = [turned[:, HALF : HALF + BLOCK] for turned in skews]
                under = [turned[:, :BLOCK] for turned in skews]
                near_keys = full_k[:, columns]
                far_keys = far_ref[0, one, odd]
                for half in range(2):
                    lines_here = pl.ds(pl.multiple_of((odd + half) * HALF, HALF), HALF)
                    near, far = weigh(
                        all_q[lines_here, columns], near_keys, far_keys, *(upper, under)[half]
                    )
                    part = slice(half * HALF, (half + 1) * HALF)
                    weights_f[one, part, :BLOCK] = near
                    weights_f[one, part, BLOCK:] = far
                mixed = [jnp.where(odd == 1, u, o) for u, o in zip(under, upper)]
                near, far = weigh(
                    all_q[half_rows, columns], mid_k[:, columns], far_ref[0, one, 1 - odd], *mixed
                )
                weights_b[one, :, :BLOCK] = near
                weights_b[one, :, BLOCK:] = far
            return carry

        lax.fori_loop(first // GROUP, last // GROUP, body, 0)

    def blend(weights, near_values, far_values):
        summed = jnp.dot(
            weights[:, :BLOCK],
            jnp.concatenate([near_values, ones], axis=1),
            preferred_element_type=jnp.float32,
        ) + jnp.dot(
            weights[:, BLOCK:],
            jnp.concatenate([far_values, ones], axis=1),
            preferred_element_type=jnp.float32,
        )
        return (summed[:, :LANES] / summed[:, LANES:]).astype(jnp.bfloat16)

    def blend_heads(first, last):
        def body(i, carry):
            for g in range(GROUP):
                one = i * GROUP + g
                columns = pl.ds(pl.multiple_of(one * LANES, LANES), LANES)
                all_out[full_rows, columns] = blend(
                    weights_f[one], full_v[:, columns], far_ref[1, one, odd]
                )
                all_out[half_rows, columns] = blend(
                    weights_b[one], mid_v[:, columns], far_ref[1, one, 1 - odd]
                )
            return carry

        lax.fori_loop(first // GROUP, last // GROUP, body, 0)

    spread(0)
    spread(1)
    show_rows()
    for load in loads:
        load.start()
    for step in range(chunks + 2):
        if step < chunks:
            leg_one(step)
            if step + 2 < chunks:
                spread(step + 2)
        if step == 1:
            share_rows()
            swap_halves()
        if 1 <= step <= chunks:
            leg_two(step - 1)
        if step >= 2:
            deliver(step - 2)
        turn = step - chunks + 2
        if turn == 0:
            for chunk in range(PARTS):
                finish_far(chunk)
            finish(mid_k, half_recv.at[0])
            finish(mid_v, half_recv.at[1])
            finish(far_rows, row_recv.at[1])
            for load in loads:
                load.wait()
        if turn >= 0:
            weigh_heads(turn * HEADS // 4, (turn + 1) * HEADS // 4)
    finish_far(chunks - 2)
    finish_far(chunks - 1)
    stores = []
    for side in range(2):
        blend_heads(side * HEADS // 2, (side + 1) * HEADS // 2)
        columns = pl.ds(side * HEADS // 2 * LANES, HEADS // 2 * LANES)
        store = pltpu.make_async_copy(
            all_out.at[:, columns], out_ref.at[:, columns], out_sem.at[side]
        )
        store.start()
        stores.append(store)
    for chunk in range(chunks):
        finish(arrived(chunk, PLANE_DEVICES - 1).at[:, 0], p0_send.at[chunk])

        @pl.when(odd == chunk % PARTS // 2)
        def _():
            finish(arrived(chunk, PLANE_DEVICES - 1).at[:, 0], p0b_send.at[chunk])

    for chunk in range(chunks - 2, chunks):
        finish(staged_one.at[chunk % 2], z1_send.at[chunk])
        finish(staged_two.at[chunk % 2], z2_send.at[chunk])
        finish(arrived(chunk, PLANE_DEVICES - 1), out_send.at[chunk])
    for i, target in enumerate((mid_k, mid_v)):
        finish(target.at[pl.ds(0, HALF), :], half_send.at[i])
    finish(rows.at[pl.ds(0, 3 * ROW_SET)], row_send.at[0])
    finish(near_rows, row_send.at[1])
    for store in stores:
        store.wait()


def short_move(routes, queries, keys, values, own_rows):
    lines, columns = keys.shape
    kind = keys.dtype
    chunks = 2 * PARTS
    sizes = [room_size(room) for room in ROOM]
    anywhere = pl.BlockSpec(memory_space=pltpu.HBM)

    def vmem(*shape):
        return pltpu.VMEM(shape, kind)

    piece = (PIECE, LANES)
    scratch = []
    for count in (HELD, *sizes):
        scratch += [vmem(count, *piece)] * chunks
    scratch += [vmem(2, count, *piece) for count in (*sizes, HELD)]
    scratch += [
        vmem(2, HEADS, 2, BLOCK, LANES),
        vmem(HEADS, BLOCK, 2 * BLOCK),
        vmem(HEADS, HALF, 2 * BLOCK),
        vmem(lines, columns),
    ]
    scratch += [vmem(BLOCK, columns)] * 4 + [vmem(lines, columns)]
    scratch += [pltpu.VMEM((2 * HEADS, 2 * BLOCK), jnp.float32)]
    scratch += [pltpu.SemaphoreType.DMA((2,))] * 2
    scratch += [pltpu.SemaphoreType.DMA((3,))]
    scratch += [pltpu.SemaphoreType.DMA((2,))] * 3
    scratch += [pltpu.SemaphoreType.DMA((chunks,))] * 9
    return pl.pallas_call(
        short_kernel,
        in_specs=[pl.BlockSpec(memory_space=pltpu.SMEM)] * 3
        + [anywhere] * 3
        + [pl.BlockSpec(memory_space=pltpu.VMEM)],
        out_specs=anywhere,
        out_shape=jax.ShapeDtypeStruct((lines, columns), kind),
        scratch_shapes=scratch,
        compiler_params=pltpu.CompilerParams(
            collective_id=1, has_side_effects=True, vmem_limit_bytes=60 * 1024 * 1024
        ),
        name="short_move",
    )(*routes, queries, keys, values, own_rows)


def tile_table(partner):
    trio = partner // 3
    member = partner - 3 * trio
    entries = []
    for source, slot in (
        (jnp.where(member == 2, 1, 0), jnp.where(member == 1, 2, 0)),
        (jnp.where(member == 0, 0, 1), jnp.where(member == 1, 2, 1)),
    ):
        device = 2 * trio + source
        seq, head = device // 8, device % 8
        plane = (seq // 8) * 2 + head // 4
        spot = (seq % 8) * 4 + head % 4
        entries.append((slot * PLANE_DEVICES + spot) * PLANES + plane)
    return jnp.concatenate(entries)


def on_device(queries, key_states, value_states, partner, buckets, bias_table):
    one_hot = (
        buckets[..., None] == jnp.arange(bias_table.shape[0], dtype=jnp.int32)
    ).astype(jnp.float32)
    own_rows = jnp.einsum("skb,bh->hsk", one_hot, bias_table, precision=lax.Precision.HIGHEST)
    own_rows = jnp.pad(own_rows * math.log2(math.e), ((0, 0), (0, 0), (0, 1)))

    own_rows = own_rows.reshape(ROW_SET, 2 * BLOCK)
    *routes, over = plan_routes(partner)
    return lax.cond(
        over[0, 0] == 0,
        lambda: short_move(routes, queries, key_states, value_states, own_rows),
        lambda: move_tiles(
            tile_table(partner), queries, key_states, value_states, own_rows
        ),
    )


def solution(mesh):
    whole = P(("seq", "head"), None)
    return jax.shard_map(
        on_device,
        mesh=mesh,
        in_specs=(whole, whole, whole, P(), P(), P(None, "head")),
        out_specs=whole,
        check_vma=False,
    )
```

```python
import math

import jax
import jax.numpy as jnp
from jax import lax
from jax.experimental import pallas as pl
from jax.experimental.pallas import tpu as pltpu
from jax.sharding import PartitionSpec as P

BLOCK = 256
HALF = 128
HEADS = 32
LANES = 128
ROWS = 16
CHUNKS = 8
GROUP = 4


MESH = pl.DeviceIdType.MESH
PLANES = 8
PLANE_DEVICES = 32
SLOTS = 3
ROW_SET = 8
ORDER = (1, 0, 2)


def place_of(plane, spot):
    return ((plane // 2) * 8 + spot // 4, lax.rem(plane, 2) * 4 + lax.rem(spot, 4))


def move_kernel(
    table_ref,
    q_ref,
    k_ref,
    v_ref,
    row_ref,
    out_ref,
    far_ref,
    mid_q_ref,
    mid_k_ref,
    mid_v_ref,
    whole_q,
    whole_k,
    whole_v,
    whole_out,
    middle_out,
    weights,
    fanned,
    held_k,
    held_v,
    picked_k,
    picked_v,
    landed,
    rows,
    skewed,
    row_send,
    row_recv,
    whole_sem,
    out_sem,
    swap_send,
    swap_recv,
    half_send,
    half_recv,
    z1_send,
    z1_recv,
    p1_send,
    p1_recv,
    z2_send,
    z2_recv,
    p2_send,
    p2_recv,
):
    seq = lax.axis_index("seq")
    head = lax.axis_index("head")
    plane = 2 * (seq // 8) + head // 4
    spot = lax.rem(seq, 8) * 4 + lax.rem(head, 4)
    odd = lax.rem(head, 2)
    pair = spot + 1 - 2 * odd

    barrier = pltpu.get_barrier_semaphore()
    for step in range(1, PLANES):
        pl.semaphore_signal(
            barrier,
            inc=1,
            device_id=place_of(lax.rem(plane + step, PLANES), spot),
            device_id_type=MESH,
        )

    def greet(step, carry):
        pl.semaphore_signal(
            barrier,
            inc=1,
            device_id=place_of(plane, lax.rem(spot + step, PLANE_DEVICES)),
            device_id_type=MESH,
        )
        return carry

    lax.fori_loop(1, PLANE_DEVICES, greet, 0)
    pl.semaphore_wait(barrier, PLANES - 1 + PLANE_DEVICES - 1)

    def finish(ref, sem):
        pltpu.make_async_copy(ref, ref, sem).wait()

    def z_stage(source, target, send, recv):
        for step in (4, 3, 5, 2, 6, 1, 7):
            other = lax.rem(plane + step, PLANES)
            pltpu.make_async_remote_copy(
                src_ref=source(other),
                dst_ref=target,
                send_sem=send,
                recv_sem=recv,
                device_id=place_of(other, spot),
                device_id_type=MESH,
            ).start()
        pltpu.make_async_copy(source(plane), target, recv).start()

    def plane_stage(source, target, send, recv):
        def body(step, carry):
            other = lax.rem(spot + step, PLANE_DEVICES)
            pltpu.make_async_remote_copy(
                src_ref=source(other),
                dst_ref=target,
                send_sem=send,
                recv_sem=recv,
                device_id=place_of(plane, other),
                device_id_type=MESH,
            ).start()
            return carry

        lax.fori_loop(1, PLANE_DEVICES, body, 0)
        pltpu.make_async_copy(source(spot), target, recv).start()

    def fan_out(chunk):
        kind, slot = divmod(chunk, SLOTS)
        ref = (k_ref, v_ref)[kind]
        first = (odd * HALF, odd * HALF + HALF, 2 * HALF * (1 - odd))[slot]
        z_stage(
            lambda other: ref.at[pl.ds(pl.multiple_of(first + ROWS * other, ROWS), ROWS), :],
            fanned.at[chunk, plane],
            z1_send.at[chunk],
            z1_recv.at[chunk],
        )

    def by_head(chunk):
        kind, slot = divmod(chunk, SLOTS)
        held = (held_k, held_v)[kind]
        shift = (0, HEADS // 2, odd * (HEADS // 2))[slot]

        def source(other):
            start = pl.multiple_of(lax.rem(other + shift, HEADS) * LANES, LANES)
            return fanned.at[chunk, :, :, pl.ds(start, LANES)]

        plane_stage(
            source,
            held.at[pl.ds((slot * PLANE_DEVICES + spot) * PLANES, PLANES)],
            p1_send.at[chunk],
            p1_recv.at[chunk],
        )

    side = spot // (HEADS // 2)
    blocks = table_ref.shape[0] // 2

    def pick(kind, slot):
        held = (held_k, held_v)[kind]
        picked = (picked_k, picked_v)[kind]

        def body(z, carry):
            first = (z // 2) * 96 + lax.rem(z, 2) * 6
            base = slot * PLANES * PLANE_DEVICES + z
            for p in range(PLANE_DEVICES):
                e = p % 2
                low = (True, e == 0, False)[slot]
                member = 1 if slot == 1 else 2 * e
                block = first + (p // 4) * 12 + (p % 4 // 2) * 3 + member
                chosen = side if low else 1 - side
                picked[base + p * PLANES] = held[table_ref[chosen * blocks + block]]
            return carry

        lax.fori_loop(0, PLANES, body, 0)

    def share_picked(chunk):
        kind, slot = divmod(chunk, SLOTS)
        picked = (picked_k, picked_v)[kind]
        plane_stage(
            lambda other: picked.at[pl.ds((slot * PLANE_DEVICES + other) * PLANES, PLANES)],
            landed.at[chunk, :, spot],
            p2_send.at[chunk],
            p2_recv.at[chunk],
        )

    def deliver(chunk):
        finish(landed.at[chunk], p2_recv.at[chunk])
        z_stage(
            lambda other: landed.at[chunk, other],
            far_ref.at[chunk, plane],
            z2_send.at[chunk],
            z2_recv.at[chunk],
        )

    lower = lax.rem(plane, 2)
    set_rows = 4 * ROW_SET
    near_rows = rows.at[pl.ds(pl.multiple_of(lower * set_rows, ROW_SET), set_rows)]
    far_rows = rows.at[pl.ds(pl.multiple_of((1 - lower) * set_rows, ROW_SET), set_rows)]
    own_rows = rows.at[pl.ds(pl.multiple_of(head * ROW_SET, ROW_SET), ROW_SET)]

    for step in range(1, 4):
        other = spot - lax.rem(spot, 4) + lax.rem(spot + step, 4)
        pltpu.make_async_remote_copy(
            src_ref=row_ref,
            dst_ref=own_rows,
            send_sem=row_send.at[0],
            recv_sem=row_recv.at[0],
            device_id=place_of(plane, other),
            device_id_type=MESH,
        ).start()
    pltpu.make_async_copy(row_ref, own_rows, row_recv.at[0]).start()

    def share_rows():
        finish(near_rows, row_recv.at[0])
        pltpu.make_async_remote_copy(
            src_ref=near_rows,
            dst_ref=near_rows,
            send_sem=row_send.at[1],
            recv_sem=row_recv.at[1],
            device_id=place_of(plane + 1 - 2 * lower, spot),
            device_id_type=MESH,
        ).start()

    def skew_rows():
        finish(far_rows, row_recv.at[1])

        def body(i, carry):
            start = pl.multiple_of(i * ROW_SET, ROW_SET)
            some = rows[pl.ds(start, ROW_SET), :]
            for j in range(ROW_SET):
                turned = pltpu.roll(
                    jnp.broadcast_to(some[j : j + 1], (HALF, 2 * BLOCK)),
                    2 * BLOCK - HALF + 1,
                    1,
                    stride=1,
                    stride_axis=0,
                )
                skewed[start + j] = turned[:, : BLOCK + HALF]
            return carry

        lax.fori_loop(0, 2 * HEADS // ROW_SET, body, 0)

    scale = math.log2(math.e) / math.sqrt(LANES)
    contract = (((1,), (1,)), ((), ()))
    half_heads = HEADS // 2

    ones = jnp.ones((BLOCK, LANES), jnp.bfloat16)

    def far_block(chunk, head):
        other = lax.rem(head + half_heads, HEADS)
        return jnp.concatenate(
            [far_ref[chunk, :, one].reshape(HALF, LANES) for one in (head, other)], axis=0
        )

    def weigh(query, near_keys, far_keys, head, half):
        shift = HALF * (1 - half)
        near = lax.dot_general(query, near_keys, contract, preferred_element_type=jnp.float32)
        far = lax.dot_general(query, far_keys, contract, preferred_element_type=jnp.float32)
        near = near * scale + skewed[2 * head, :, shift : shift + BLOCK]
        far = far * scale + skewed[2 * head + 1, :, shift : shift + BLOCK]
        highest = jnp.max(jnp.maximum(near, far), axis=1, keepdims=True)
        return tuple(jnp.exp2(part - highest).astype(jnp.bfloat16) for part in (near, far))

    def blend(near, far, near_values, far_values):
        summed = jnp.dot(near, near_values, preferred_element_type=jnp.float32) + jnp.dot(
            far, far_values, preferred_element_type=jnp.float32
        )
        return (summed[:, :LANES] / summed[:, LANES:]).astype(jnp.bfloat16)

    def over_heads(slot, visit):
        middle = slot == 1
        first = (0, half_heads * odd, half_heads)[slot]

        def body(i, carry):
            for g in range(GROUP):
                place = i * GROUP + g
                start = (place if middle else first + place) * LANES
                visit(place, first + place, pl.ds(pl.multiple_of(start, LANES), LANES))
            return carry

        lax.fori_loop(0, half_heads // GROUP, body, 0)

    def attend(slot):
        middle = slot == 1
        q, k, v = (mid_q_ref, mid_k_ref, mid_v_ref) if middle else (whole_q, whole_k, whole_v)
        target = middle_out if middle else whole_out

        def visit(place, head, columns):
            near_keys = k[:, columns]
            far_keys = far_block(slot, head)
            near_values = jnp.concatenate([v[:, columns], ones], axis=1)
            far_values = jnp.concatenate([far_block(SLOTS + slot, head), ones], axis=1)
            for half in range(2):
                part = slice(half * HALF, (half + 1) * HALF)
                near, far = weigh(q[part, columns], near_keys, far_keys, head, half)
                target[part, columns] = blend(near, far, near_values, far_values)

        over_heads(slot, visit)

    def weigh_last():
        def visit(place, head, columns):
            near_keys = whole_k[:, columns]
            far_keys = far_block(2, head)
            for half in range(2):
                part = slice(half * HALF, (half + 1) * HALF)
                near, far = weigh(whole_q[part, columns], near_keys, far_keys, head, half)
                weights[place, part, :BLOCK] = near
                weights[place, part, BLOCK:] = far

        over_heads(2, visit)

    def blend_last():
        def visit(place, head, columns):
            near_values = jnp.concatenate([whole_v[:, columns], ones], axis=1)
            far_values = jnp.concatenate([far_block(SLOTS + 2, head), ones], axis=1)
            whole_out[:, columns] = blend(
                weights[place, :, :BLOCK], weights[place, :, BLOCK:], near_values, far_values
            )

        over_heads(2, visit)

    whole_rows = pl.ds(pl.multiple_of(odd * HALF, HALF), BLOCK)
    side_width = half_heads * LANES

    def store_whole(side):
        columns = pl.ds(side * side_width, side_width)
        return pltpu.make_async_copy(
            whole_out.at[:, columns], out_ref.at[whole_rows, columns], out_sem.at[side]
        )

    own_columns = pl.ds(pl.multiple_of(odd * side_width, LANES), side_width)
    own_place = out_ref.at[pl.ds(pl.multiple_of(2 * HALF * (1 - odd), HALF), HALF), own_columns]
    store_middle = pltpu.make_async_copy(
        middle_out.at[pl.ds(pl.multiple_of(odd * HALF, HALF), HALF), :], own_place, out_sem.at[2]
    )
    swap_middle = pltpu.make_async_remote_copy(
        src_ref=middle_out.at[pl.ds(pl.multiple_of((1 - odd) * HALF, HALF), HALF), :],
        dst_ref=out_ref.at[pl.ds(pl.multiple_of(2 * HALF * odd, HALF), HALF), own_columns],
        send_sem=swap_send,
        recv_sem=swap_recv,
        device_id=place_of(plane, pair),
        device_id_type=MESH,
    )
    loads = [
        pltpu.make_async_copy(source.at[whole_rows, :], target, whole_sem.at[i])
        for i, (source, target) in enumerate(((q_ref, whole_q), (k_ref, whole_k), (v_ref, whole_v)))
    ]

    for chunk in range(SLOTS):
        fan_out(chunk)
    for i, (source, target) in enumerate(((q_ref, mid_q_ref), (k_ref, mid_k_ref), (v_ref, mid_v_ref))):
        half_rows = pl.ds(pl.multiple_of(2 * HALF * (1 - odd), HALF), HALF)
        width = target.shape[1]
        own = pl.ds(pl.multiple_of(odd * width, LANES), width)
        given = pl.ds(pl.multiple_of((1 - odd) * width, LANES), width)
        place = target.at[pl.ds(pl.multiple_of(odd * HALF, HALF), HALF), :]
        pltpu.make_async_remote_copy(
            src_ref=source.at[half_rows, given],
            dst_ref=place,
            send_sem=half_send.at[i],
            recv_sem=half_recv.at[i],
            device_id=place_of(plane, pair),
            device_id_type=MESH,
        ).start()
        pltpu.make_async_copy(source.at[half_rows, own], place, half_recv.at[i]).start()
    for load in loads:
        load.start()
    def choose(kind):
        held = (held_k, held_v)[kind]
        for slot in range(SLOTS):
            part = held.at[pl.ds(slot * PLANE_DEVICES * PLANES, PLANE_DEVICES * PLANES)]
            finish(part, p1_recv.at[kind * SLOTS + slot])
        for slot in ORDER:
            pick(kind, slot)
            share_picked(kind * SLOTS + slot)

    for chunk in range(SLOTS):
        finish(fanned.at[chunk], z1_recv.at[chunk])
        by_head(chunk)
        fan_out(chunk + SLOTS)
    choose(0)
    share_rows()
    for i, slot in enumerate(ORDER):
        finish(fanned.at[SLOTS + i], z1_recv.at[SLOTS + i])
        by_head(SLOTS + i)
        deliver(slot)
    skew_rows()
    choose(1)
    for slot in ORDER:
        deliver(SLOTS + slot)
    for slot in ORDER:
        finish(far_ref.at[slot], z2_recv.at[slot])
    for i, target in enumerate((mid_q_ref, mid_k_ref, mid_v_ref)):
        finish(target, half_recv.at[i])
    for load in loads:
        load.wait()
    weigh_last()
    for slot in ORDER:
        finish(far_ref.at[SLOTS + slot], z2_recv.at[SLOTS + slot])
        if slot == 2:
            blend_last()
        else:
            attend(slot)
        if slot == 1:
            store_middle.start()
            swap_middle.start()
        else:
            store_whole(slot // 2).start()
    for i, target in enumerate((mid_q_ref, mid_k_ref, mid_v_ref)):
        finish(target.at[pl.ds(0, HALF), :], half_send.at[i])
    for chunk in range(2 * SLOTS):
        finish(fanned.at[chunk, pl.ds(0, PLANES - 1)], z1_send.at[chunk])
        finish(landed.at[chunk, :, pl.ds(0, PLANE_DEVICES - 1)], p1_send.at[chunk])
        finish(landed.at[chunk, :, pl.ds(0, PLANE_DEVICES - 1)], p2_send.at[chunk])
        finish(landed.at[chunk, pl.ds(0, PLANES - 1)], z2_send.at[chunk])
    finish(rows.at[pl.ds(0, 3 * ROW_SET)], row_send.at[0])
    finish(near_rows, row_send.at[1])
    store_middle.wait()
    swap_middle.wait()
    store_whole(0).wait()
    store_whole(1).wait()


def move_tiles(table, queries, keys, values, own_rows):
    rows, columns = keys.shape
    kind = keys.dtype
    chunks = 2 * SLOTS
    tiles = SLOTS * PLANES * PLANE_DEVICES
    anywhere = pl.BlockSpec(memory_space=pltpu.HBM)
    semaphores = (
        [pltpu.SemaphoreType.DMA((2,))] * 2
        + [pltpu.SemaphoreType.DMA((3,))] * 2
        + [pltpu.SemaphoreType.DMA] * 2
        + [pltpu.SemaphoreType.DMA((3,))] * 2
        + [pltpu.SemaphoreType.DMA((chunks,))] * 8
    )
    return pl.pallas_call(
        move_kernel,
        in_specs=[pl.BlockSpec(memory_space=pltpu.SMEM)]
        + [anywhere] * 3
        + [pl.BlockSpec(memory_space=pltpu.VMEM)],
        out_specs=anywhere,
        out_shape=jax.ShapeDtypeStruct((rows, columns), kind),
        scratch_shapes=[pltpu.VMEM((chunks, PLANES, PLANE_DEVICES, ROWS, LANES), kind)]
        + [pltpu.VMEM((BLOCK, columns // 2), kind)] * 3
        + [pltpu.VMEM((BLOCK, columns), kind)] * 4
        + [pltpu.VMEM((BLOCK, columns // 2), kind)]
        + [pltpu.VMEM((HEADS // 2, BLOCK, 2 * BLOCK), kind)]
        + [pltpu.VMEM((chunks, PLANES, ROWS, columns), kind)]
        + [pltpu.VMEM((tiles, ROWS, LANES), kind)] * 4
        + [
            pltpu.VMEM((chunks, PLANES, PLANE_DEVICES, ROWS, LANES), kind),
            pltpu.VMEM((2 * HEADS, 2 * BLOCK), jnp.float32),
            pltpu.VMEM((2 * HEADS, HALF, BLOCK + HALF), jnp.float32),
        ]
        + semaphores,
        cost_estimate=pl.CostEstimate(
            flops=0, transcendentals=0, bytes_accessed=1024 * 1024 * 1024
        ),
        compiler_params=pltpu.CompilerParams(
            collective_id=0, has_side_effects=True, vmem_limit_bytes=60 * 1024 * 1024
        ),
        name="move_tiles",
    )(table, queries, keys, values, own_rows)


PARTS = 4
SPANS = (((0, 32), (32, 96), (128, 64), (192, 64)), ((0, 64), (64, 64), (128, 96), (224, 32)))
HELD = 48
ROOM = ((13, 10), (12, 11))
FLIP = (11, 12)
HOPS = (2, 1, -1, -2)


def span_of(chunk):
    kind, part = divmod(chunk, PARTS)
    return kind, *SPANS[kind][part]


def room_starts(room):
    far, near = room
    return (0, far, far + near, far + 2 * near)


def room_size(room):
    return 2 * sum(room)


def route_kernel(partner_ref, send_ref, relay_ref, final_ref, over_ref):
    count = partner_ref.shape[1]
    i_row = lax.broadcasted_iota(jnp.int32, (1, count), 1)
    i_column = lax.broadcasted_iota(jnp.int32, (count, 1), 0)

    def both(f, *pairs):
        return tuple(f(*(pair[s] for pair in pairs)) for s in range(2))

    i = (i_row, i_column)

    def rank(key, order=i):
        same = key[1] == key[0]
        before = jnp.where(same & (order[1] < order[0]), 1.0, 0.0)
        after = jnp.where(same & (order[0] < order[1]), 1.0, 0.0)
        in_row = jnp.sum(before, axis=0, keepdims=True)
        in_column = jnp.sum(after, axis=1, keepdims=True)
        return in_row.astype(jnp.int32), in_column.astype(jnp.int32)

    asked = partner_ref[...].astype(jnp.float32)
    in_plane = i_column - HELD * (i_column // HELD)
    group = in_plane // 6
    wanted = ((i_column // 96) * 8 + group) * 12 + in_plane - 6 * group
    wanted = wanted + jnp.where(i_column - 96 * (i_column // 96) >= HELD, 6, 0)
    block_column = jnp.sum(jnp.where(wanted == i_row, asked, 0.0), axis=1, keepdims=True)
    block_row = jnp.sum(jnp.where(i_column == i_row, block_column, 0.0), axis=0, keepdims=True)
    block = (block_row.astype(jnp.int32), block_column.astype(jnp.int32))
    seq = both(lambda m: m // 12, block)
    rest = both(lambda m, s: m - 12 * s, block, seq)
    source = both(lambda s, r: (s // 8) * 2 + jnp.where(r >= 6, 1, 0), seq, rest)
    local = both(
        lambda s, r: (s - 8 * (s // 8)) * 6 + jnp.where(r >= 6, r - 6, r), seq, rest
    )
    target = both(lambda i: i // HELD, i)
    ahead = both(lambda a, b: jnp.where(b >= a, b - a, b - a + PLANES), source, target)
    turn = both(lambda r: r - 2 * (r // 2), rank(both(lambda a, b: a * 8 + b, source, target)))
    sign = both(
        lambda k, t: jnp.where(k < 4, 1, jnp.where((k == 4) & (t == 0), 1, -1)), ahead, turn
    )
    distance = both(lambda k: jnp.where(k <= 4, k, PLANES - k), ahead)
    def split(turn):
        first = both(
            lambda d, t: jnp.where(
                d == 0,
                0,
                jnp.where(d == 1, t, jnp.where(d == 2, 2 * t, jnp.where(d == 3, 1 + t, 2))),
            ),
            distance,
            turn,
        )
        second = both(lambda d, o: d - o, distance, first)
        relay = both(
            lambda z, s, o: jnp.bitwise_and(z + s * o + PLANES, PLANES - 1), source, sign, first
        )
        return first, second, relay

    late = both(lambda d, i: jnp.where(d == 4, i, i + count), distance, i)
    for leg in range(2):
        first, second, relay = split(turn)
        plane, hop = ((source, first), (relay, second))[leg]
        crowd = rank(both(lambda p, s, h: p * 8 + s * h + 2, plane, sign, hop), late)
        turn = both(
            lambda t, d, h, r: jnp.where((h == 2) & (d < 4) & (r >= FLIP[leg]), leg, t),
            turn,
            distance,
            hop,
            crowd,
        )
    first, second, relay = split(turn)

    def slots(plane, hop, room):
        way = both(lambda s, h: jnp.where(h == 0, 0, s * h), sign, hop)
        order = rank(both(lambda p, w: p * 8 + w + 2, plane, way))
        at = room_starts(room)
        slot = both(
            lambda w, r: r
            + jnp.where(w == 2, at[0], jnp.where(w == 1, at[1], jnp.where(w == -1, at[2], at[3]))),
            way,
            order,
        )
        limit = jnp.where(hop[0] == 2, room[0], room[1])
        over = jnp.where((way[0] != 0) & (order[0] >= limit), 1.0, 0.0)
        return slot, jnp.sum(over, axis=1, keepdims=True)

    slot_one, over_one = slots(source, first, ROOM[0])
    slot_two, over_two = slots(relay, second, ROOM[1])
    at_relay = both(lambda o, l, s: jnp.where(o == 0, l, HELD + s), first, local, slot_one)

    def fill(out_ref, plane, hop, slot, room, value):
        size = room_size(room)
        place = lax.broadcasted_iota(jnp.int32, (1, PLANES * size), 1)
        code = jnp.where(hop[1] == 0, -1, plane[1] * size + slot[1])
        chosen = jnp.where(code == place, value[1].astype(jnp.float32), 0.0)
        out_ref[...] = jnp.sum(chosen, axis=0, keepdims=True).astype(jnp.int32)

    fill(send_ref, source, first, slot_one, ROOM[0], local)
    fill(relay_ref, relay, second, slot_two, ROOM[1], at_relay)
    final_ref[...] = jnp.where(
        second[0] == 0, at_relay[0], HELD + room_size(ROOM[0]) + slot_two[0]
    )
    over_ref[...] = (over_one + over_two).astype(jnp.int32)


def plan_routes(partner):
    full = pl.BlockSpec(memory_space=pltpu.VMEM)
    count = partner.shape[0]
    shapes = [(1, PLANES * room_size(room)) for room in ROOM] + [(1, count), (1, 1)]
    return pl.pallas_call(
        route_kernel,
        in_specs=[full],
        out_specs=[full] * 4,
        out_shape=[jax.ShapeDtypeStruct(shape, jnp.int32) for shape in shapes],
        name="plan_routes",
    )(partner.reshape(1, -1))


def short_kernel(
    send_ref, relay_ref, final_ref, q_ref, k_ref, v_ref, row_ref, out_ref, *scratch
):
    chunks = 2 * PARTS
    held, near_in, far_in = (scratch[i * chunks : (i + 1) * chunks] for i in range(3))
    (
        staged_one,
        staged_two,
        staged_out,
        far_ref,
        weights_f,
        weights_b,
        all_q,
        full_k,
        full_v,
        mid_k,
        mid_v,
        all_out,
        rows,
        row_send,
        row_recv,
        load_sem,
        out_sem,
        half_send,
        half_recv,
        p0_send,
        p0b_send,
        p0_recv,
        z1_send,
        z1_recv,
        z2_send,
        z2_recv,
        out_send,
        out_recv,
    ) = scratch[3 * chunks :]
    seq = lax.axis_index("seq")
    head = lax.axis_index("head")
    plane = 2 * (seq // 8) + head // 4
    spot = lax.rem(seq, 8) * 4 + lax.rem(head, 4)
    odd = lax.rem(head, 2)
    pair = spot + 1 - 2 * odd

    def above(hop):
        return lax.rem(plane + hop + PLANES, PLANES)

    barrier = pltpu.get_barrier_semaphore()
    for hop in HOPS:
        pl.semaphore_signal(
            barrier, inc=1, device_id=place_of(above(hop), spot), device_id_type=MESH
        )

    def greet(step, carry):
        pl.semaphore_signal(
            barrier,
            inc=1,
            device_id=place_of(plane, lax.rem(spot + step, PLANE_DEVICES)),
            device_id_type=MESH,
        )
        return carry

    lax.fori_loop(1, PLANE_DEVICES, greet, 0)
    pl.semaphore_wait(barrier, len(HOPS) + PLANE_DEVICES - 1)

    def finish(ref, sem):
        pltpu.make_async_copy(ref, ref, sem).wait()

    def plane_stage(source, target, send, recv):
        def body(step, carry):
            other = lax.rem(spot + step, PLANE_DEVICES)
            pltpu.make_async_remote_copy(
                src_ref=source(other),
                dst_ref=target,
                send_sem=send,
                recv_sem=recv,
                device_id=place_of(plane, other),
                device_id_type=MESH,
            ).start()
            return carry

        lax.fori_loop(1, PLANE_DEVICES, body, 0)
        pltpu.make_async_copy(source(spot), target, recv).start()

    def first_block(place):
        return (place // 4) * 6 + (lax.rem(place, 4) // 2) * 3

    full_rows = pl.ds(pl.multiple_of(odd * HALF, HALF), BLOCK)
    half_rows = pl.ds(pl.multiple_of(2 * HALF * (1 - odd), HALF), HALF)

    def spread(chunk):
        kind, start, size = span_of(chunk)
        ref = (k_ref, v_ref)[kind]

        def piece(base):
            lines = pl.ds(pl.multiple_of(base, 2 * ROWS), size)
            return lambda other: ref.at[
                lines, pl.ds(pl.multiple_of(other * LANES, LANES), LANES)
            ]

        plane_stage(
            piece(odd * HALF + start),
            held[chunk].at[first_block(spot) + 2 * odd],
            p0_send.at[chunk],
            p0_recv.at[chunk],
        )

        @pl.when(odd == start // HALF)
        def _():
            plane_stage(
                piece(2 * HALF * (1 - odd) + start % HALF),
                held[chunk].at[first_block(spot) + 1],
                p0b_send.at[chunk],
                p0_recv.at[chunk],
            )

    def staged(ref, chunk):
        return ref.at[chunk % 2, :, pl.ds(0, span_of(chunk)[2])]

    def z_stage(source, landed, room, send, recv):
        for start, size, hop in zip(room_starts(room), (*room, *room[::-1]), HOPS):
            pltpu.make_async_remote_copy(
                src_ref=source.at[pl.ds(start, size)],
                dst_ref=landed.at[pl.ds(start, size)],
                send_sem=send,
                recv_sem=recv,
                device_id=place_of(above(hop), spot),
                device_id_type=MESH,
            ).start()

    size_one, size_two = (room_size(room) for room in ROOM)

    def leg_one(chunk):
        finish(held[chunk], p0_recv.at[chunk])
        slot, size = chunk % 2, span_of(chunk)[2]
        if chunk >= 2:
            finish(staged(staged_one, chunk - 2), z1_send.at[chunk - 2])

        def body(i, carry):
            for j in range(2):
                where = 2 * i + j
                index = send_ref[0, plane * size_one + where]
                staged_one[slot, where, :size] = held[chunk][index]
            return carry

        lax.fori_loop(0, size_one // 2, body, 0)
        z_stage(
            staged(staged_one, chunk), near_in[chunk], ROOM[0], z1_send.at[chunk], z1_recv.at[chunk]
        )

    def held_or_near(chunk, index):
        kept = held[chunk][jnp.minimum(index, HELD - 1)]
        came = near_in[chunk][jnp.clip(index - HELD, 0, size_one - 1)]
        return jnp.where(index < HELD, kept, came)

    def leg_two(chunk):
        finish(near_in[chunk], z1_recv.at[chunk])
        slot, size = chunk % 2, span_of(chunk)[2]
        if chunk >= 2:
            finish(staged(staged_two, chunk - 2), z2_send.at[chunk - 2])

        def body(i, carry):
            for j in range(2):
                where = 2 * i + j
                index = relay_ref[0, plane * size_two + where]
                staged_two[slot, where, :size] = held_or_near(chunk, index)
            return carry

        lax.fori_loop(0, size_two // 2, body, 0)
        z_stage(
            staged(staged_two, chunk), far_in[chunk], ROOM[1], z2_send.at[chunk], z2_recv.at[chunk]
        )

    def arrived(chunk, count=PLANE_DEVICES):
        kind, start, size = span_of(chunk)
        return far_ref.at[kind, pl.ds(0, count), :, pl.ds(start, size)]

    done = set()

    def finish_far(chunk):
        if chunk not in done:
            done.add(chunk)
            finish(arrived(chunk), out_recv.at[chunk])

    def deliver(chunk):
        finish(far_in[chunk], z2_recv.at[chunk])
        slot, (kind, start, size) = chunk % 2, span_of(chunk)
        if chunk >= 2:
            finish(arrived(chunk - 2, PLANE_DEVICES - 1), out_send.at[chunk - 2])
            finish_far(chunk - 2)
        border = HELD + size_one

        def body(i, carry):
            for j in range(2):
                where = 2 * i + j
                index = final_ref[0, plane * HELD + where]
                last = far_in[chunk][jnp.clip(index - border, 0, size_two - 1)]
                staged_out[slot, where, :size] = jnp.where(
                    index < border, held_or_near(chunk, index), last
                )
            return carry

        lax.fori_loop(0, HELD // 2, body, 0)
        ready = staged(staged_out, chunk)
        plane_stage(
            lambda other: ready.at[pl.ds(first_block(other) + lax.rem(other, 2), 2)],
            far_ref.at[kind, spot, :, pl.ds(start, size)],
            out_send.at[chunk],
            out_recv.at[chunk],
        )

    lower = lax.rem(plane, 2)
    set_rows = 4 * ROW_SET
    near_rows = rows.at[pl.ds(pl.multiple_of(lower * set_rows, ROW_SET), set_rows)]
    far_rows = rows.at[pl.ds(pl.multiple_of((1 - lower) * set_rows, ROW_SET), set_rows)]
    own_rows = rows.at[pl.ds(pl.multiple_of(head * ROW_SET, ROW_SET), ROW_SET)]

    def show_rows():
        for step in range(1, 4):
            other = spot - lax.rem(spot, 4) + lax.rem(spot + step, 4)
            pltpu.make_async_remote_copy(
                src_ref=row_ref,
                dst_ref=own_rows,
                send_sem=row_send.at[0],
                recv_sem=row_recv.at[0],
                device_id=place_of(plane, other),
                device_id_type=MESH,
            ).start()
        pltpu.make_async_copy(row_ref, own_rows, row_recv.at[0]).start()

    def share_rows():
        finish(near_rows, row_recv.at[0])
        pltpu.make_async_remote_copy(
            src_ref=near_rows,
            dst_ref=near_rows,
            send_sem=row_send.at[1],
            recv_sem=row_recv.at[1],
            device_id=place_of(plane + 1 - 2 * lower, spot),
            device_id_type=MESH,
        ).start()

    loads = [
        pltpu.make_async_copy(source, target, load_sem.at[i])
        for i, (source, target) in enumerate(
            ((q_ref, all_q), (k_ref.at[full_rows, :], full_k), (v_ref.at[full_rows, :], full_v))
        )
    ]

    def swap_halves():
        for i, (source, target) in enumerate(((k_ref, mid_k), (v_ref, mid_v))):
            place = target.at[pl.ds(pl.multiple_of(odd * HALF, HALF), HALF), :]
            pltpu.make_async_remote_copy(
                src_ref=source.at[half_rows, :],
                dst_ref=place,
                send_sem=half_send.at[i],
                recv_sem=half_recv.at[i],
                device_id=place_of(plane, pair),
                device_id_type=MESH,
            ).start()
            pltpu.make_async_copy(source.at[half_rows, :], place, half_recv.at[i]).start()

    scale = math.log2(math.e) / math.sqrt(LANES)
    contract = (((1,), (1,)), ((), ()))
    ones = jnp.ones((BLOCK, LANES), jnp.bfloat16)

    def weigh(query, near_keys, far_keys, near_bias, far_bias):
        near = lax.dot_general(query, near_keys, contract, preferred_element_type=jnp.float32)
        far = lax.dot_general(query, far_keys, contract, preferred_element_type=jnp.float32)
        near = near * scale + near_bias
        far = far * scale + far_bias
        highest = jnp.max(jnp.maximum(near, far), axis=1, keepdims=True)
        return tuple(jnp.exp2(part - highest).astype(jnp.bfloat16) for part in (near, far))

    def skew(line):
        return pltpu.roll(
            jnp.broadcast_to(line, (HALF, 2 * BLOCK)),
            2 * BLOCK - HALF + 1,
            1,
            stride=1,
            stride_axis=0,
        )

    def weigh_heads(first, last):
        def body(i, carry):
            lines = rows[pl.ds(pl.multiple_of(i * ROW_SET, ROW_SET), ROW_SET), :]
            for g in range(GROUP):
                one = i * GROUP + g
                columns = pl.ds(pl.multiple_of(one * LANES, LANES), LANES)
                skews = [skew(lines[2 * g + side : 2 * g + side + 1]) for side in range(2)]
                upper = [turned[:, HALF : HALF + BLOCK] for turned in skews]
                under = [turned[:, :BLOCK] for turned in skews]
                near_keys = full_k[:, columns]
                far_keys = far_ref[0, one, odd]
                for half in range(2):
                    lines_here = pl.ds(pl.multiple_of((odd + half) * HALF, HALF), HALF)
                    near, far = weigh(
                        all_q[lines_here, columns], near_keys, far_keys, *(upper, under)[half]
                    )
                    part = slice(half * HALF, (half + 1) * HALF)
                    weights_f[one, part, :BLOCK] = near
                    weights_f[one, part, BLOCK:] = far
                mixed = [jnp.where(odd == 1, u, o) for u, o in zip(under, upper)]
                near, far = weigh(
                    all_q[half_rows, columns], mid_k[:, columns], far_ref[0, one, 1 - odd], *mixed
                )
                weights_b[one, :, :BLOCK] = near
                weights_b[one, :, BLOCK:] = far
            return carry

        lax.fori_loop(first // GROUP, last // GROUP, body, 0)

    def blend(weights, near_values, far_values):
        summed = jnp.dot(
            weights[:, :BLOCK],
            jnp.concatenate([near_values, ones], axis=1),
            preferred_element_type=jnp.float32,
        ) + jnp.dot(
            weights[:, BLOCK:],
            jnp.concatenate([far_values, ones], axis=1),
            preferred_element_type=jnp.float32,
        )
        return (summed[:, :LANES] / summed[:, LANES:]).astype(jnp.bfloat16)

    def blend_heads(first, last):
        def body(i, carry):
            for g in range(GROUP):
                one = i * GROUP + g
                columns = pl.ds(pl.multiple_of(one * LANES, LANES), LANES)
                all_out[full_rows, columns] = blend(
                    weights_f[one], full_v[:, columns], far_ref[1, one, odd]
                )
                all_out[half_rows, columns] = blend(
                    weights_b[one], mid_v[:, columns], far_ref[1, one, 1 - odd]
                )
            return carry

        lax.fori_loop(first // GROUP, last // GROUP, body, 0)

    spread(0)
    spread(1)
    show_rows()
    for load in loads:
        load.start()
    for step in range(chunks + 2):
        if step < chunks:
            leg_one(step)
            if step + 2 < chunks:
                spread(step + 2)
        if step == 1:
            share_rows()
            swap_halves()
        if 1 <= step <= chunks:
            leg_two(step - 1)
        if step >= 2:
            deliver(step - 2)
        turn = step - chunks + 2
        if turn == 0:
            for chunk in range(PARTS):
                finish_far(chunk)
            finish(mid_k, half_recv.at[0])
            finish(mid_v, half_recv.at[1])
            finish(far_rows, row_recv.at[1])
            for load in loads:
                load.wait()
        if turn >= 0:
            weigh_heads(turn * HEADS // 4, (turn + 1) * HEADS // 4)
    finish_far(chunks - 2)
    finish_far(chunks - 1)
    stores = []
    for side in range(2):
        blend_heads(side * HEADS // 2, (side + 1) * HEADS // 2)
        columns = pl.ds(side * HEADS // 2 * LANES, HEADS // 2 * LANES)
        store = pltpu.make_async_copy(
            all_out.at[:, columns], out_ref.at[:, columns], out_sem.at[side]
        )
        store.start()
        stores.append(store)
    for chunk in range(chunks):
        finish(arrived(chunk, PLANE_DEVICES - 1).at[:, 0], p0_send.at[chunk])

        @pl.when(odd == span_of(chunk)[1] // HALF)
        def _():
            finish(arrived(chunk, PLANE_DEVICES - 1).at[:, 0], p0b_send.at[chunk])

    for chunk in range(chunks - 2, chunks):
        finish(staged(staged_one, chunk), z1_send.at[chunk])
        finish(staged(staged_two, chunk), z2_send.at[chunk])
        finish(arrived(chunk, PLANE_DEVICES - 1), out_send.at[chunk])
    for i, target in enumerate((mid_k, mid_v)):
        finish(target.at[pl.ds(0, HALF), :], half_send.at[i])
    finish(rows.at[pl.ds(0, 3 * ROW_SET)], row_send.at[0])
    finish(near_rows, row_send.at[1])
    for store in stores:
        store.wait()


def short_move(routes, queries, keys, values, own_rows):
    lines, columns = keys.shape
    kind = keys.dtype
    chunks = 2 * PARTS
    sizes = [room_size(room) for room in ROOM]
    anywhere = pl.BlockSpec(memory_space=pltpu.HBM)

    def vmem(*shape):
        return pltpu.VMEM(shape, kind)

    spans = [span_of(chunk)[2] for chunk in range(chunks)]
    scratch = []
    for count in (HELD, *sizes):
        scratch += [vmem(count, size, LANES) for size in spans]
    scratch += [vmem(2, count, max(spans), LANES) for count in (*sizes, HELD)]
    scratch += [
        vmem(2, HEADS, 2, BLOCK, LANES),
        vmem(HEADS, BLOCK, 2 * BLOCK),
        vmem(HEADS, HALF, 2 * BLOCK),
        vmem(lines, columns),
    ]
    scratch += [vmem(BLOCK, columns)] * 4 + [vmem(lines, columns)]
    scratch += [pltpu.VMEM((2 * HEADS, 2 * BLOCK), jnp.float32)]
    scratch += [pltpu.SemaphoreType.DMA((2,))] * 2
    scratch += [pltpu.SemaphoreType.DMA((3,))]
    scratch += [pltpu.SemaphoreType.DMA((2,))] * 3
    scratch += [pltpu.SemaphoreType.DMA((chunks,))] * 9
    return pl.pallas_call(
        short_kernel,
        in_specs=[pl.BlockSpec(memory_space=pltpu.SMEM)] * 3
        + [anywhere] * 3
        + [pl.BlockSpec(memory_space=pltpu.VMEM)],
        out_specs=anywhere,
        out_shape=jax.ShapeDtypeStruct((lines, columns), kind),
        scratch_shapes=scratch,
        compiler_params=pltpu.CompilerParams(
            collective_id=1, has_side_effects=True, vmem_limit_bytes=60 * 1024 * 1024
        ),
        name="short_move",
    )(*routes, queries, keys, values, own_rows)


def tile_table(partner):
    trio = partner // 3
    member = partner - 3 * trio
    entries = []
    for source, slot in (
        (jnp.where(member == 2, 1, 0), jnp.where(member == 1, 2, 0)),
        (jnp.where(member == 0, 0, 1), jnp.where(member == 1, 2, 1)),
    ):
        device = 2 * trio + source
        seq, head = device // 8, device % 8
        plane = (seq // 8) * 2 + head // 4
        spot = (seq % 8) * 4 + head % 4
        entries.append((slot * PLANE_DEVICES + spot) * PLANES + plane)
    return jnp.concatenate(entries)


def on_device(queries, key_states, value_states, partner, buckets, bias_table):
    one_hot = (
        buckets[..., None] == jnp.arange(bias_table.shape[0], dtype=jnp.int32)
    ).astype(jnp.float32)
    own_rows = jnp.einsum("skb,bh->hsk", one_hot, bias_table, precision=lax.Precision.HIGHEST)
    own_rows = jnp.pad(own_rows * math.log2(math.e), ((0, 0), (0, 0), (0, 1)))

    own_rows = own_rows.reshape(ROW_SET, 2 * BLOCK)
    *routes, over = plan_routes(partner)
    return lax.cond(
        over[0, 0] == 0,
        lambda: short_move(routes, queries, key_states, value_states, own_rows),
        lambda: move_tiles(
            tile_table(partner), queries, key_states, value_states, own_rows
        ),
    )


def solution(mesh):
    whole = P(("seq", "head"), None)
    return jax.shard_map(
        on_device,
        mesh=mesh,
        in_specs=(whole, whole, whole, P(), P(), P(None, "head")),
        out_specs=whole,
        check_vma=False,
    )
```

```python
import math

import jax
import jax.numpy as jnp
from jax import lax
from jax.experimental import pallas as pl
from jax.experimental.pallas import tpu as pltpu
from jax.sharding import PartitionSpec as P

BLOCK = 256
HALF = 128
HEADS = 32
LANES = 128
ROWS = 16
CHUNKS = 8
GROUP = 4


MESH = pl.DeviceIdType.MESH
PLANES = 8
PLANE_DEVICES = 32
SLOTS = 3
ROW_SET = 8
ORDER = (1, 0, 2)


def place_of(plane, spot):
    return ((plane // 2) * 8 + spot // 4, lax.rem(plane, 2) * 4 + lax.rem(spot, 4))


def move_kernel(
    table_ref,
    q_ref,
    k_ref,
    v_ref,
    row_ref,
    out_ref,
    far_ref,
    mid_q_ref,
    mid_k_ref,
    mid_v_ref,
    whole_q,
    whole_k,
    whole_v,
    whole_out,
    middle_out,
    weights,
    fanned,
    held_k,
    held_v,
    picked_k,
    picked_v,
    landed,
    rows,
    skewed,
    row_send,
    row_recv,
    whole_sem,
    out_sem,
    swap_send,
    swap_recv,
    half_send,
    half_recv,
    z1_send,
    z1_recv,
    p1_send,
    p1_recv,
    z2_send,
    z2_recv,
    p2_send,
    p2_recv,
):
    seq = lax.axis_index("seq")
    head = lax.axis_index("head")
    plane = 2 * (seq // 8) + head // 4
    spot = lax.rem(seq, 8) * 4 + lax.rem(head, 4)
    odd = lax.rem(head, 2)
    pair = spot + 1 - 2 * odd

    barrier = pltpu.get_barrier_semaphore()
    for step in range(1, PLANES):
        pl.semaphore_signal(
            barrier,
            inc=1,
            device_id=place_of(lax.rem(plane + step, PLANES), spot),
            device_id_type=MESH,
        )

    def greet(step, carry):
        pl.semaphore_signal(
            barrier,
            inc=1,
            device_id=place_of(plane, lax.rem(spot + step, PLANE_DEVICES)),
            device_id_type=MESH,
        )
        return carry

    lax.fori_loop(1, PLANE_DEVICES, greet, 0)
    pl.semaphore_wait(barrier, PLANES - 1 + PLANE_DEVICES - 1)

    def finish(ref, sem):
        pltpu.make_async_copy(ref, ref, sem).wait()

    def z_stage(source, target, send, recv):
        for step in (4, 3, 5, 2, 6, 1, 7):
            other = lax.rem(plane + step, PLANES)
            pltpu.make_async_remote_copy(
                src_ref=source(other),
                dst_ref=target,
                send_sem=send,
                recv_sem=recv,
                device_id=place_of(other, spot),
                device_id_type=MESH,
            ).start()
        pltpu.make_async_copy(source(plane), target, recv).start()

    def plane_stage(source, target, send, recv):
        def body(step, carry):
            other = lax.rem(spot + step, PLANE_DEVICES)
            pltpu.make_async_remote_copy(
                src_ref=source(other),
                dst_ref=target,
                send_sem=send,
                recv_sem=recv,
                device_id=place_of(plane, other),
                device_id_type=MESH,
            ).start()
            return carry

        lax.fori_loop(1, PLANE_DEVICES, body, 0)
        pltpu.make_async_copy(source(spot), target, recv).start()

    def fan_out(chunk):
        kind, slot = divmod(chunk, SLOTS)
        ref = (k_ref, v_ref)[kind]
        first = (odd * HALF, odd * HALF + HALF, 2 * HALF * (1 - odd))[slot]
        z_stage(
            lambda other: ref.at[pl.ds(pl.multiple_of(first + ROWS * other, ROWS), ROWS), :],
            fanned.at[chunk, plane],
            z1_send.at[chunk],
            z1_recv.at[chunk],
        )

    def by_head(chunk):
        kind, slot = divmod(chunk, SLOTS)
        held = (held_k, held_v)[kind]
        shift = (0, HEADS // 2, odd * (HEADS // 2))[slot]

        def source(other):
            start = pl.multiple_of(lax.rem(other + shift, HEADS) * LANES, LANES)
            return fanned.at[chunk, :, :, pl.ds(start, LANES)]

        plane_stage(
            source,
            held.at[pl.ds((slot * PLANE_DEVICES + spot) * PLANES, PLANES)],
            p1_send.at[chunk],
            p1_recv.at[chunk],
        )

    side = spot // (HEADS // 2)
    blocks = table_ref.shape[0] // 2

    def pick(kind, slot):
        held = (held_k, held_v)[kind]
        picked = (picked_k, picked_v)[kind]

        def body(z, carry):
            first = (z // 2) * 96 + lax.rem(z, 2) * 6
            base = slot * PLANES * PLANE_DEVICES + z
            for p in range(PLANE_DEVICES):
                e = p % 2
                low = (True, e == 0, False)[slot]
                member = 1 if slot == 1 else 2 * e
                block = first + (p // 4) * 12 + (p % 4 // 2) * 3 + member
                chosen = side if low else 1 - side
                picked[base + p * PLANES] = held[table_ref[chosen * blocks + block]]
            return carry

        lax.fori_loop(0, PLANES, body, 0)

    def share_picked(chunk):
        kind, slot = divmod(chunk, SLOTS)
        picked = (picked_k, picked_v)[kind]
        plane_stage(
            lambda other: picked.at[pl.ds((slot * PLANE_DEVICES + other) * PLANES, PLANES)],
            landed.at[chunk, :, spot],
            p2_send.at[chunk],
            p2_recv.at[chunk],
        )

    def deliver(chunk):
        finish(landed.at[chunk], p2_recv.at[chunk])
        z_stage(
            lambda other: landed.at[chunk, other],
            far_ref.at[chunk, plane],
            z2_send.at[chunk],
            z2_recv.at[chunk],
        )

    lower = lax.rem(plane, 2)
    set_rows = 4 * ROW_SET
    near_rows = rows.at[pl.ds(pl.multiple_of(lower * set_rows, ROW_SET), set_rows)]
    far_rows = rows.at[pl.ds(pl.multiple_of((1 - lower) * set_rows, ROW_SET), set_rows)]
    own_rows = rows.at[pl.ds(pl.multiple_of(head * ROW_SET, ROW_SET), ROW_SET)]

    for step in range(1, 4):
        other = spot - lax.rem(spot, 4) + lax.rem(spot + step, 4)
        pltpu.make_async_remote_copy(
            src_ref=row_ref,
            dst_ref=own_rows,
            send_sem=row_send.at[0],
            recv_sem=row_recv.at[0],
            device_id=place_of(plane, other),
            device_id_type=MESH,
        ).start()
    pltpu.make_async_copy(row_ref, own_rows, row_recv.at[0]).start()

    def share_rows():
        finish(near_rows, row_recv.at[0])
        pltpu.make_async_remote_copy(
            src_ref=near_rows,
            dst_ref=near_rows,
            send_sem=row_send.at[1],
            recv_sem=row_recv.at[1],
            device_id=place_of(plane + 1 - 2 * lower, spot),
            device_id_type=MESH,
        ).start()

    def skew_rows():
        finish(far_rows, row_recv.at[1])

        def body(i, carry):
            start = pl.multiple_of(i * ROW_SET, ROW_SET)
            some = rows[pl.ds(start, ROW_SET), :]
            for j in range(ROW_SET):
                turned = pltpu.roll(
                    jnp.broadcast_to(some[j : j + 1], (HALF, 2 * BLOCK)),
                    2 * BLOCK - HALF + 1,
                    1,
                    stride=1,
                    stride_axis=0,
                )
                skewed[start + j] = turned[:, : BLOCK + HALF]
            return carry

        lax.fori_loop(0, 2 * HEADS // ROW_SET, body, 0)

    scale = math.log2(math.e) / math.sqrt(LANES)
    contract = (((1,), (1,)), ((), ()))
    half_heads = HEADS // 2

    ones = jnp.ones((BLOCK, LANES), jnp.bfloat16)

    def far_block(chunk, head):
        other = lax.rem(head + half_heads, HEADS)
        return jnp.concatenate(
            [far_ref[chunk, :, one].reshape(HALF, LANES) for one in (head, other)], axis=0
        )

    def weigh(query, near_keys, far_keys, head, half):
        shift = HALF * (1 - half)
        near = lax.dot_general(query, near_keys, contract, preferred_element_type=jnp.float32)
        far = lax.dot_general(query, far_keys, contract, preferred_element_type=jnp.float32)
        near = near * scale + skewed[2 * head, :, shift : shift + BLOCK]
        far = far * scale + skewed[2 * head + 1, :, shift : shift + BLOCK]
        highest = jnp.max(jnp.maximum(near, far), axis=1, keepdims=True)
        return tuple(jnp.exp2(part - highest).astype(jnp.bfloat16) for part in (near, far))

    def blend(near, far, near_values, far_values):
        summed = jnp.dot(near, near_values, preferred_element_type=jnp.float32) + jnp.dot(
            far, far_values, preferred_element_type=jnp.float32
        )
        return (summed[:, :LANES] / summed[:, LANES:]).astype(jnp.bfloat16)

    def over_heads(slot, visit):
        middle = slot == 1
        first = (0, half_heads * odd, half_heads)[slot]

        def body(i, carry):
            for g in range(GROUP):
                place = i * GROUP + g
                start = (place if middle else first + place) * LANES
                visit(place, first + place, pl.ds(pl.multiple_of(start, LANES), LANES))
            return carry

        lax.fori_loop(0, half_heads // GROUP, body, 0)

    def attend(slot):
        middle = slot == 1
        q, k, v = (mid_q_ref, mid_k_ref, mid_v_ref) if middle else (whole_q, whole_k, whole_v)
        target = middle_out if middle else whole_out

        def visit(place, head, columns):
            near_keys = k[:, columns]
            far_keys = far_block(slot, head)
            near_values = jnp.concatenate([v[:, columns], ones], axis=1)
            far_values = jnp.concatenate([far_block(SLOTS + slot, head), ones], axis=1)
            for half in range(2):
                part = slice(half * HALF, (half + 1) * HALF)
                near, far = weigh(q[part, columns], near_keys, far_keys, head, half)
                target[part, columns] = blend(near, far, near_values, far_values)

        over_heads(slot, visit)

    def weigh_last():
        def visit(place, head, columns):
            near_keys = whole_k[:, columns]
            far_keys = far_block(2, head)
            for half in range(2):
                part = slice(half * HALF, (half + 1) * HALF)
                near, far = weigh(whole_q[part, columns], near_keys, far_keys, head, half)
                weights[place, part, :BLOCK] = near
                weights[place, part, BLOCK:] = far

        over_heads(2, visit)

    def blend_last():
        def visit(place, head, columns):
            near_values = jnp.concatenate([whole_v[:, columns], ones], axis=1)
            far_values = jnp.concatenate([far_block(SLOTS + 2, head), ones], axis=1)
            whole_out[:, columns] = blend(
                weights[place, :, :BLOCK], weights[place, :, BLOCK:], near_values, far_values
            )

        over_heads(2, visit)

    whole_rows = pl.ds(pl.multiple_of(odd * HALF, HALF), BLOCK)
    side_width = half_heads * LANES

    def store_whole(side):
        columns = pl.ds(side * side_width, side_width)
        return pltpu.make_async_copy(
            whole_out.at[:, columns], out_ref.at[whole_rows, columns], out_sem.at[side]
        )

    own_columns = pl.ds(pl.multiple_of(odd * side_width, LANES), side_width)
    own_place = out_ref.at[pl.ds(pl.multiple_of(2 * HALF * (1 - odd), HALF), HALF), own_columns]
    store_middle = pltpu.make_async_copy(
        middle_out.at[pl.ds(pl.multiple_of(odd * HALF, HALF), HALF), :], own_place, out_sem.at[2]
    )
    swap_middle = pltpu.make_async_remote_copy(
        src_ref=middle_out.at[pl.ds(pl.multiple_of((1 - odd) * HALF, HALF), HALF), :],
        dst_ref=out_ref.at[pl.ds(pl.multiple_of(2 * HALF * odd, HALF), HALF), own_columns],
        send_sem=swap_send,
        recv_sem=swap_recv,
        device_id=place_of(plane, pair),
        device_id_type=MESH,
    )
    loads = [
        pltpu.make_async_copy(source.at[whole_rows, :], target, whole_sem.at[i])
        for i, (source, target) in enumerate(((q_ref, whole_q), (k_ref, whole_k), (v_ref, whole_v)))
    ]

    for chunk in range(SLOTS):
        fan_out(chunk)
    for i, (source, target) in enumerate(((q_ref, mid_q_ref), (k_ref, mid_k_ref), (v_ref, mid_v_ref))):
        half_rows = pl.ds(pl.multiple_of(2 * HALF * (1 - odd), HALF), HALF)
        width = target.shape[1]
        own = pl.ds(pl.multiple_of(odd * width, LANES), width)
        given = pl.ds(pl.multiple_of((1 - odd) * width, LANES), width)
        place = target.at[pl.ds(pl.multiple_of(odd * HALF, HALF), HALF), :]
        pltpu.make_async_remote_copy(
            src_ref=source.at[half_rows, given],
            dst_ref=place,
            send_sem=half_send.at[i],
            recv_sem=half_recv.at[i],
            device_id=place_of(plane, pair),
            device_id_type=MESH,
        ).start()
        pltpu.make_async_copy(source.at[half_rows, own], place, half_recv.at[i]).start()
    for load in loads:
        load.start()
    def choose(kind):
        held = (held_k, held_v)[kind]
        for slot in range(SLOTS):
            part = held.at[pl.ds(slot * PLANE_DEVICES * PLANES, PLANE_DEVICES * PLANES)]
            finish(part, p1_recv.at[kind * SLOTS + slot])
        for slot in ORDER:
            pick(kind, slot)
            share_picked(kind * SLOTS + slot)

    for chunk in range(SLOTS):
        finish(fanned.at[chunk], z1_recv.at[chunk])
        by_head(chunk)
        fan_out(chunk + SLOTS)
    choose(0)
    share_rows()
    for i, slot in enumerate(ORDER):
        finish(fanned.at[SLOTS + i], z1_recv.at[SLOTS + i])
        by_head(SLOTS + i)
        deliver(slot)
    skew_rows()
    choose(1)
    for slot in ORDER:
        deliver(SLOTS + slot)
    for slot in ORDER:
        finish(far_ref.at[slot], z2_recv.at[slot])
    for i, target in enumerate((mid_q_ref, mid_k_ref, mid_v_ref)):
        finish(target, half_recv.at[i])
    for load in loads:
        load.wait()
    weigh_last()
    for slot in ORDER:
        finish(far_ref.at[SLOTS + slot], z2_recv.at[SLOTS + slot])
        if slot == 2:
            blend_last()
        else:
            attend(slot)
        if slot == 1:
            store_middle.start()
            swap_middle.start()
        else:
            store_whole(slot // 2).start()
    for i, target in enumerate((mid_q_ref, mid_k_ref, mid_v_ref)):
        finish(target.at[pl.ds(0, HALF), :], half_send.at[i])
    for chunk in range(2 * SLOTS):
        finish(fanned.at[chunk, pl.ds(0, PLANES - 1)], z1_send.at[chunk])
        finish(landed.at[chunk, :, pl.ds(0, PLANE_DEVICES - 1)], p1_send.at[chunk])
        finish(landed.at[chunk, :, pl.ds(0, PLANE_DEVICES - 1)], p2_send.at[chunk])
        finish(landed.at[chunk, pl.ds(0, PLANES - 1)], z2_send.at[chunk])
    finish(rows.at[pl.ds(0, 3 * ROW_SET)], row_send.at[0])
    finish(near_rows, row_send.at[1])
    store_middle.wait()
    swap_middle.wait()
    store_whole(0).wait()
    store_whole(1).wait()


def move_tiles(table, queries, keys, values, own_rows):
    rows, columns = keys.shape
    kind = keys.dtype
    chunks = 2 * SLOTS
    tiles = SLOTS * PLANES * PLANE_DEVICES
    anywhere = pl.BlockSpec(memory_space=pltpu.HBM)
    semaphores = (
        [pltpu.SemaphoreType.DMA((2,))] * 2
        + [pltpu.SemaphoreType.DMA((3,))] * 2
        + [pltpu.SemaphoreType.DMA] * 2
        + [pltpu.SemaphoreType.DMA((3,))] * 2
        + [pltpu.SemaphoreType.DMA((chunks,))] * 8
    )
    return pl.pallas_call(
        move_kernel,
        in_specs=[pl.BlockSpec(memory_space=pltpu.SMEM)]
        + [anywhere] * 3
        + [pl.BlockSpec(memory_space=pltpu.VMEM)],
        out_specs=anywhere,
        out_shape=jax.ShapeDtypeStruct((rows, columns), kind),
        scratch_shapes=[pltpu.VMEM((chunks, PLANES, PLANE_DEVICES, ROWS, LANES), kind)]
        + [pltpu.VMEM((BLOCK, columns // 2), kind)] * 3
        + [pltpu.VMEM((BLOCK, columns), kind)] * 4
        + [pltpu.VMEM((BLOCK, columns // 2), kind)]
        + [pltpu.VMEM((HEADS // 2, BLOCK, 2 * BLOCK), kind)]
        + [pltpu.VMEM((chunks, PLANES, ROWS, columns), kind)]
        + [pltpu.VMEM((tiles, ROWS, LANES), kind)] * 4
        + [
            pltpu.VMEM((chunks, PLANES, PLANE_DEVICES, ROWS, LANES), kind),
            pltpu.VMEM((2 * HEADS, 2 * BLOCK), jnp.float32),
            pltpu.VMEM((2 * HEADS, HALF, BLOCK + HALF), jnp.float32),
        ]
        + semaphores,
        cost_estimate=pl.CostEstimate(
            flops=0, transcendentals=0, bytes_accessed=1024 * 1024 * 1024
        ),
        compiler_params=pltpu.CompilerParams(
            collective_id=0, has_side_effects=True, vmem_limit_bytes=60 * 1024 * 1024
        ),
        name="move_tiles",
    )(table, queries, keys, values, own_rows)


PARTS = 4
SPANS = (((0, 32), (32, 96), (128, 64), (192, 64)), ((0, 64), (64, 64), (128, 96), (224, 32)))
HELD = 48
ROOM = ((13, 10), (12, 11))
FLIP = (11, 12)
HOPS = (2, 1, -1, -2)


def span_of(chunk):
    kind, part = divmod(chunk, PARTS)
    return kind, *SPANS[kind][part]


def room_starts(room):
    far, near = room
    return (0, far, far + near, far + 2 * near)


def room_size(room):
    return 2 * sum(room)


def route_kernel(partner_ref, send_ref, relay_ref, final_ref, over_ref):
    count = partner_ref.shape[1]
    i_row = lax.broadcasted_iota(jnp.int32, (1, count), 1)
    i_column = lax.broadcasted_iota(jnp.int32, (count, 1), 0)

    def both(f, *pairs):
        return tuple(f(*(pair[s] for pair in pairs)) for s in range(2))

    i = (i_row, i_column)

    def rank(key, order=i):
        same = key[1] == key[0]
        before = jnp.where(same & (order[1] < order[0]), 1.0, 0.0)
        after = jnp.where(same & (order[0] < order[1]), 1.0, 0.0)
        in_row = jnp.sum(before, axis=0, keepdims=True)
        in_column = jnp.sum(after, axis=1, keepdims=True)
        return in_row.astype(jnp.int32), in_column.astype(jnp.int32)

    asked = partner_ref[...].astype(jnp.float32)
    in_plane = i_column - HELD * (i_column // HELD)
    group = in_plane // 6
    wanted = ((i_column // 96) * 8 + group) * 12 + in_plane - 6 * group
    wanted = wanted + jnp.where(i_column - 96 * (i_column // 96) >= HELD, 6, 0)
    block_column = jnp.sum(jnp.where(wanted == i_row, asked, 0.0), axis=1, keepdims=True)
    block_row = jnp.sum(jnp.where(i_column == i_row, block_column, 0.0), axis=0, keepdims=True)
    block = (block_row.astype(jnp.int32), block_column.astype(jnp.int32))
    seq = both(lambda m: m // 12, block)
    rest = both(lambda m, s: m - 12 * s, block, seq)
    source = both(lambda s, r: (s // 8) * 2 + jnp.where(r >= 6, 1, 0), seq, rest)
    local = both(
        lambda s, r: (s - 8 * (s // 8)) * 6 + jnp.where(r >= 6, r - 6, r), seq, rest
    )
    target = both(lambda i: i // HELD, i)
    ahead = both(lambda a, b: jnp.where(b >= a, b - a, b - a + PLANES), source, target)
    turn = both(lambda r: r - 2 * (r // 2), rank(both(lambda a, b: a * 8 + b, source, target)))
    sign = both(
        lambda k, t: jnp.where(k < 4, 1, jnp.where((k == 4) & (t == 0), 1, -1)), ahead, turn
    )
    distance = both(lambda k: jnp.where(k <= 4, k, PLANES - k), ahead)
    def split(turn):
        first = both(
            lambda d, t: jnp.where(
                d == 0,
                0,
                jnp.where(d == 1, t, jnp.where(d == 2, 2 * t, jnp.where(d == 3, 1 + t, 2))),
            ),
            distance,
            turn,
        )
        second = both(lambda d, o: d - o, distance, first)
        relay = both(
            lambda z, s, o: jnp.bitwise_and(z + s * o + PLANES, PLANES - 1), source, sign, first
        )
        return first, second, relay

    late = both(lambda d, i: jnp.where(d == 4, i, i + count), distance, i)
    for leg in range(2):
        first, second, relay = split(turn)
        plane, hop = ((source, first), (relay, second))[leg]
        crowd = rank(both(lambda p, s, h: p * 8 + s * h + 2, plane, sign, hop), late)
        turn = both(
            lambda t, d, h, r: jnp.where((h == 2) & (d < 4) & (r >= FLIP[leg]), leg, t),
            turn,
            distance,
            hop,
            crowd,
        )
    first, second, relay = split(turn)

    def slots(plane, hop, room):
        way = both(lambda s, h: jnp.where(h == 0, 0, s * h), sign, hop)
        order = rank(both(lambda p, w: p * 8 + w + 2, plane, way))
        at = room_starts(room)
        slot = both(
            lambda w, r: r
            + jnp.where(w == 2, at[0], jnp.where(w == 1, at[1], jnp.where(w == -1, at[2], at[3]))),
            way,
            order,
        )
        limit = jnp.where(hop[0] == 2, room[0], room[1])
        over = jnp.where((way[0] != 0) & (order[0] >= limit), 1.0, 0.0)
        return slot, jnp.sum(over, axis=1, keepdims=True)

    slot_one, over_one = slots(source, first, ROOM[0])
    slot_two, over_two = slots(relay, second, ROOM[1])
    at_relay = both(lambda o, l, s: jnp.where(o == 0, l, HELD + s), first, local, slot_one)

    def fill(out_ref, plane, hop, slot, room, value):
        size = room_size(room)
        place = lax.broadcasted_iota(jnp.int32, (1, PLANES * size), 1)
        code = jnp.where(hop[1] == 0, -1, plane[1] * size + slot[1])
        chosen = jnp.where(code == place, value[1].astype(jnp.float32), 0.0)
        out_ref[...] = jnp.sum(chosen, axis=0, keepdims=True).astype(jnp.int32)

    fill(send_ref, source, first, slot_one, ROOM[0], local)
    fill(relay_ref, relay, second, slot_two, ROOM[1], at_relay)
    final_ref[...] = jnp.where(
        second[0] == 0, at_relay[0], HELD + room_size(ROOM[0]) + slot_two[0]
    )
    over_ref[...] = (over_one + over_two).astype(jnp.int32)


def plan_routes(partner):
    full = pl.BlockSpec(memory_space=pltpu.VMEM)
    count = partner.shape[0]
    shapes = [(1, PLANES * room_size(room)) for room in ROOM] + [(1, count), (1, 1)]
    return pl.pallas_call(
        route_kernel,
        in_specs=[full],
        out_specs=[full] * 4,
        out_shape=[jax.ShapeDtypeStruct(shape, jnp.int32) for shape in shapes],
        name="plan_routes",
    )(partner.reshape(1, -1))


def short_kernel(
    send_ref, relay_ref, final_ref, q_ref, k_ref, v_ref, row_ref, out_ref, *scratch
):
    chunks = 2 * PARTS
    held, near_in, far_in = (scratch[i * chunks : (i + 1) * chunks] for i in range(3))
    (
        staged_one,
        staged_two,
        staged_out,
        far_ref,
        weights_f,
        weights_b,
        all_q,
        full_k,
        full_v,
        mid_k,
        mid_v,
        all_out,
        rows,
        row_send,
        row_recv,
        load_sem,
        out_sem,
        half_send,
        half_recv,
        p0_send,
        p0b_send,
        p0_recv,
        z1_send,
        z1_recv,
        z2_send,
        z2_recv,
        out_send,
        out_recv,
    ) = scratch[3 * chunks :]
    seq = lax.axis_index("seq")
    head = lax.axis_index("head")
    plane = 2 * (seq // 8) + head // 4
    spot = lax.rem(seq, 8) * 4 + lax.rem(head, 4)
    odd = lax.rem(head, 2)
    pair = spot + 1 - 2 * odd

    def above(hop):
        return lax.rem(plane + hop + PLANES, PLANES)

    barrier = pltpu.get_barrier_semaphore()
    for hop in HOPS:
        pl.semaphore_signal(
            barrier, inc=1, device_id=place_of(above(hop), spot), device_id_type=MESH
        )

    def greet(step, carry):
        pl.semaphore_signal(
            barrier,
            inc=1,
            device_id=place_of(plane, lax.rem(spot + step, PLANE_DEVICES)),
            device_id_type=MESH,
        )
        return carry

    lax.fori_loop(1, PLANE_DEVICES, greet, 0)
    pl.semaphore_wait(barrier, len(HOPS) + PLANE_DEVICES - 1)

    def finish(ref, sem):
        pltpu.make_async_copy(ref, ref, sem).wait()

    def plane_stage(source, target, send, recv):
        def body(step, carry):
            other = lax.rem(spot + step, PLANE_DEVICES)
            pltpu.make_async_remote_copy(
                src_ref=source(other),
                dst_ref=target,
                send_sem=send,
                recv_sem=recv,
                device_id=place_of(plane, other),
                device_id_type=MESH,
            ).start()
            return carry

        lax.fori_loop(1, PLANE_DEVICES, body, 0)
        pltpu.make_async_copy(source(spot), target, recv).start()

    def first_block(place):
        return (place // 4) * 6 + (lax.rem(place, 4) // 2) * 3

    full_rows = pl.ds(pl.multiple_of(odd * HALF, HALF), BLOCK)
    half_rows = pl.ds(pl.multiple_of(2 * HALF * (1 - odd), HALF), HALF)

    def spread(chunk):
        kind, start, size = span_of(chunk)
        ref = (k_ref, v_ref)[kind]

        def piece(base):
            lines = pl.ds(pl.multiple_of(base, 2 * ROWS), size)
            return lambda other: ref.at[
                lines, pl.ds(pl.multiple_of(other * LANES, LANES), LANES)
            ]

        plane_stage(
            piece(odd * HALF + start),
            held[chunk].at[first_block(spot) + 2 * odd],
            p0_send.at[chunk],
            p0_recv.at[chunk],
        )

        @pl.when(odd == start // HALF)
        def _():
            plane_stage(
                piece(2 * HALF * (1 - odd) + start % HALF),
                held[chunk].at[first_block(spot) + 1],
                p0b_send.at[chunk],
                p0_recv.at[chunk],
            )

    def staged(ref, chunk):
        return ref.at[chunk % 2, :, pl.ds(0, span_of(chunk)[2])]

    def z_stage(source, landed, room, send, recv):
        for start, size, hop in zip(room_starts(room), (*room, *room[::-1]), HOPS):
            pltpu.make_async_remote_copy(
                src_ref=source.at[pl.ds(start, size)],
                dst_ref=landed.at[pl.ds(start, size)],
                send_sem=send,
                recv_sem=recv,
                device_id=place_of(above(hop), spot),
                device_id_type=MESH,
            ).start()

    size_one, size_two = (room_size(room) for room in ROOM)

    def leg_one(chunk):
        finish(held[chunk], p0_recv.at[chunk])
        slot, size = chunk % 2, span_of(chunk)[2]
        if chunk >= 2:
            finish(staged(staged_one, chunk - 2), z1_send.at[chunk - 2])

        def body(i, carry):
            for j in range(2):
                where = 2 * i + j
                index = send_ref[0, plane * size_one + where]
                staged_one[slot, where, :size] = held[chunk][index]
            return carry

        lax.fori_loop(0, size_one // 2, body, 0)
        z_stage(
            staged(staged_one, chunk), near_in[chunk], ROOM[0], z1_send.at[chunk], z1_recv.at[chunk]
        )

    def held_or_near(chunk, index):
        kept = held[chunk][jnp.minimum(index, HELD - 1)]
        came = near_in[chunk][jnp.clip(index - HELD, 0, size_one - 1)]
        return jnp.where(index < HELD, kept, came)

    def leg_two(chunk):
        finish(near_in[chunk], z1_recv.at[chunk])
        slot, size = chunk % 2, span_of(chunk)[2]
        if chunk >= 2:
            finish(staged(staged_two, chunk - 2), z2_send.at[chunk - 2])

        def body(i, carry):
            for j in range(2):
                where = 2 * i + j
                index = relay_ref[0, plane * size_two + where]
                staged_two[slot, where, :size] = held_or_near(chunk, index)
            return carry

        lax.fori_loop(0, size_two // 2, body, 0)
        z_stage(
            staged(staged_two, chunk), far_in[chunk], ROOM[1], z2_send.at[chunk], z2_recv.at[chunk]
        )

    def arrived(chunk, count=PLANE_DEVICES):
        kind, start, size = span_of(chunk)
        return far_ref.at[kind, pl.ds(0, count), :, pl.ds(start, size)]

    done = set()

    def finish_far(chunk):
        if chunk not in done:
            done.add(chunk)
            finish(arrived(chunk), out_recv.at[chunk])

    def deliver(chunk):
        finish(far_in[chunk], z2_recv.at[chunk])
        slot, (kind, start, size) = chunk % 2, span_of(chunk)
        if chunk >= 2:
            finish(arrived(chunk - 2, PLANE_DEVICES - 1), out_send.at[chunk - 2])
            finish_far(chunk - 2)
        border = HELD + size_one

        def body(i, carry):
            for j in range(2):
                where = 2 * i + j
                index = final_ref[0, plane * HELD + where]
                last = far_in[chunk][jnp.clip(index - border, 0, size_two - 1)]
                staged_out[slot, where, :size] = jnp.where(
                    index < border, held_or_near(chunk, index), last
                )
            return carry

        lax.fori_loop(0, HELD // 2, body, 0)
        ready = staged(staged_out, chunk)
        plane_stage(
            lambda other: ready.at[pl.ds(first_block(other) + lax.rem(other, 2), 2)],
            far_ref.at[kind, spot, :, pl.ds(start, size)],
            out_send.at[chunk],
            out_recv.at[chunk],
        )

    lower = lax.rem(plane, 2)
    set_rows = 4 * ROW_SET
    near_rows = rows.at[pl.ds(pl.multiple_of(lower * set_rows, ROW_SET), set_rows)]
    far_rows = rows.at[pl.ds(pl.multiple_of((1 - lower) * set_rows, ROW_SET), set_rows)]
    own_rows = rows.at[pl.ds(pl.multiple_of(head * ROW_SET, ROW_SET), ROW_SET)]

    def show_rows():
        for step in range(1, 4):
            other = spot - lax.rem(spot, 4) + lax.rem(spot + step, 4)
            pltpu.make_async_remote_copy(
                src_ref=row_ref,
                dst_ref=own_rows,
                send_sem=row_send.at[0],
                recv_sem=row_recv.at[0],
                device_id=place_of(plane, other),
                device_id_type=MESH,
            ).start()
        pltpu.make_async_copy(row_ref, own_rows, row_recv.at[0]).start()

    def share_rows():
        finish(near_rows, row_recv.at[0])
        pltpu.make_async_remote_copy(
            src_ref=near_rows,
            dst_ref=near_rows,
            send_sem=row_send.at[1],
            recv_sem=row_recv.at[1],
            device_id=place_of(plane + 1 - 2 * lower, spot),
            device_id_type=MESH,
        ).start()

    loads = [
        pltpu.make_async_copy(source, target, load_sem.at[i])
        for i, (source, target) in enumerate(
            ((q_ref, all_q), (k_ref.at[full_rows, :], full_k), (v_ref.at[full_rows, :], full_v))
        )
    ]

    def swap_halves():
        for i, (source, target) in enumerate(((k_ref, mid_k), (v_ref, mid_v))):
            place = target.at[pl.ds(pl.multiple_of(odd * HALF, HALF), HALF), :]
            pltpu.make_async_remote_copy(
                src_ref=source.at[half_rows, :],
                dst_ref=place,
                send_sem=half_send.at[i],
                recv_sem=half_recv.at[i],
                device_id=place_of(plane, pair),
                device_id_type=MESH,
            ).start()
            pltpu.make_async_copy(source.at[half_rows, :], place, half_recv.at[i]).start()

    scale = math.log2(math.e) / math.sqrt(LANES)
    contract = (((1,), (1,)), ((), ()))
    ones = jnp.ones((BLOCK, LANES), jnp.bfloat16)

    def weigh(query, near_keys, far_keys, near_bias, far_bias):
        near = lax.dot_general(query, near_keys, contract, preferred_element_type=jnp.float32)
        far = lax.dot_general(query, far_keys, contract, preferred_element_type=jnp.float32)
        near = near * scale + near_bias
        far = far * scale + far_bias
        highest = jnp.max(jnp.maximum(near, far), axis=1, keepdims=True)
        return tuple(jnp.exp2(part - highest).astype(jnp.bfloat16) for part in (near, far))

    def skew(line):
        return pltpu.roll(
            jnp.broadcast_to(line, (HALF, 2 * BLOCK)),
            2 * BLOCK - HALF + 1,
            1,
            stride=1,
            stride_axis=0,
        )

    def weigh_heads(first, last):
        def body(i, carry):
            lines = rows[pl.ds(pl.multiple_of(i * ROW_SET, ROW_SET), ROW_SET), :]
            for g in range(GROUP):
                one = i * GROUP + g
                columns = pl.ds(pl.multiple_of(one * LANES, LANES), LANES)
                skews = [skew(lines[2 * g + side : 2 * g + side + 1]) for side in range(2)]
                upper = [turned[:, HALF : HALF + BLOCK] for turned in skews]
                under = [turned[:, :BLOCK] for turned in skews]
                near_keys = full_k[:, columns]
                far_keys = far_ref[0, one, odd]
                for half in range(2):
                    lines_here = pl.ds(pl.multiple_of((odd + half) * HALF, HALF), HALF)
                    near, far = weigh(
                        all_q[lines_here, columns], near_keys, far_keys, *(upper, under)[half]
                    )
                    part = slice(half * HALF, (half + 1) * HALF)
                    weights_f[one, part, :BLOCK] = near
                    weights_f[one, part, BLOCK:] = far
                mixed = [jnp.where(odd == 1, u, o) for u, o in zip(under, upper)]
                near, far = weigh(
                    all_q[half_rows, columns], mid_k[:, columns], far_ref[0, one, 1 - odd], *mixed
                )
                weights_b[one, :, :BLOCK] = near
                weights_b[one, :, BLOCK:] = far
            return carry

        lax.fori_loop(first // GROUP, last // GROUP, body, 0)

    def blend(weights, near_values, far_values):
        summed = jnp.dot(
            weights[:, :BLOCK],
            jnp.concatenate([near_values, ones], axis=1),
            preferred_element_type=jnp.float32,
        ) + jnp.dot(
            weights[:, BLOCK:],
            jnp.concatenate([far_values, ones], axis=1),
            preferred_element_type=jnp.float32,
        )
        return (summed[:, :LANES] / summed[:, LANES:]).astype(jnp.bfloat16)

    def blend_heads(first, last):
        def body(i, carry):
            for g in range(GROUP):
                one = i * GROUP + g
                columns = pl.ds(pl.multiple_of(one * LANES, LANES), LANES)
                all_out[full_rows, columns] = blend(
                    weights_f[one], full_v[:, columns], far_ref[1, one, odd]
                )
                all_out[half_rows, columns] = blend(
                    weights_b[one], mid_v[:, columns], far_ref[1, one, 1 - odd]
                )
            return carry

        lax.fori_loop(first // GROUP, last // GROUP, body, 0)

    spread(0)
    spread(1)
    show_rows()
    for load in loads:
        load.start()
    for step in range(chunks + 3):
        if step < chunks:
            leg_one(step)
            if step + 2 < chunks:
                spread(step + 2)
        if step == 1:
            share_rows()
            swap_halves()
        if 1 <= step < chunks + 1:
            leg_two(step - 1)
        if step >= 3:
            deliver(step - 3)
        turn = step - chunks + 1
        if turn == 0:
            for chunk in range(PARTS):
                finish_far(chunk)
            finish(mid_k, half_recv.at[0])
            finish(mid_v, half_recv.at[1])
            finish(far_rows, row_recv.at[1])
            for load in loads:
                load.wait()
        if turn >= 0:
            weigh_heads(turn * HEADS // 4, (turn + 1) * HEADS // 4)
    finish_far(chunks - 2)
    finish_far(chunks - 1)
    stores = []
    for side in range(2):
        blend_heads(side * HEADS // 2, (side + 1) * HEADS // 2)
        columns = pl.ds(side * HEADS // 2 * LANES, HEADS // 2 * LANES)
        store = pltpu.make_async_copy(
            all_out.at[:, columns], out_ref.at[:, columns], out_sem.at[side]
        )
        store.start()
        stores.append(store)
    for chunk in range(chunks):
        finish(arrived(chunk, PLANE_DEVICES - 1).at[:, 0], p0_send.at[chunk])

        @pl.when(odd == span_of(chunk)[1] // HALF)
        def _():
            finish(arrived(chunk, PLANE_DEVICES - 1).at[:, 0], p0b_send.at[chunk])

    for chunk in range(chunks - 2, chunks):
        finish(staged(staged_one, chunk), z1_send.at[chunk])
        finish(staged(staged_two, chunk), z2_send.at[chunk])
        finish(arrived(chunk, PLANE_DEVICES - 1), out_send.at[chunk])
    for i, target in enumerate((mid_k, mid_v)):
        finish(target.at[pl.ds(0, HALF), :], half_send.at[i])
    finish(rows.at[pl.ds(0, 3 * ROW_SET)], row_send.at[0])
    finish(near_rows, row_send.at[1])
    for store in stores:
        store.wait()


def short_move(routes, queries, keys, values, own_rows):
    lines, columns = keys.shape
    kind = keys.dtype
    chunks = 2 * PARTS
    sizes = [room_size(room) for room in ROOM]
    anywhere = pl.BlockSpec(memory_space=pltpu.HBM)

    def vmem(*shape):
        return pltpu.VMEM(shape, kind)

    spans = [span_of(chunk)[2] for chunk in range(chunks)]
    scratch = []
    for count in (HELD, *sizes):
        scratch += [vmem(count, size, LANES) for size in spans]
    scratch += [vmem(2, count, max(spans), LANES) for count in (*sizes, HELD)]
    scratch += [
        vmem(2, HEADS, 2, BLOCK, LANES),
        vmem(HEADS, BLOCK, 2 * BLOCK),
        vmem(HEADS, HALF, 2 * BLOCK),
        vmem(lines, columns),
    ]
    scratch += [vmem(BLOCK, columns)] * 4 + [vmem(lines, columns)]
    scratch += [pltpu.VMEM((2 * HEADS, 2 * BLOCK), jnp.float32)]
    scratch += [pltpu.SemaphoreType.DMA((2,))] * 2
    scratch += [pltpu.SemaphoreType.DMA((3,))]
    scratch += [pltpu.SemaphoreType.DMA((2,))] * 3
    scratch += [pltpu.SemaphoreType.DMA((chunks,))] * 9
    return pl.pallas_call(
        short_kernel,
        in_specs=[pl.BlockSpec(memory_space=pltpu.SMEM)] * 3
        + [anywhere] * 3
        + [pl.BlockSpec(memory_space=pltpu.VMEM)],
        out_specs=anywhere,
        out_shape=jax.ShapeDtypeStruct((lines, columns), kind),
        scratch_shapes=scratch,
        compiler_params=pltpu.CompilerParams(
            collective_id=1, has_side_effects=True, vmem_limit_bytes=60 * 1024 * 1024
        ),
        name="short_move",
    )(*routes, queries, keys, values, own_rows)


def tile_table(partner):
    trio = partner // 3
    member = partner - 3 * trio
    entries = []
    for source, slot in (
        (jnp.where(member == 2, 1, 0), jnp.where(member == 1, 2, 0)),
        (jnp.where(member == 0, 0, 1), jnp.where(member == 1, 2, 1)),
    ):
        device = 2 * trio + source
        seq, head = device // 8, device % 8
        plane = (seq // 8) * 2 + head // 4
        spot = (seq % 8) * 4 + head % 4
        entries.append((slot * PLANE_DEVICES + spot) * PLANES + plane)
    return jnp.concatenate(entries)


def on_device(queries, key_states, value_states, partner, buckets, bias_table):
    one_hot = (
        buckets[..., None] == jnp.arange(bias_table.shape[0], dtype=jnp.int32)
    ).astype(jnp.float32)
    own_rows = jnp.einsum("skb,bh->hsk", one_hot, bias_table, precision=lax.Precision.HIGHEST)
    own_rows = jnp.pad(own_rows * math.log2(math.e), ((0, 0), (0, 0), (0, 1)))

    own_rows = own_rows.reshape(ROW_SET, 2 * BLOCK)
    *routes, over = plan_routes(partner)
    return lax.cond(
        over[0, 0] == 0,
        lambda: short_move(routes, queries, key_states, value_states, own_rows),
        lambda: move_tiles(
            tile_table(partner), queries, key_states, value_states, own_rows
        ),
    )


def solution(mesh):
    whole = P(("seq", "head"), None)
    return jax.shard_map(
        on_device,
        mesh=mesh,
        in_specs=(whole, whole, whole, P(), P(), P(None, "head")),
        out_specs=whole,
        check_vma=False,
    )
```

```python
import math

import jax
import jax.numpy as jnp
from jax import lax
from jax.experimental import pallas as pl
from jax.experimental.pallas import tpu as pltpu
from jax.sharding import PartitionSpec as P

BLOCK = 256
HALF = 128
HEADS = 32
LANES = 128
ROWS = 16
CHUNKS = 8
GROUP = 4


MESH = pl.DeviceIdType.MESH
PLANES = 8
PLANE_DEVICES = 32
SLOTS = 3
ROW_SET = 8
ORDER = (1, 0, 2)


def place_of(plane, spot):
    return ((plane // 2) * 8 + spot // 4, lax.rem(plane, 2) * 4 + lax.rem(spot, 4))


def move_kernel(
    table_ref,
    q_ref,
    k_ref,
    v_ref,
    row_ref,
    out_ref,
    far_ref,
    mid_q_ref,
    mid_k_ref,
    mid_v_ref,
    whole_q,
    whole_k,
    whole_v,
    whole_out,
    middle_out,
    weights,
    fanned,
    held_k,
    held_v,
    picked_k,
    picked_v,
    landed,
    rows,
    skewed,
    row_send,
    row_recv,
    whole_sem,
    out_sem,
    swap_send,
    swap_recv,
    half_send,
    half_recv,
    z1_send,
    z1_recv,
    p1_send,
    p1_recv,
    z2_send,
    z2_recv,
    p2_send,
    p2_recv,
):
    seq = lax.axis_index("seq")
    head = lax.axis_index("head")
    plane = 2 * (seq // 8) + head // 4
    spot = lax.rem(seq, 8) * 4 + lax.rem(head, 4)
    odd = lax.rem(head, 2)
    pair = spot + 1 - 2 * odd

    barrier = pltpu.get_barrier_semaphore()
    for step in range(1, PLANES):
        pl.semaphore_signal(
            barrier,
            inc=1,
            device_id=place_of(lax.rem(plane + step, PLANES), spot),
            device_id_type=MESH,
        )

    def greet(step, carry):
        pl.semaphore_signal(
            barrier,
            inc=1,
            device_id=place_of(plane, lax.rem(spot + step, PLANE_DEVICES)),
            device_id_type=MESH,
        )
        return carry

    lax.fori_loop(1, PLANE_DEVICES, greet, 0)
    pl.semaphore_wait(barrier, PLANES - 1 + PLANE_DEVICES - 1)

    def finish(ref, sem):
        pltpu.make_async_copy(ref, ref, sem).wait()

    def z_stage(source, target, send, recv):
        for step in (4, 3, 5, 2, 6, 1, 7):
            other = lax.rem(plane + step, PLANES)
            pltpu.make_async_remote_copy(
                src_ref=source(other),
                dst_ref=target,
                send_sem=send,
                recv_sem=recv,
                device_id=place_of(other, spot),
                device_id_type=MESH,
            ).start()
        pltpu.make_async_copy(source(plane), target, recv).start()

    def plane_stage(source, target, send, recv):
        def body(step, carry):
            other = lax.rem(spot + step, PLANE_DEVICES)
            pltpu.make_async_remote_copy(
                src_ref=source(other),
                dst_ref=target,
                send_sem=send,
                recv_sem=recv,
                device_id=place_of(plane, other),
                device_id_type=MESH,
            ).start()
            return carry

        lax.fori_loop(1, PLANE_DEVICES, body, 0)
        pltpu.make_async_copy(source(spot), target, recv).start()

    def fan_out(chunk):
        kind, slot = divmod(chunk, SLOTS)
        ref = (k_ref, v_ref)[kind]
        first = (odd * HALF, odd * HALF + HALF, 2 * HALF * (1 - odd))[slot]
        z_stage(
            lambda other: ref.at[pl.ds(pl.multiple_of(first + ROWS * other, ROWS), ROWS), :],
            fanned.at[chunk, plane],
            z1_send.at[chunk],
            z1_recv.at[chunk],
        )

    def by_head(chunk):
        kind, slot = divmod(chunk, SLOTS)
        held = (held_k, held_v)[kind]
        shift = (0, HEADS // 2, odd * (HEADS // 2))[slot]

        def source(other):
            start = pl.multiple_of(lax.rem(other + shift, HEADS) * LANES, LANES)
            return fanned.at[chunk, :, :, pl.ds(start, LANES)]

        plane_stage(
            source,
            held.at[pl.ds((slot * PLANE_DEVICES + spot) * PLANES, PLANES)],
            p1_send.at[chunk],
            p1_recv.at[chunk],
        )

    side = spot // (HEADS // 2)
    blocks = table_ref.shape[0] // 2

    def pick(kind, slot):
        held = (held_k, held_v)[kind]
        picked = (picked_k, picked_v)[kind]

        def body(z, carry):
            first = (z // 2) * 96 + lax.rem(z, 2) * 6
            base = slot * PLANES * PLANE_DEVICES + z
            for p in range(PLANE_DEVICES):
                e = p % 2
                low = (True, e == 0, False)[slot]
                member = 1 if slot == 1 else 2 * e
                block = first + (p // 4) * 12 + (p % 4 // 2) * 3 + member
                chosen = side if low else 1 - side
                picked[base + p * PLANES] = held[table_ref[chosen * blocks + block]]
            return carry

        lax.fori_loop(0, PLANES, body, 0)

    def share_picked(chunk):
        kind, slot = divmod(chunk, SLOTS)
        picked = (picked_k, picked_v)[kind]
        plane_stage(
            lambda other: picked.at[pl.ds((slot * PLANE_DEVICES + other) * PLANES, PLANES)],
            landed.at[chunk, :, spot],
            p2_send.at[chunk],
            p2_recv.at[chunk],
        )

    def deliver(chunk):
        finish(landed.at[chunk], p2_recv.at[chunk])
        z_stage(
            lambda other: landed.at[chunk, other],
            far_ref.at[chunk, plane],
            z2_send.at[chunk],
            z2_recv.at[chunk],
        )

    lower = lax.rem(plane, 2)
    set_rows = 4 * ROW_SET
    near_rows = rows.at[pl.ds(pl.multiple_of(lower * set_rows, ROW_SET), set_rows)]
    far_rows = rows.at[pl.ds(pl.multiple_of((1 - lower) * set_rows, ROW_SET), set_rows)]
    own_rows = rows.at[pl.ds(pl.multiple_of(head * ROW_SET, ROW_SET), ROW_SET)]

    for step in range(1, 4):
        other = spot - lax.rem(spot, 4) + lax.rem(spot + step, 4)
        pltpu.make_async_remote_copy(
            src_ref=row_ref,
            dst_ref=own_rows,
            send_sem=row_send.at[0],
            recv_sem=row_recv.at[0],
            device_id=place_of(plane, other),
            device_id_type=MESH,
        ).start()
    pltpu.make_async_copy(row_ref, own_rows, row_recv.at[0]).start()

    def share_rows():
        finish(near_rows, row_recv.at[0])
        pltpu.make_async_remote_copy(
            src_ref=near_rows,
            dst_ref=near_rows,
            send_sem=row_send.at[1],
            recv_sem=row_recv.at[1],
            device_id=place_of(plane + 1 - 2 * lower, spot),
            device_id_type=MESH,
        ).start()

    def skew_rows():
        finish(far_rows, row_recv.at[1])

        def body(i, carry):
            start = pl.multiple_of(i * ROW_SET, ROW_SET)
            some = rows[pl.ds(start, ROW_SET), :]
            for j in range(ROW_SET):
                turned = pltpu.roll(
                    jnp.broadcast_to(some[j : j + 1], (HALF, 2 * BLOCK)),
                    2 * BLOCK - HALF + 1,
                    1,
                    stride=1,
                    stride_axis=0,
                )
                skewed[start + j] = turned[:, : BLOCK + HALF]
            return carry

        lax.fori_loop(0, 2 * HEADS // ROW_SET, body, 0)

    scale = math.log2(math.e) / math.sqrt(LANES)
    contract = (((1,), (1,)), ((), ()))
    half_heads = HEADS // 2

    ones = jnp.ones((BLOCK, LANES), jnp.bfloat16)

    def far_block(chunk, head):
        other = lax.rem(head + half_heads, HEADS)
        return jnp.concatenate(
            [far_ref[chunk, :, one].reshape(HALF, LANES) for one in (head, other)], axis=0
        )

    def weigh(query, near_keys, far_keys, head, half):
        shift = HALF * (1 - half)
        near = lax.dot_general(query, near_keys, contract, preferred_element_type=jnp.float32)
        far = lax.dot_general(query, far_keys, contract, preferred_element_type=jnp.float32)
        near = near * scale + skewed[2 * head, :, shift : shift + BLOCK]
        far = far * scale + skewed[2 * head + 1, :, shift : shift + BLOCK]
        highest = jnp.max(jnp.maximum(near, far), axis=1, keepdims=True)
        return tuple(jnp.exp2(part - highest).astype(jnp.bfloat16) for part in (near, far))

    def blend(near, far, near_values, far_values):
        summed = jnp.dot(near, near_values, preferred_element_type=jnp.float32) + jnp.dot(
            far, far_values, preferred_element_type=jnp.float32
        )
        return (summed[:, :LANES] / summed[:, LANES:]).astype(jnp.bfloat16)

    def over_heads(slot, visit):
        middle = slot == 1
        first = (0, half_heads * odd, half_heads)[slot]

        def body(i, carry):
            for g in range(GROUP):
                place = i * GROUP + g
                start = (place if middle else first + place) * LANES
                visit(place, first + place, pl.ds(pl.multiple_of(start, LANES), LANES))
            return carry

        lax.fori_loop(0, half_heads // GROUP, body, 0)

    def attend(slot):
        middle = slot == 1
        q, k, v = (mid_q_ref, mid_k_ref, mid_v_ref) if middle else (whole_q, whole_k, whole_v)
        target = middle_out if middle else whole_out

        def visit(place, head, columns):
            near_keys = k[:, columns]
            far_keys = far_block(slot, head)
            near_values = jnp.concatenate([v[:, columns], ones], axis=1)
            far_values = jnp.concatenate([far_block(SLOTS + slot, head), ones], axis=1)
            for half in range(2):
                part = slice(half * HALF, (half + 1) * HALF)
                near, far = weigh(q[part, columns], near_keys, far_keys, head, half)
                target[part, columns] = blend(near, far, near_values, far_values)

        over_heads(slot, visit)

    def weigh_last():
        def visit(place, head, columns):
            near_keys = whole_k[:, columns]
            far_keys = far_block(2, head)
            for half in range(2):
                part = slice(half * HALF, (half + 1) * HALF)
                near, far = weigh(whole_q[part, columns], near_keys, far_keys, head, half)
                weights[place, part, :BLOCK] = near
                weights[place, part, BLOCK:] = far

        over_heads(2, visit)

    def blend_last():
        def visit(place, head, columns):
            near_values = jnp.concatenate([whole_v[:, columns], ones], axis=1)
            far_values = jnp.concatenate([far_block(SLOTS + 2, head), ones], axis=1)
            whole_out[:, columns] = blend(
                weights[place, :, :BLOCK], weights[place, :, BLOCK:], near_values, far_values
            )

        over_heads(2, visit)

    whole_rows = pl.ds(pl.multiple_of(odd * HALF, HALF), BLOCK)
    side_width = half_heads * LANES

    def store_whole(side):
        columns = pl.ds(side * side_width, side_width)
        return pltpu.make_async_copy(
            whole_out.at[:, columns], out_ref.at[whole_rows, columns], out_sem.at[side]
        )

    own_columns = pl.ds(pl.multiple_of(odd * side_width, LANES), side_width)
    own_place = out_ref.at[pl.ds(pl.multiple_of(2 * HALF * (1 - odd), HALF), HALF), own_columns]
    store_middle = pltpu.make_async_copy(
        middle_out.at[pl.ds(pl.multiple_of(odd * HALF, HALF), HALF), :], own_place, out_sem.at[2]
    )
    swap_middle = pltpu.make_async_remote_copy(
        src_ref=middle_out.at[pl.ds(pl.multiple_of((1 - odd) * HALF, HALF), HALF), :],
        dst_ref=out_ref.at[pl.ds(pl.multiple_of(2 * HALF * odd, HALF), HALF), own_columns],
        send_sem=swap_send,
        recv_sem=swap_recv,
        device_id=place_of(plane, pair),
        device_id_type=MESH,
    )
    loads = [
        pltpu.make_async_copy(source.at[whole_rows, :], target, whole_sem.at[i])
        for i, (source, target) in enumerate(((q_ref, whole_q), (k_ref, whole_k), (v_ref, whole_v)))
    ]

    for chunk in range(SLOTS):
        fan_out(chunk)
    for i, (source, target) in enumerate(((q_ref, mid_q_ref), (k_ref, mid_k_ref), (v_ref, mid_v_ref))):
        half_rows = pl.ds(pl.multiple_of(2 * HALF * (1 - odd), HALF), HALF)
        width = target.shape[1]
        own = pl.ds(pl.multiple_of(odd * width, LANES), width)
        given = pl.ds(pl.multiple_of((1 - odd) * width, LANES), width)
        place = target.at[pl.ds(pl.multiple_of(odd * HALF, HALF), HALF), :]
        pltpu.make_async_remote_copy(
            src_ref=source.at[half_rows, given],
            dst_ref=place,
            send_sem=half_send.at[i],
            recv_sem=half_recv.at[i],
            device_id=place_of(plane, pair),
            device_id_type=MESH,
        ).start()
        pltpu.make_async_copy(source.at[half_rows, own], place, half_recv.at[i]).start()
    for load in loads:
        load.start()
    def choose(kind):
        held = (held_k, held_v)[kind]
        for slot in range(SLOTS):
            part = held.at[pl.ds(slot * PLANE_DEVICES * PLANES, PLANE_DEVICES * PLANES)]
            finish(part, p1_recv.at[kind * SLOTS + slot])
        for slot in ORDER:
            pick(kind, slot)
            share_picked(kind * SLOTS + slot)

    for chunk in range(SLOTS):
        finish(fanned.at[chunk], z1_recv.at[chunk])
        by_head(chunk)
        fan_out(chunk + SLOTS)
    choose(0)
    share_rows()
    for i, slot in enumerate(ORDER):
        finish(fanned.at[SLOTS + i], z1_recv.at[SLOTS + i])
        by_head(SLOTS + i)
        deliver(slot)
    skew_rows()
    choose(1)
    for slot in ORDER:
        deliver(SLOTS + slot)
    for slot in ORDER:
        finish(far_ref.at[slot], z2_recv.at[slot])
    for i, target in enumerate((mid_q_ref, mid_k_ref, mid_v_ref)):
        finish(target, half_recv.at[i])
    for load in loads:
        load.wait()
    weigh_last()
    for slot in ORDER:
        finish(far_ref.at[SLOTS + slot], z2_recv.at[SLOTS + slot])
        if slot == 2:
            blend_last()
        else:
            attend(slot)
        if slot == 1:
            store_middle.start()
            swap_middle.start()
        else:
            store_whole(slot // 2).start()
    for i, target in enumerate((mid_q_ref, mid_k_ref, mid_v_ref)):
        finish(target.at[pl.ds(0, HALF), :], half_send.at[i])
    for chunk in range(2 * SLOTS):
        finish(fanned.at[chunk, pl.ds(0, PLANES - 1)], z1_send.at[chunk])
        finish(landed.at[chunk, :, pl.ds(0, PLANE_DEVICES - 1)], p1_send.at[chunk])
        finish(landed.at[chunk, :, pl.ds(0, PLANE_DEVICES - 1)], p2_send.at[chunk])
        finish(landed.at[chunk, pl.ds(0, PLANES - 1)], z2_send.at[chunk])
    finish(rows.at[pl.ds(0, 3 * ROW_SET)], row_send.at[0])
    finish(near_rows, row_send.at[1])
    store_middle.wait()
    swap_middle.wait()
    store_whole(0).wait()
    store_whole(1).wait()


def move_tiles(table, queries, keys, values, own_rows):
    rows, columns = keys.shape
    kind = keys.dtype
    chunks = 2 * SLOTS
    tiles = SLOTS * PLANES * PLANE_DEVICES
    anywhere = pl.BlockSpec(memory_space=pltpu.HBM)
    semaphores = (
        [pltpu.SemaphoreType.DMA((2,))] * 2
        + [pltpu.SemaphoreType.DMA((3,))] * 2
        + [pltpu.SemaphoreType.DMA] * 2
        + [pltpu.SemaphoreType.DMA((3,))] * 2
        + [pltpu.SemaphoreType.DMA((chunks,))] * 8
    )
    return pl.pallas_call(
        move_kernel,
        in_specs=[pl.BlockSpec(memory_space=pltpu.SMEM)]
        + [anywhere] * 3
        + [pl.BlockSpec(memory_space=pltpu.VMEM)],
        out_specs=anywhere,
        out_shape=jax.ShapeDtypeStruct((rows, columns), kind),
        scratch_shapes=[pltpu.VMEM((chunks, PLANES, PLANE_DEVICES, ROWS, LANES), kind)]
        + [pltpu.VMEM((BLOCK, columns // 2), kind)] * 3
        + [pltpu.VMEM((BLOCK, columns), kind)] * 4
        + [pltpu.VMEM((BLOCK, columns // 2), kind)]
        + [pltpu.VMEM((HEADS // 2, BLOCK, 2 * BLOCK), kind)]
        + [pltpu.VMEM((chunks, PLANES, ROWS, columns), kind)]
        + [pltpu.VMEM((tiles, ROWS, LANES), kind)] * 4
        + [
            pltpu.VMEM((chunks, PLANES, PLANE_DEVICES, ROWS, LANES), kind),
            pltpu.VMEM((2 * HEADS, 2 * BLOCK), jnp.float32),
            pltpu.VMEM((2 * HEADS, HALF, BLOCK + HALF), jnp.float32),
        ]
        + semaphores,
        cost_estimate=pl.CostEstimate(
            flops=0, transcendentals=0, bytes_accessed=1024 * 1024 * 1024
        ),
        compiler_params=pltpu.CompilerParams(
            collective_id=0, has_side_effects=True, vmem_limit_bytes=60 * 1024 * 1024
        ),
        name="move_tiles",
    )(table, queries, keys, values, own_rows)


PARTS = 4
SPANS = (((0, 64), (64, 64), (128, 64), (192, 64)), ((0, 64), (64, 64), (128, 64), (192, 64)))
HELD = 48
ROOM = ((13, 10), (12, 11))
FLIP = (11, 12)
HOPS = (2, 1, -1, -2)


def span_of(chunk):
    kind, part = divmod(chunk, PARTS)
    return kind, *SPANS[kind][part]


def room_starts(room):
    far, near = room
    return (0, far, far + near, far + 2 * near)


def room_size(room):
    return 2 * sum(room)


def route_kernel(partner_ref, send_ref, relay_ref, final_ref, over_ref):
    count = partner_ref.shape[1]
    i_row = lax.broadcasted_iota(jnp.int32, (1, count), 1)
    i_column = lax.broadcasted_iota(jnp.int32, (count, 1), 0)

    def both(f, *pairs):
        return tuple(f(*(pair[s] for pair in pairs)) for s in range(2))

    i = (i_row, i_column)

    def rank(key, order=i):
        same = key[1] == key[0]
        before = jnp.where(same & (order[1] < order[0]), 1.0, 0.0)
        after = jnp.where(same & (order[0] < order[1]), 1.0, 0.0)
        in_row = jnp.sum(before, axis=0, keepdims=True)
        in_column = jnp.sum(after, axis=1, keepdims=True)
        return in_row.astype(jnp.int32), in_column.astype(jnp.int32)

    asked = partner_ref[...].astype(jnp.float32)
    in_plane = i_column - HELD * (i_column // HELD)
    group = in_plane // 6
    wanted = ((i_column // 96) * 8 + group) * 12 + in_plane - 6 * group
    wanted = wanted + jnp.where(i_column - 96 * (i_column // 96) >= HELD, 6, 0)
    block_column = jnp.sum(jnp.where(wanted == i_row, asked, 0.0), axis=1, keepdims=True)
    block_row = jnp.sum(jnp.where(i_column == i_row, block_column, 0.0), axis=0, keepdims=True)
    block = (block_row.astype(jnp.int32), block_column.astype(jnp.int32))
    seq = both(lambda m: m // 12, block)
    rest = both(lambda m, s: m - 12 * s, block, seq)
    source = both(lambda s, r: (s // 8) * 2 + jnp.where(r >= 6, 1, 0), seq, rest)
    local = both(
        lambda s, r: (s - 8 * (s // 8)) * 6 + jnp.where(r >= 6, r - 6, r), seq, rest
    )
    target = both(lambda i: i // HELD, i)
    ahead = both(lambda a, b: jnp.where(b >= a, b - a, b - a + PLANES), source, target)
    turn = both(lambda r: r - 2 * (r // 2), rank(both(lambda a, b: a * 8 + b, source, target)))
    sign = both(
        lambda k, t: jnp.where(k < 4, 1, jnp.where((k == 4) & (t == 0), 1, -1)), ahead, turn
    )
    distance = both(lambda k: jnp.where(k <= 4, k, PLANES - k), ahead)
    def split(turn):
        first = both(
            lambda d, t: jnp.where(
                d == 0,
                0,
                jnp.where(d == 1, t, jnp.where(d == 2, 2 * t, jnp.where(d == 3, 1 + t, 2))),
            ),
            distance,
            turn,
        )
        second = both(lambda d, o: d - o, distance, first)
        relay = both(
            lambda z, s, o: jnp.bitwise_and(z + s * o + PLANES, PLANES - 1), source, sign, first
        )
        return first, second, relay

    late = both(lambda d, i: jnp.where(d == 4, i, i + count), distance, i)
    for leg in range(2):
        first, second, relay = split(turn)
        plane, hop = ((source, first), (relay, second))[leg]
        crowd = rank(both(lambda p, s, h: p * 8 + s * h + 2, plane, sign, hop), late)
        turn = both(
            lambda t, d, h, r: jnp.where((h == 2) & (d < 4) & (r >= FLIP[leg]), leg, t),
            turn,
            distance,
            hop,
            crowd,
        )
    first, second, relay = split(turn)

    def slots(plane, hop, room):
        way = both(lambda s, h: jnp.where(h == 0, 0, s * h), sign, hop)
        order = rank(both(lambda p, w: p * 8 + w + 2, plane, way))
        at = room_starts(room)
        slot = both(
            lambda w, r: r
            + jnp.where(w == 2, at[0], jnp.where(w == 1, at[1], jnp.where(w == -1, at[2], at[3]))),
            way,
            order,
        )
        limit = jnp.where(hop[0] == 2, room[0], room[1])
        over = jnp.where((way[0] != 0) & (order[0] >= limit), 1.0, 0.0)
        return slot, jnp.sum(over, axis=1, keepdims=True)

    slot_one, over_one = slots(source, first, ROOM[0])
    slot_two, over_two = slots(relay, second, ROOM[1])
    at_relay = both(lambda o, l, s: jnp.where(o == 0, l, HELD + s), first, local, slot_one)

    def fill(out_ref, plane, hop, slot, room, value):
        size = room_size(room)
        place = lax.broadcasted_iota(jnp.int32, (1, PLANES * size), 1)
        code = jnp.where(hop[1] == 0, -1, plane[1] * size + slot[1])
        chosen = jnp.where(code == place, value[1].astype(jnp.float32), 0.0)
        out_ref[...] = jnp.sum(chosen, axis=0, keepdims=True).astype(jnp.int32)

    fill(send_ref, source, first, slot_one, ROOM[0], local)
    fill(relay_ref, relay, second, slot_two, ROOM[1], at_relay)
    final_ref[...] = jnp.where(
        second[0] == 0, at_relay[0], HELD + room_size(ROOM[0]) + slot_two[0]
    )
    over_ref[...] = (over_one + over_two).astype(jnp.int32)


def plan_routes(partner):
    full = pl.BlockSpec(memory_space=pltpu.VMEM)
    count = partner.shape[0]
    shapes = [(1, PLANES * room_size(room)) for room in ROOM] + [(1, count), (1, 1)]
    return pl.pallas_call(
        route_kernel,
        in_specs=[full],
        out_specs=[full] * 4,
        out_shape=[jax.ShapeDtypeStruct(shape, jnp.int32) for shape in shapes],
        name="plan_routes",
    )(partner.reshape(1, -1))


def short_kernel(
    send_ref, relay_ref, final_ref, q_ref, k_ref, v_ref, row_ref, out_ref, *scratch
):
    chunks = 2 * PARTS
    held, near_in, far_in = (scratch[i * chunks : (i + 1) * chunks] for i in range(3))
    (
        staged_one,
        staged_two,
        staged_out,
        far_ref,
        weights_f,
        weights_b,
        all_q,
        full_k,
        full_v,
        mid_k,
        mid_v,
        all_out,
        rows,
        row_send,
        row_recv,
        load_sem,
        out_sem,
        half_send,
        half_recv,
        p0_send,
        p0b_send,
        p0_recv,
        z1_send,
        z1_recv,
        z2_send,
        z2_recv,
        out_send,
        out_recv,
    ) = scratch[3 * chunks :]
    seq = lax.axis_index("seq")
    head = lax.axis_index("head")
    plane = 2 * (seq // 8) + head // 4
    spot = lax.rem(seq, 8) * 4 + lax.rem(head, 4)
    odd = lax.rem(head, 2)
    pair = spot + 1 - 2 * odd

    def above(hop):
        return lax.rem(plane + hop + PLANES, PLANES)

    barrier = pltpu.get_barrier_semaphore()
    for hop in HOPS:
        pl.semaphore_signal(
            barrier, inc=1, device_id=place_of(above(hop), spot), device_id_type=MESH
        )

    def greet(step, carry):
        pl.semaphore_signal(
            barrier,
            inc=1,
            device_id=place_of(plane, lax.rem(spot + step, PLANE_DEVICES)),
            device_id_type=MESH,
        )
        return carry

    lax.fori_loop(1, PLANE_DEVICES, greet, 0)
    pl.semaphore_wait(barrier, len(HOPS) + PLANE_DEVICES - 1)

    def finish(ref, sem):
        pltpu.make_async_copy(ref, ref, sem).wait()

    def plane_stage(source, target, send, recv):
        def body(step, carry):
            other = lax.rem(spot + step, PLANE_DEVICES)
            pltpu.make_async_remote_copy(
                src_ref=source(other),
                dst_ref=target,
                send_sem=send,
                recv_sem=recv,
                device_id=place_of(plane, other),
                device_id_type=MESH,
            ).start()
            return carry

        lax.fori_loop(1, PLANE_DEVICES, body, 0)
        pltpu.make_async_copy(source(spot), target, recv).start()

    def first_block(place):
        return (place // 4) * 6 + (lax.rem(place, 4) // 2) * 3

    full_rows = pl.ds(pl.multiple_of(odd * HALF, HALF), BLOCK)
    half_rows = pl.ds(pl.multiple_of(2 * HALF * (1 - odd), HALF), HALF)

    def spread(chunk):
        kind, start, size = span_of(chunk)
        ref = (k_ref, v_ref)[kind]

        def piece(base):
            lines = pl.ds(pl.multiple_of(base, 2 * ROWS), size)
            return lambda other: ref.at[
                lines, pl.ds(pl.multiple_of(other * LANES, LANES), LANES)
            ]

        plane_stage(
            piece(odd * HALF + start),
            held[chunk].at[first_block(spot) + 2 * odd],
            p0_send.at[chunk],
            p0_recv.at[chunk],
        )

        @pl.when(odd == start // HALF)
        def _():
            plane_stage(
                piece(2 * HALF * (1 - odd) + start % HALF),
                held[chunk].at[first_block(spot) + 1],
                p0b_send.at[chunk],
                p0_recv.at[chunk],
            )

    def staged(ref, chunk):
        return ref.at[chunk % 2, :, pl.ds(0, span_of(chunk)[2])]

    def z_stage(source, landed, room, send, recv):
        for start, size, hop in zip(room_starts(room), (*room, *room[::-1]), HOPS):
            pltpu.make_async_remote_copy(
                src_ref=source.at[pl.ds(start, size)],
                dst_ref=landed.at[pl.ds(start, size)],
                send_sem=send,
                recv_sem=recv,
                device_id=place_of(above(hop), spot),
                device_id_type=MESH,
            ).start()

    size_one, size_two = (room_size(room) for room in ROOM)

    def leg_one(chunk):
        finish(held[chunk], p0_recv.at[chunk])
        slot, size = chunk % 2, span_of(chunk)[2]
        if chunk >= 2:
            finish(staged(staged_one, chunk - 2), z1_send.at[chunk - 2])

        def body(i, carry):
            for j in range(2):
                where = 2 * i + j
                index = send_ref[0, plane * size_one + where]
                staged_one[slot, where, :size] = held[chunk][index]
            return carry

        lax.fori_loop(0, size_one // 2, body, 0)
        z_stage(
            staged(staged_one, chunk), near_in[chunk], ROOM[0], z1_send.at[chunk], z1_recv.at[chunk]
        )

    def held_or_near(chunk, index):
        kept = held[chunk][jnp.minimum(index, HELD - 1)]
        came = near_in[chunk][jnp.clip(index - HELD, 0, size_one - 1)]
        return jnp.where(index < HELD, kept, came)

    def leg_two(chunk):
        finish(near_in[chunk], z1_recv.at[chunk])
        slot, size = chunk % 2, span_of(chunk)[2]
        if chunk >= 2:
            finish(staged(staged_two, chunk - 2), z2_send.at[chunk - 2])

        def body(i, carry):
            for j in range(2):
                where = 2 * i + j
                index = relay_ref[0, plane * size_two + where]
                staged_two[slot, where, :size] = held_or_near(chunk, index)
            return carry

        lax.fori_loop(0, size_two // 2, body, 0)
        z_stage(
            staged(staged_two, chunk), far_in[chunk], ROOM[1], z2_send.at[chunk], z2_recv.at[chunk]
        )

    def arrived(chunk, count=PLANE_DEVICES):
        kind, start, size = span_of(chunk)
        return far_ref.at[kind, pl.ds(0, count), :, pl.ds(start, size)]

    done = set()

    def finish_far(chunk):
        if chunk not in done:
            done.add(chunk)
            finish(arrived(chunk), out_recv.at[chunk])

    def deliver(chunk):
        finish(far_in[chunk], z2_recv.at[chunk])
        slot, (kind, start, size) = chunk % 2, span_of(chunk)
        if chunk >= 2:
            finish(arrived(chunk - 2, PLANE_DEVICES - 1), out_send.at[chunk - 2])
            finish_far(chunk - 2)
        border = HELD + size_one

        def body(i, carry):
            for j in range(2):
                where = 2 * i + j
                index = final_ref[0, plane * HELD + where]
                last = far_in[chunk][jnp.clip(index - border, 0, size_two - 1)]
                staged_out[slot, where, :size] = jnp.where(
                    index < border, held_or_near(chunk, index), last
                )
            return carry

        lax.fori_loop(0, HELD // 2, body, 0)
        ready = staged(staged_out, chunk)
        plane_stage(
            lambda other: ready.at[pl.ds(first_block(other) + lax.rem(other, 2), 2)],
            far_ref.at[kind, spot, :, pl.ds(start, size)],
            out_send.at[chunk],
            out_recv.at[chunk],
        )

    lower = lax.rem(plane, 2)
    set_rows = 4 * ROW_SET
    near_rows = rows.at[pl.ds(pl.multiple_of(lower * set_rows, ROW_SET), set_rows)]
    far_rows = rows.at[pl.ds(pl.multiple_of((1 - lower) * set_rows, ROW_SET), set_rows)]
    own_rows = rows.at[pl.ds(pl.multiple_of(head * ROW_SET, ROW_SET), ROW_SET)]

    def show_rows():
        for step in range(1, 4):
            other = spot - lax.rem(spot, 4) + lax.rem(spot + step, 4)
            pltpu.make_async_remote_copy(
                src_ref=row_ref,
                dst_ref=own_rows,
                send_sem=row_send.at[0],
                recv_sem=row_recv.at[0],
                device_id=place_of(plane, other),
                device_id_type=MESH,
            ).start()
        pltpu.make_async_copy(row_ref, own_rows, row_recv.at[0]).start()

    def share_rows():
        finish(near_rows, row_recv.at[0])
        pltpu.make_async_remote_copy(
            src_ref=near_rows,
            dst_ref=near_rows,
            send_sem=row_send.at[1],
            recv_sem=row_recv.at[1],
            device_id=place_of(plane + 1 - 2 * lower, spot),
            device_id_type=MESH,
        ).start()

    loads = [
        pltpu.make_async_copy(source, target, load_sem.at[i])
        for i, (source, target) in enumerate(
            ((q_ref, all_q), (k_ref.at[full_rows, :], full_k), (v_ref.at[full_rows, :], full_v))
        )
    ]

    def swap_halves():
        for i, (source, target) in enumerate(((k_ref, mid_k), (v_ref, mid_v))):
            place = target.at[pl.ds(pl.multiple_of(odd * HALF, HALF), HALF), :]
            pltpu.make_async_remote_copy(
                src_ref=source.at[half_rows, :],
                dst_ref=place,
                send_sem=half_send.at[i],
                recv_sem=half_recv.at[i],
                device_id=place_of(plane, pair),
                device_id_type=MESH,
            ).start()
            pltpu.make_async_copy(source.at[half_rows, :], place, half_recv.at[i]).start()

    scale = math.log2(math.e) / math.sqrt(LANES)
    contract = (((1,), (1,)), ((), ()))
    ones = jnp.ones((BLOCK, LANES), jnp.bfloat16)

    def weigh(query, near_keys, far_keys, near_bias, far_bias):
        near = lax.dot_general(query, near_keys, contract, preferred_element_type=jnp.float32)
        far = lax.dot_general(query, far_keys, contract, preferred_element_type=jnp.float32)
        near = near * scale + near_bias
        far = far * scale + far_bias
        highest = jnp.max(jnp.maximum(near, far), axis=1, keepdims=True)
        return tuple(jnp.exp2(part - highest).astype(jnp.bfloat16) for part in (near, far))

    def skew(line):
        return pltpu.roll(
            jnp.broadcast_to(line, (HALF, 2 * BLOCK)),
            2 * BLOCK - HALF + 1,
            1,
            stride=1,
            stride_axis=0,
        )

    def weigh_heads(first, last):
        def body(i, carry):
            lines = rows[pl.ds(pl.multiple_of(i * ROW_SET, ROW_SET), ROW_SET), :]
            for g in range(GROUP):
                one = i * GROUP + g
                columns = pl.ds(pl.multiple_of(one * LANES, LANES), LANES)
                skews = [skew(lines[2 * g + side : 2 * g + side + 1]) for side in range(2)]
                upper = [turned[:, HALF : HALF + BLOCK] for turned in skews]
                under = [turned[:, :BLOCK] for turned in skews]
                near_keys = full_k[:, columns]
                far_keys = far_ref[0, one, odd]
                for half in range(2):
                    lines_here = pl.ds(pl.multiple_of((odd + half) * HALF, HALF), HALF)
                    near, far = weigh(
                        all_q[lines_here, columns], near_keys, far_keys, *(upper, under)[half]
                    )
                    part = slice(half * HALF, (half + 1) * HALF)
                    weights_f[one, part, :BLOCK] = near
                    weights_f[one, part, BLOCK:] = far
                mixed = [jnp.where(odd == 1, u, o) for u, o in zip(under, upper)]
                near, far = weigh(
                    all_q[half_rows, columns], mid_k[:, columns], far_ref[0, one, 1 - odd], *mixed
                )
                weights_b[one, :, :BLOCK] = near
                weights_b[one, :, BLOCK:] = far
            return carry

        lax.fori_loop(first // GROUP, last // GROUP, body, 0)

    def blend(weights, near_values, far_values):
        summed = jnp.dot(
            weights[:, :BLOCK],
            jnp.concatenate([near_values, ones], axis=1),
            preferred_element_type=jnp.float32,
        ) + jnp.dot(
            weights[:, BLOCK:],
            jnp.concatenate([far_values, ones], axis=1),
            preferred_element_type=jnp.float32,
        )
        return (summed[:, :LANES] / summed[:, LANES:]).astype(jnp.bfloat16)

    def blend_heads(first, last):
        def body(i, carry):
            for g in range(GROUP):
                one = i * GROUP + g
                columns = pl.ds(pl.multiple_of(one * LANES, LANES), LANES)
                all_out[full_rows, columns] = blend(
                    weights_f[one], full_v[:, columns], far_ref[1, one, odd]
                )
                all_out[half_rows, columns] = blend(
                    weights_b[one], mid_v[:, columns], far_ref[1, one, 1 - odd]
                )
            return carry

        lax.fori_loop(first // GROUP, last // GROUP, body, 0)

    spread(0)
    spread(1)
    show_rows()
    for load in loads:
        load.start()
    for step in range(chunks + 3):
        if step < chunks:
            leg_one(step)
            if step + 2 < chunks:
                spread(step + 2)
        if step == 1:
            share_rows()
            swap_halves()
        if 1 <= step < chunks + 1:
            leg_two(step - 1)
        if step >= 3:
            deliver(step - 3)
        turn = step - chunks + 1
        if turn == 0:
            for chunk in range(PARTS):
                finish_far(chunk)
            finish(mid_k, half_recv.at[0])
            finish(mid_v, half_recv.at[1])
            finish(far_rows, row_recv.at[1])
            for load in loads:
                load.wait()
        if turn >= 0:
            weigh_heads(turn * HEADS // 4, (turn + 1) * HEADS // 4)
    finish_far(chunks - 2)
    finish_far(chunks - 1)
    stores = []
    for side in range(2):
        blend_heads(side * HEADS // 2, (side + 1) * HEADS // 2)
        columns = pl.ds(side * HEADS // 2 * LANES, HEADS // 2 * LANES)
        store = pltpu.make_async_copy(
            all_out.at[:, columns], out_ref.at[:, columns], out_sem.at[side]
        )
        store.start()
        stores.append(store)
    for chunk in range(chunks):
        finish(arrived(chunk, PLANE_DEVICES - 1).at[:, 0], p0_send.at[chunk])

        @pl.when(odd == span_of(chunk)[1] // HALF)
        def _():
            finish(arrived(chunk, PLANE_DEVICES - 1).at[:, 0], p0b_send.at[chunk])

    for chunk in range(chunks - 2, chunks):
        finish(staged(staged_one, chunk), z1_send.at[chunk])
        finish(staged(staged_two, chunk), z2_send.at[chunk])
        finish(arrived(chunk, PLANE_DEVICES - 1), out_send.at[chunk])
    for i, target in enumerate((mid_k, mid_v)):
        finish(target.at[pl.ds(0, HALF), :], half_send.at[i])
    finish(rows.at[pl.ds(0, 3 * ROW_SET)], row_send.at[0])
    finish(near_rows, row_send.at[1])
    for store in stores:
        store.wait()


def short_move(routes, queries, keys, values, own_rows):
    lines, columns = keys.shape
    kind = keys.dtype
    chunks = 2 * PARTS
    sizes = [room_size(room) for room in ROOM]
    anywhere = pl.BlockSpec(memory_space=pltpu.HBM)

    def vmem(*shape):
        return pltpu.VMEM(shape, kind)

    spans = [span_of(chunk)[2] for chunk in range(chunks)]
    scratch = []
    for count in (HELD, *sizes):
        scratch += [vmem(count, size, LANES) for size in spans]
    scratch += [vmem(2, count, max(spans), LANES) for count in (*sizes, HELD)]
    scratch += [
        vmem(2, HEADS, 2, BLOCK, LANES),
        vmem(HEADS, BLOCK, 2 * BLOCK),
        vmem(HEADS, HALF, 2 * BLOCK),
        vmem(lines, columns),
    ]
    scratch += [vmem(BLOCK, columns)] * 4 + [vmem(lines, columns)]
    scratch += [pltpu.VMEM((2 * HEADS, 2 * BLOCK), jnp.float32)]
    scratch += [pltpu.SemaphoreType.DMA((2,))] * 2
    scratch += [pltpu.SemaphoreType.DMA((3,))]
    scratch += [pltpu.SemaphoreType.DMA((2,))] * 3
    scratch += [pltpu.SemaphoreType.DMA((chunks,))] * 9
    return pl.pallas_call(
        short_kernel,
        in_specs=[pl.BlockSpec(memory_space=pltpu.SMEM)] * 3
        + [anywhere] * 3
        + [pl.BlockSpec(memory_space=pltpu.VMEM)],
        out_specs=anywhere,
        out_shape=jax.ShapeDtypeStruct((lines, columns), kind),
        scratch_shapes=scratch,
        compiler_params=pltpu.CompilerParams(
            collective_id=1, has_side_effects=True, vmem_limit_bytes=60 * 1024 * 1024
        ),
        name="short_move",
    )(*routes, queries, keys, values, own_rows)


def tile_table(partner):
    trio = partner // 3
    member = partner - 3 * trio
    entries = []
    for source, slot in (
        (jnp.where(member == 2, 1, 0), jnp.where(member == 1, 2, 0)),
        (jnp.where(member == 0, 0, 1), jnp.where(member == 1, 2, 1)),
    ):
        device = 2 * trio + source
        seq, head = device // 8, device % 8
        plane = (seq // 8) * 2 + head // 4
        spot = (seq % 8) * 4 + head % 4
        entries.append((slot * PLANE_DEVICES + spot) * PLANES + plane)
    return jnp.concatenate(entries)


def on_device(queries, key_states, value_states, partner, buckets, bias_table):
    one_hot = (
        buckets[..., None] == jnp.arange(bias_table.shape[0], dtype=jnp.int32)
    ).astype(jnp.float32)
    own_rows = jnp.einsum("skb,bh->hsk", one_hot, bias_table, precision=lax.Precision.HIGHEST)
    own_rows = jnp.pad(own_rows * math.log2(math.e), ((0, 0), (0, 0), (0, 1)))

    own_rows = own_rows.reshape(ROW_SET, 2 * BLOCK)
    *routes, over = plan_routes(partner)
    return lax.cond(
        over[0, 0] == 0,
        lambda: short_move(routes, queries, key_states, value_states, own_rows),
        lambda: move_tiles(
            tile_table(partner), queries, key_states, value_states, own_rows
        ),
    )


def solution(mesh):
    whole = P(("seq", "head"), None)
    return jax.shard_map(
        on_device,
        mesh=mesh,
        in_specs=(whole, whole, whole, P(), P(), P(None, "head")),
        out_specs=whole,
        check_vma=False,
    )
```
